32 devices in a mesh: groups: 2 (over y), space: 4 (over z), tm: 2 (over x), chan: 2 (over core).
Axes of the slice: x: 2, y: 2, z: 4, core: 2. Of those that a mesh axis runs over, the one named last changes fastest.
Arguments:
- features: float32 [48, 40, 384], P(('groups', 'space'), 'tm'), parts along dimension 0, may hold values from -50 to 50
- norm1_gain: float32 [384], replicated, may hold values from 0.25 to 1.75
- norm1_shift: float32 [384], replicated, may hold values from -3 to 3
- conv1_weight: float32 [3, 3, 384, 384], P(None, None, 'space', 'chan'), may hold values from -0.109375 to 0.109375
- norm2_gain: float32 [384], replicated, may hold values from 0.25 to 1.75
- norm2_shift: float32 [384], replicated, may hold values from -3 to 3
- conv2_weight: float32 [3, 3, 384, 384], P(None, None, 'space', 'chan'), may hold values from -0.109375 to 0.109375
- head_gain: float32 [384], replicated, may hold values from 0.25 to 1.75
- head_shift: float32 [384], replicated, may hold values from -3 to 3
- head_weight: float32 [3, 3, 384, 16], P(None, None, 'space', 'chan'), may hold values from -0.109375 to 0.109375
- head_bias: float32 [16], P('chan'), may hold values from -3 to 3
- noisy_latents: float32 [4, 16, 24, 40], P(('groups', 'tm'), None, 'space'), parts along dimension 0, may hold values from -6 to 6
- later_cond: float32 [4, 16, 24, 40], P(('groups', 'tm'), None, 'space'), parts along dimension 0, may hold values from -6 to 6
- patch_weight: float32 [144, 5120], P(None, 'chan'), may hold values from -0.5 to 0.5
- patch_bias: float32 [5120], P('chan'), may hold values from -3 to 3
Outputs:
- tokens: float32 [4, 12, 20, 5120], P(('groups', 'tm'), 'space', None, 'chan'), parts along dimension 0
- image_latent: float32 [48, 40, 16], P(('groups', 'space'), 'tm'), parts along dimension 0
The draws below stay inside these ranges and needn't reach their ends.
There are 2 independent parts, one for each index of `groups`. The reference program is written for one: setup_inputs(seed, part) draws one part's arguments, and reference() takes and returns one part's arrays. A program takes and returns all parts, laid end to end along the dimension named above; an argument that names none is the same for every part. Nothing has to cross between parts.
All inputs are finite; a program needn't handle non-finite values.
Results may differ from the reference program's by a relative error of at most 0.00007.
Values sent between devices are 32-bit elements; how exact they have to be, the bound alone decides.
A program may use at most 64 MiB of HBM per device.

```python
import math
import jax
import jax.numpy as jnp
from jax import lax

CH = 384
NGROUP = 32
ZDIM = 16
DIM = 5120
LAT_H = 24
LAT_W = 40
FRAMES = 2
PATCH_IN = 144


def draw_features(key, part):
    subkeys = jax.random.split(key, 4)
    row_pos = jnp.arange(LAT_H, dtype=jnp.float32) / (LAT_H - 1)
    row_ramp = 3.0 ** row_pos
    column_scale = jax.random.uniform(subkeys[0], (LAT_W,), minval=0.7, maxval=1.3)
    offsets = jax.random.uniform(subkeys[1], (CH,), minval=-1.0, maxval=1.0)
    random_part = jax.random.truncated_normal(subkeys[2], -4.0, 4.0, (LAT_H, LAT_W, CH))
    amplitude = jnp.exp(jax.random.uniform(subkeys[3], (CH,), minval=math.log(0.5), maxval=math.log(1.5)))
    return offsets + amplitude * row_ramp[:, None, None] * column_scale[None, :, None] * random_part


def shard_levels(own_key, extent, pieces, least, high):
    def one(position, blocks):
        draws = jax.random.uniform(jax.random.fold_in(jax.random.fold_in(own_key, 6), position), (blocks,), jnp.float32, least / len(pieces), high / len(pieces))
        return jnp.repeat(jnp.exp(draws), extent[position] // blocks).reshape((-1,) + (1,) * (len(extent) - position - 1))

    level = one(*pieces[0])
    for cut in pieces[1:]:
        level = level * one(*cut)
    return level


def centred(key, extent, deviation, most, pieces=(), kind=jnp.bfloat16):
    level = shard_levels(key, extent, pieces, -0.22, 0.18) if pieces else 1.0
    values = jax.random.normal(key, extent, jnp.float32) * deviation * level
    return jnp.minimum(jnp.maximum(values, -most), most).astype(kind)


def setup_inputs(seed: int = 0, part: int = 0) -> dict:
    key_list = jax.random.split(jax.random.key(seed), 16)
    own_keys = jax.random.split(jax.random.fold_in(key_list[15], part), 16)
    return {
        "features": draw_features(jax.random.fold_in(jax.random.fold_in(key_list[15], part), 71), part),
        "norm1_gain": jnp.clip(1.0 + 0.15 * jax.random.normal(key_list[1], (CH,), jnp.float32), 0.25, 1.75),
        "norm1_shift": centred(key_list[2], (CH,), 0.5, 3.0, (), jnp.float32),
        "conv1_weight": centred(key_list[3], (3, 3, CH, CH), (9 * CH) ** -0.5, 0.109375, ((2, 4), (3, 2)), jnp.float32),
        "norm2_gain": jnp.clip(1.0 + 0.15 * jax.random.normal(key_list[4], (CH,), jnp.float32), 0.25, 1.75),
        "norm2_shift": centred(key_list[5], (CH,), 0.5, 3.0, (), jnp.float32),
        "conv2_weight": centred(key_list[6], (3, 3, CH, CH), (9 * CH) ** -0.5, 0.109375, ((2, 4), (3, 2)), jnp.float32),
        "head_gain": jnp.clip(1.0 + 0.15 * jax.random.normal(key_list[7], (CH,), jnp.float32), 0.25, 1.75),
        "head_shift": centred(key_list[8], (CH,), 0.5, 3.0, (), jnp.float32),
        "head_weight": centred(key_list[9], (3, 3, CH, ZDIM), (9 * CH) ** -0.5, 0.109375, ((2, 4), (3, 2)), jnp.float32),
        "head_bias": centred(key_list[10], (ZDIM,), 0.5, 3.0, ((0, 2),), jnp.float32),
        "noisy_latents": centred(own_keys[11], (FRAMES, ZDIM, LAT_H, LAT_W), 1.0, 6.0, ((0, 2), (2, 4)), jnp.float32),
        "later_cond": centred(own_keys[12], (FRAMES, ZDIM, LAT_H, LAT_W), 1.0, 6.0, ((0, 2), (2, 4)), jnp.float32),
        "patch_weight": centred(key_list[13], (PATCH_IN, DIM), PATCH_IN ** -0.5, 0.5, ((1, 2),), jnp.float32),
        "patch_bias": centred(key_list[14], (DIM,), 0.5, 3.0, ((0, 2),), jnp.float32),
    }


EPSILON = 1e-06

def group_norm_act(values, gain, shift):
    height, width, depth = values.shape
    grouped = values.reshape(height * width, NGROUP, depth // NGROUP)
    center = lax.optimization_barrier(jnp.mean(grouped, axis=(0, 2), keepdims=True))
    spread = lax.optimization_barrier(jnp.mean(jnp.square(grouped - center), axis=(0, 2), keepdims=True))
    scaled = ((grouped - center) * lax.rsqrt(spread + EPSILON)).reshape(height, width, depth)
    return jax.nn.silu(scaled * gain + shift)

def conv_three(values, weight):
    result = lax.conv_general_dilated(values[None], weight, (1, 1), ((1, 1), (1, 1)), dimension_numbers=('NHWC', 'HWIO', 'NHWC'), precision=lax.Precision.HIGHEST)
    return result[0]

def reference(features, norm1_gain, norm1_shift, conv1_weight, norm2_gain, norm2_shift, conv2_weight, head_gain, head_shift, head_weight, head_bias, noisy_latents, later_cond, patch_weight, patch_bias):
    first_conv = conv_three(group_norm_act(features, norm1_gain, norm1_shift), conv1_weight)
    hidden = features + conv_three(group_norm_act(first_conv, norm2_gain, norm2_shift), conv2_weight)
    image_latent = conv_three(group_norm_act(hidden, head_gain, head_shift), head_weight) + head_bias
    frame_count = noisy_latents.shape[0]
    height = noisy_latents.shape[2]
    width = noisy_latents.shape[3]
    opening = jnp.arange(frame_count) == 0
    condition = jnp.where(opening[:, None, None, None], jnp.transpose(image_latent, (2, 0, 1))[None], later_cond)
    marks = jnp.broadcast_to(opening.astype(jnp.float32)[:, None, None, None], (frame_count, 4, height, width))
    stacked = jnp.concatenate([noisy_latents, marks, condition], axis=1)
    channel_count = stacked.shape[1]
    patches = stacked.reshape(frame_count, channel_count, height // 2, 2, width // 2, 2).transpose(0, 2, 4, 1, 3, 5).reshape(-1, channel_count * 4)
    tokens = jnp.dot(patches, patch_weight, precision=lax.Precision.HIGHEST, preferred_element_type=jnp.float32) + patch_bias
    return (tokens.reshape(frame_count, height // 2, width // 2, -1), image_latent)
```

```python
import functools
import types

import jax
import jax.numpy as jnp
from jax import lax
from jax.experimental import pallas as pl
from jax.experimental.pallas import tpu as pltpu
from jax.sharding import PartitionSpec as P

NGROUP = 32


EPSILON = 1e-06
HIGHEST = lax.Precision.HIGHEST


def padded_2(cells, sides, width):
    for axis, dim in sides:
        count = lax.axis_size(axis)
        ends = count - 1
        head = lax.slice_in_dim(cells, 0, width, axis=dim)
        tail = lax.slice_in_dim(cells, cells.shape[dim] - width, cells.shape[dim], axis=dim)
        cells = jnp.concatenate(
            [
                lax.ppermute(tail, axis, [(i, (i + 1) % count) for i in range(ends)]),
                cells,
                lax.ppermute(head, axis, [((i + 1) % count, i) for i in range(ends)]),
            ],
            axis=dim,
        )
    return cells


def group_stats(inner, count_all):
    grouped = inner.reshape(-1, NGROUP, inner.shape[-1] // NGROUP)
    totals, squares = lax.psum(
        (jnp.sum(grouped, axis=(0, 2)), jnp.sum(grouped * grouped, axis=(0, 2))), ("space", "tm")
    )
    center = totals / count_all
    spread = squares / count_all - center * center
    return (center, lax.rsqrt(spread + EPSILON))


def normalize_act(values, stats, gain, shift):
    center, inverse = stats
    grouped = values.reshape(values.shape[:-1] + (NGROUP, values.shape[-1] // NGROUP))
    scaled = (grouped - center[:, None]) * inverse[:, None]
    return jax.nn.silu(scaled.reshape(values.shape) * gain + shift)


def tap_columns(padded, rows_out, cols_out):
    shifted = [
        padded[row_tap : row_tap + rows_out, col_tap : col_tap + cols_out, :]
        for row_tap in range(3)
        for col_tap in range(3)
    ]
    return jnp.stack(shifted, axis=2).reshape(rows_out * cols_out, 9, padded.shape[-1])


def add_taps(columns, piece):
    depth = piece.shape[2]
    picked = columns.reshape(columns.shape[0], 9 * depth)
    return jnp.dot(
        picked,
        piece.reshape(9 * depth, piece.shape[3]),
        precision=HIGHEST,
        preferred_element_type=jnp.float32,
    )


def wide_conv(padded, weight, rows_out, cols_out):
    columns = tap_columns(padded, rows_out, cols_out)
    summed = add_taps(columns, lax.all_gather(weight, "space", axis=2, tiled=True))
    return lax.all_gather(summed.reshape(rows_out, cols_out, -1), "chan", axis=2, tiled=True)


def border_rim(values):
    return padded_2(values, (("space", 0), ("tm", 1)), 1)


def on_device(
    features,
    norm1_gain,
    norm1_shift,
    conv1_weight,
    norm2_gain,
    norm2_shift,
    conv2_weight,
    head_gain,
    head_shift,
    head_weight,
    head_bias,
    noisy_latents,
    later_cond,
    patch_weight,
    patch_bias,
):
    tile_rows = features.shape[0]
    tile_cols = features.shape[1]
    count_all = float(
        tile_rows
        * tile_cols
        * lax.axis_size("space")
        * lax.axis_size("tm")
        * (features.shape[2] // NGROUP)
    )
    first_stats = group_stats(features, count_all)
    active = normalize_act(features, first_stats, norm1_gain, norm1_shift)
    first_conv = wide_conv(border_rim(active), conv1_weight, tile_rows, tile_cols)
    second_stats = group_stats(first_conv, count_all)
    second_act = normalize_act(first_conv, second_stats, norm2_gain, norm2_shift)
    second_conv = wide_conv(border_rim(second_act), conv2_weight, tile_rows, tile_cols)
    hidden = features + second_conv
    head_stats = group_stats(hidden, count_all)
    head_act = normalize_act(hidden, head_stats, head_gain, head_shift)
    head_pad = padded_2(head_act, (("space", 0), ("tm", 1)), 1)
    head_columns = tap_columns(head_pad, tile_rows, tile_cols)
    latent_part = (
        add_taps(head_columns, lax.all_gather(head_weight, "space", axis=2, tiled=True)) + head_bias
    )
    image_latent = lax.all_gather(
        latent_part.reshape(tile_rows, tile_cols, -1), "chan", axis=2, tiled=True
    )
    latent_row = lax.all_gather(image_latent, "tm", axis=1, tiled=True)
    frame_count = noisy_latents.shape[0]
    full_width = noisy_latents.shape[3]
    frame_ids = lax.axis_index("tm") * frame_count + jnp.arange(frame_count)
    opening = frame_ids == 0
    condition = jnp.where(
        opening[:, None, None, None], jnp.transpose(latent_row, (2, 0, 1))[None], later_cond
    )
    marks = jnp.broadcast_to(
        opening.astype(jnp.float32)[:, None, None, None], (frame_count, 4, tile_rows, full_width)
    )
    stacked = jnp.concatenate([noisy_latents, marks, condition], axis=1)
    channel_count = stacked.shape[1]
    patches = (
        stacked.reshape(frame_count, channel_count, tile_rows // 2, 2, full_width // 2, 2)
        .transpose(0, 2, 4, 1, 3, 5)
        .reshape(-1, channel_count * 4)
    )
    tokens = (
        jnp.dot(patches, patch_weight, precision=HIGHEST, preferred_element_type=jnp.float32)
        + patch_bias
    )
    return (tokens.reshape(frame_count, tile_rows // 2, full_width // 2, -1), image_latent)


MESH = pl.DeviceIdType.MESH
LANES = 128
BF16 = jnp.bfloat16
F32 = jnp.float32


def split_pair(values):
    high = values.astype(BF16)
    return high, (values - high.astype(F32)).astype(BF16)


def split_columns(values):
    high, low = split_pair(values)
    return jnp.concatenate([high, low, high], axis=1)


def finish_kernel(dims, parts, patch, base, wc, latent_in, tokens, latent, tok, sem):
    PC, PP, Z, FR = dims["PC"], dims["PP"], dims["Z"], dims["FR"]
    width = dims["N"] // parts
    copies = [pltpu.make_async_copy(latent_in, latent, sem.at[parts])]
    copies[0].start()
    lhs = [split_columns(patch[f, :, 0 : 4 * Z]) for f in range(FR)]
    for n in range(parts):
        lanes = slice(n * width, (n + 1) * width)
        for f in range(FR):
            got = base[f, :, lanes] + jnp.dot(lhs[f], wc[:, lanes], preferred_element_type=F32)
            for p in range(dims["PR"]):
                tok[p, :, f, lanes] = got[p * PP : p * PP + PC, :]
        view = (slice(None), slice(None), slice(None), pl.ds(n * width, width))
        copies.append(pltpu.make_async_copy(tok.at[view], tokens.at[view], sem.at[n]))
        copies[-1].start()
    for copy in copies:
        copy.wait()


def fused_kernel(dims, names, *refs):
    S, T, C = dims["S"], dims["T"], dims["C"]
    R, W, CH = dims["R"], dims["W"], dims["CH"]
    Z, FR = dims["Z"], dims["FR"]
    CB = CH // S
    TILE = R * W
    REG = 2 * TILE
    per_group = CH // NGROUP
    ZH = Z // C
    AM, PM, WQ, WM = dims["AM"], dims["PM"], dims["WQ"], dims["WM"]
    QR = CB // 4
    AT = 8
    LAST = 2 * R + 1
    MR = up(2 * R + 2, 8)
    (
        feat_hbm, gain1_hbm, shift1_hbm, w1_hbm, gain2_hbm, shift2_hbm, w2_hbm, gain3_hbm,
        shift3_hbm, head_w_hbm, head_b_hbm, noisy_hbm, later_hbm, pw_hbm, patch_b_hbm,
    ) = refs[:15]
    patch_out, base_out, wc_out, latent = refs[15:19]
    v = types.SimpleNamespace(**dict(zip(names, refs[19:])))
    s = lax.axis_index("space")
    t = lax.axis_index("tm")
    c = lax.axis_index("chan")
    g = lax.axis_index("groups")
    p, hh = lax.rem(s, 2), lax.div(s, 2)
    pair, far, far2 = s + 1 - 2 * p, lax.rem(s + 2, 4), 3 - s
    tx, oc, gy = 1 - t, 1 - c, 1 - g
    inner = (p + hh) == 1
    own, side = 2 * t + p, 2 * tx + p
    near, cross = 2 * t + 1 - p, 2 * tx + 1 - p
    home = c == t
    stray = c != t
    sent = []

    def remote(src, dst, ssem, rsem, **where):
        return pltpu.make_async_remote_copy(
            src_ref=src, dst_ref=dst, send_sem=ssem, recv_sem=rsem, device_id=where,
            device_id_type=MESH,
        )

    def go(copy):
        copy.start()
        sent.append((None, copy))

    def go_if(condition, copy):
        @pl.when(condition)
        def _():
            copy.start()

        sent.append((condition, copy))

    early = (
        (feat_hbm, v.feat), (w1_hbm, v.w1_raw), (gain1_hbm, v.gain1), (shift1_hbm, v.shift1),
        (w2_hbm, v.w2_raw), (gain2_hbm, v.gain2), (shift2_hbm, v.shift2),
        (gain3_hbm, v.gain3), (shift3_hbm, v.shift3), (head_w_hbm, v.head_w),
        (head_b_hbm, v.head_b), (noisy_hbm, v.noisy), (later_hbm, v.later),
        (patch_b_hbm, v.patch_b),
    )
    loads = [
        pltpu.make_async_copy(src, dst, v.load_sem.at[k]) for k, (src, dst) in enumerate(early)
    ]
    strips = v.pw_raw.shape[0]
    loads += [
        pltpu.make_async_copy(
            pw_hbm.at[:, n * LANES : (n + 1) * LANES], v.pw_raw.at[n], v.load_sem.at[len(early) + n]
        )
        for n in range(strips)
    ]
    for load in loads:
        load.start()

    v.lat_in[...] = jnp.zeros(v.lat_in.shape, F32)
    barrier = pltpu.get_barrier_semaphore()
    for ds in range(S):
        for dt in range(T):
            for dc in range(C):
                if ds or dt or dc:
                    pl.semaphore_signal(
                        barrier,
                        inc=1,
                        device_id={
                            "space": lax.rem(s + ds, S),
                            "tm": lax.rem(t + dt, T),
                            "chan": lax.rem(c + dc, C),
                        },
                        device_id_type=MESH,
                    )
    pl.semaphore_signal(barrier, inc=1, device_id={"groups": gy}, device_id_type=MESH)

    def padded(values, width=LANES):
        rows = values.shape[0]
        if width == values.shape[1]:
            return values
        return jnp.concatenate([values, jnp.zeros((rows, width - values.shape[1]), values.dtype)], axis=1)

    def pack(dst, value, main):
        rows = value.shape[0]
        dst[...] = value[0:main]
        rest = rows - main
        free = LANES - CB
        for j in range(CB // free if rest else 0):
            dst[j * rest : (j + 1) * rest, CB:LANES] = value[main:rows, j * free : (j + 1) * free]

    def unpack(value, rows):
        main = value.shape[0]
        rest = rows - main
        if not rest:
            return (value,)
        free = LANES - CB
        columns = [value[j * rest : (j + 1) * rest, CB:LANES] for j in range(CB // free)]
        return value, padded(jnp.concatenate(columns, axis=1))

    def channel_stats(values):
        total = jnp.sum(values, axis=0, keepdims=True)
        middle = total * (1.0 / values.shape[0])
        away = values - middle
        return total, jnp.sum(away * away, axis=0, keepdims=True)

    loads[0].wait()
    for r in range(R):
        line = v.feat[r]
        for q in range(S):
            v.tile[q, r * W : (r + 1) * W, :] = padded(line[:, q * CB : (q + 1) * CB])
    own_rows = pl.ds(pl.multiple_of(p * TILE, 8), TILE)
    for q in range(S):
        value = v.tile[q]
        v.feat_all[q, own_rows, :] = value
        pack(v.a_pack.at[q], value, AM)
        total, spread = channel_stats(value)
        v.st[q : q + 1, :] = total
        v.st[S + q : S + q + 1, :] = spread
        edge = jnp.where(
            t == 0, v.tile[q, pl.ds(W - 1, R, stride=W), :], v.tile[q, pl.ds(0, R, stride=W), :]
        )
        v.colf[q, 0:R, :] = edge
        v.rowf[q, 0:W, :] = jnp.where(hh == 0, value[TILE - W : TILE], value[0:W])
        v.corf[q : q + 1, :] = jnp.where(hh == 0, edge[R - 1 : R], edge[0:1])
    v.st_in[t, s] = v.st[...]

    @pl.when(stray)
    def _():
        v.colf_in[p] = v.colf[...]

    def w_pack(k, raw):
        @pl.when(home)
        def _():
            for cc in range(C):
                rows = pl.ds(pl.multiple_of(QR * (2 * g + cc), 8), QR)
                for pp in range(2):
                    pieces = [raw[tap, rows, :][:, pp * CB : (pp + 1) * CB] for tap in range(9)]
                    pack(v.wpack.at[k, pp, cc], padded(jnp.concatenate(pieces, axis=0)), WM)

    loads[1].wait()
    w_pack(0, v.w1_raw)

    def w_own(k, raw):
        @pl.when(home)
        def _():
            for tap in range(9):
                w = raw[tap]
                v.wown[k, tap * CB : (tap + 1) * CB, :] = padded(
                    jnp.where(p == 0, w[:, 0:CB], w[:, CB : 2 * CB])
                )

    w_own(0, v.w1_raw)

    row_id = lax.broadcasted_iota(jnp.int32, (LANES, LANES), 0)
    col_id = lax.broadcasted_iota(jnp.int32, (LANES, LANES), 1)
    same = ((row_id // per_group) == (col_id // per_group)) & (row_id < CB) & (col_id < CB)
    member = jnp.where(same, 1.0, 0.0).astype(F32)

    def group_sum(rows8):
        return jnp.dot(rows8, member, precision=HIGHEST, preferred_element_type=F32)

    def store_mat(k, q, tap, w):
        high, low = split_pair(w)
        v.mat[k, q, tap * LANES : tap * LANES + CB, 0:LANES] = high
        v.mat[k, q, tap * LANES : tap * LANES + CB, LANES : 2 * LANES] = low

    def own_copy(k):
        return remote(v.wown.at[k], v.wown.at[k], v.es.at[k], v.er.at[k], chan=oc)

    def own_mat(k):
        pl.when(stray)(own_copy(k).wait_recv)
        for tap in range(9):
            store_mat(k, s, tap, v.wown[k, tap * CB : (tap + 1) * CB, :])

    gap = jnp.zeros((LANES - CB, 2 * LANES), BF16)
    for k in range(2):
        for q in range(S):
            for tap in range(9):
                v.mat[k, q, tap * LANES + CB : (tap + 1) * LANES, :] = gap

    def z_copy(k, peer, slot, cc):
        return remote(
            v.wpack.at[k, lax.rem(peer, 2), cc], v.wq.at[k, slot, 2 * g + cc],
            v.zs.at[k, peer, cc], v.zr.at[k, slot], space=peer, chan=cc,
        )

    def y_copy(k, z, which):
        ref = v.wq.at[k, z, which]
        return remote(ref, ref, v.ys.at[k, z], v.yr.at[k, z], groups=gy)

    def b_copy(k, z, which, n):
        ref = v.wq.at[k, z, which]
        return remote(ref, ref, v.bs.at[k, z, n], v.br.at[k, z, n], chan=oc)

    order = (far, far2, pair)

    def z_send(k, z):
        for cc in range(C):
            go_if(home, z_copy(k, z, s, cc))

    def relay(k, z):
        remote(
            v.wpack.at[k, 0, 0], v.wq.at[k, z, 2 * g + c], v.zs.at[k, z, 0], v.zr.at[k, z],
            space=z, chan=t,
        ).wait_recv()
        go(y_copy(k, z, 2 * g + c))
        go(b_copy(k, z, 2 * g + c, 0))

    def relay2(k, z):
        y_copy(k, z, 2 * gy + c).wait_recv()
        go(b_copy(k, z, 2 * gy + c, 1))

    def finish_weights(k, z):
        b_copy(k, z, 2 * g + oc, 0).wait_recv()
        b_copy(k, z, 2 * gy + oc, 1).wait_recv()
        for kk in range(4):
            at = 0
            for value in unpack(v.wq[k, z, kk], WQ):
                for n in range(value.shape[0] // 8):
                    tap, off = divmod(at, QR)
                    to = tap * CB + kk * QR + off
                    v.wf[to : to + 8, :] = value[n * 8 : n * 8 + 8]
                    at += 8
        for tap in range(9):
            store_mat(k, z, tap, v.wf[tap * CB : (tap + 1) * CB, :])

    pl.semaphore_wait(barrier, S * T * C)

    def feat_copy(n, slot, **where):
        return remote(v.a_pack, v.a_in.at[slot], v.as_sem.at[n], v.ar_sem.at[slot], **where)

    def feat_part(m):
        blocks = pl.ds(2 * m, 2)
        return remote(
            v.a_pack.at[blocks], v.a_in.at[p, blocks], v.fs.at[m], v.fr.at[m], space=pair
        )

    def st_copy(dt, peer, mt, ms):
        return remote(
            v.st, v.st_in.at[mt, ms], v.ss_sem.at[dt, peer], v.sr_sem.at[mt, ms],
            space=peer, tm=tx if dt else t,
        )

    def col_copy(n, slot, **where):
        return remote(v.colf, v.colf_in.at[slot], v.cs_sem.at[n], v.cr_sem.at[slot], **where)

    hub = inner & home
    row_copy = remote(v.rowf, v.rowf_in, v.rs_sem.at[0], v.rr_sem.at[0], space=far2)

    def row_forward(n, **where):
        return remote(v.rowf_in, v.rowf_in, v.rs_sem.at[1 + n], v.rr_sem.at[1], **where)

    def cor_copy(n, **where):
        return remote(v.corf, v.corf_in, v.os_sem.at[n], v.or_sem.at[0], **where)

    st_peers = [(0, far), (0, far2), (1, far), (1, far2), (0, pair), (1, pair), (1, s)]
    go_if(hub, row_copy)
    for dt, peer in st_peers:
        go(st_copy(dt, peer, t, s))
    for n, (peer, column) in enumerate(((far, t), (far2, t), (far, tx), (far2, tx))):
        go_if(inner & stray, cor_copy(n, space=peer, tm=column))
    go_if(stray, col_copy(0, p, tm=tx))
    go_if(stray, col_copy(1, p, space=pair))
    go_if(stray, col_copy(2, p, space=pair, tm=tx))
    go_if(home, feat_part(0))
    go_if(home, feat_part(1))
    go_if(home, feat_copy(0, p, tm=tx))
    z_send(0, far)
    go_if(home, own_copy(0))
    z_send(0, far2)
    bias_copy = remote(v.bias_out, v.bias_in, v.is_sem.at[0], v.ir_sem.at[0], chan=oc)

    for load in loads[2:]:
        load.wait()
    for n, (gain, shift) in enumerate(
        ((v.gain1, v.shift1), (v.gain2, v.shift2), (v.gain3, v.shift3))
    ):
        for j, ref in enumerate((gain, shift)):
            row = ref[...].reshape(1, CH)
            for q in range(S):
                v.prm[n, q, j : j + 1, :] = padded(row[:, q * CB : (q + 1) * CB])
    bias_row = jnp.broadcast_to(v.head_b[...].reshape(1, ZH), (ZH, ZH))
    diagonal = lax.broadcasted_iota(jnp.int32, (ZH, ZH), 0) == lax.broadcasted_iota(
        jnp.int32, (ZH, ZH), 1
    )
    my_bias = jnp.sum(jnp.where(diagonal, bias_row, 0.0), axis=1, keepdims=True)
    v.bias_out[...] = jnp.broadcast_to(my_bias, (ZH, LANES))
    go(bias_copy)
    own_mat(0)
    for tap in range(9):
        v.hw_send[tap] = padded(v.head_w[tap])

    @pl.when(hub)
    def _():
        row_copy.wait_recv()

    for n, where in enumerate((dict(space=pair), dict(tm=tx), dict(space=pair, tm=tx))):
        go_if(hub, row_forward(n, **where))
    z_send(0, pair)
    w_pack(1, v.w2_raw)
    w_own(1, v.w2_raw)
    go_if(home, own_copy(1))
    def feat_pass(m):
        ref = v.a_in.at[1 - p, pl.ds(2 * m, 2)]
        return remote(ref, ref, v.gs.at[m], v.fr.at[m], tm=tx)

    relay(0, far)
    for m in range(2):
        pl.when(home)(feat_part(m).wait_recv)
        go_if(home, feat_pass(m))

    def hw_copy(n, slot, **where):
        return remote(v.hw_send, v.hwq.at[slot], v.hs.at[n], v.hr.at[slot], **where)

    @pl.when(hh == t)
    def _():
        v.hwq[c] = v.hw_send[...]

    def unpack_features(slot):
        for q in range(S):
            at = 0
            for value in unpack(v.a_in[slot, q], TILE):
                rows = pl.ds(pl.multiple_of(slot * TILE + at, 8), value.shape[0])
                v.feat_all[q, rows, :] = value
                at += value.shape[0]

    @pl.when(stray)
    def _():
        feat_copy(0, p, tm=tx).wait_recv()
        unpack_features(p)

    @pl.when(stray)
    def _():
        for m in range(2):
            feat_pass(m).wait_recv()

    unpack_features(1 - p)
    for dt, peer in st_peers:
        st_copy(dt, peer, tx if dt else t, peer).wait_recv()
    col_copy(1, 1 - p, space=pair).wait_recv()
    pl.when(home)(col_copy(0, p, tm=tx).wait_recv)
    cor_copy(0, space=far).wait_recv()
    pl.when(jnp.logical_not(hub))(row_forward(0, space=pair).wait_recv)

    for z in order:
        z_send(1, z)
    scale = 1.0 / float(per_group * TILE * S * T)
    everyone = [v.st_in[tt, ss] for tt in range(T) for ss in range(S)]
    total8 = everyone[0]
    for part in everyone[1:]:
        total8 = total8 + part
    summed = group_sum(total8)
    center8 = summed * scale
    gathered = jnp.zeros((8, LANES), F32)
    for part in everyone:
        away = part * (1.0 / TILE) - center8
        gathered = gathered + away * away * float(TILE)
    inverse4 = lax.rsqrt((group_sum(gathered)[0:S] + summed[S : 2 * S]) * scale + EPSILON)

    def build_taps(n, q, value, columns, corner, row, center, inverse):
        gain, shift = v.prm[n, q, 0:1, :], v.prm[n, q, 1:2, :]

        def act(values):
            u = (values - center) * inverse * gain + shift
            return u / (1.0 + jnp.exp(-u))

        inside = act(value)
        line = act(row)
        top, bottom = jnp.where(hh == 1, line, 0.0), jnp.where(hh == 0, line, 0.0)
        tail = jnp.zeros((8, LANES), F32)
        for b in range(3):
            at = AT + 1 - b
            v.taps[q, b, AT + (LAST + 1) * W : AT + (LAST + 1) * W + 8, :] = tail
            v.taps[q, b, at : at + W, :] = top
            v.taps[q, b, at + W : at + W + REG, :] = inside
            v.taps[q, b, at + W + REG : at + 2 * W + REG, :] = bottom
        tip = act(corner)
        sides = [(0, 1, jnp.where(hh == 1, tip, 0.0)), (LAST, 1, jnp.where(hh == 0, tip, 0.0))]
        sides += [(1 + first, count, act(raw)) for first, count, raw in columns]
        for first, count, piece in sides:
            at = AT + first * W
            from_left = jnp.where(c == 1, piece, 0.0)
            from_right = jnp.where(c == 0, piece, 0.0)
            if count == 1:
                v.taps[q, 0, at : at + 1, :] = from_left
                v.taps[q, 2, at + W - 1 : at + W, :] = from_right
            else:
                v.taps[q, 0, pl.ds(at, count, stride=W), :] = from_left
                v.taps[q, 2, pl.ds(at + W - 1, count, stride=W), :] = from_right

    def first_taps(q):
        build_taps(
            0, q, v.feat_all[q],
            [(0, R, v.colf_in[0, q, 0:R, :]), (R, R, v.colf_in[1, q, 0:R, :])],
            v.corf_in[q : q + 1, :], v.rowf_in[q, 0:W, :],
            center8[q : q + 1], inverse4[q : q + 1],
        )

    def operand(q):
        highs, lows = [], []
        for a in range(3):
            for b in range(3):
                high, low = split_pair(v.taps[q, b, AT + a * W : AT + a * W + REG, :])
                highs.append(high)
                lows.append(low)
        return jnp.concatenate(
            [jnp.concatenate(highs, axis=1), jnp.concatenate(lows, axis=1)], axis=0
        )

    def conv_block(k, q):
        part = jnp.dot(operand(q), v.mat[k, q], preferred_element_type=F32)
        return part[0:REG, 0:LANES] + part[0:REG, LANES:] + part[REG:, 0:LANES]

    for q in range(S):
        first_taps(q)
    relay(0, far2)
    relay2(0, far)
    v.acc[...] = conv_block(0, s)
    relay(0, pair)
    go_if(hh == t, hw_copy(0, c, chan=oc))
    go_if(hh == t, hw_copy(1, c, space=far))
    go_if(hh == t, hw_copy(2, c, space=far, chan=oc))
    relay2(0, far2)
    finish_weights(0, far)
    v.acc[...] += conv_block(0, far)
    relay(1, far)
    relay2(0, pair)
    finish_weights(0, far2)
    v.acc[...] += conv_block(0, far2)
    own_mat(1)
    finish_weights(0, pair)
    first = v.acc[...] + conv_block(0, pair)
    v.conv_raw[own] = first

    def rim_exchange(k, full):
        value = full[...]
        total, spread = channel_stats(value)
        column = jnp.where(
            c == 0, full[pl.ds(W - 1, 2 * R, stride=W), :], full[pl.ds(0, 2 * R, stride=W), :]
        )
        row = jnp.where(hh == 0, value[REG - W : REG], value[0:W])
        corner = jnp.where(hh == 0, column[2 * R - 1 : 2 * R], column[0:1])
        for ref, first, rows in ((v.rowm, W, row), (v.colm, 2 * R, column), (v.corm, 1, corner)):
            ref[k, 0:first, :] = rows
            ref[k, first : first + 1, :] = total
            ref[k, first + 1 : first + 2, :] = spread
        copies = [
            remote(v.corm.at[k], v.corm_in.at[k], v.ks.at[k, 0], v.kr.at[k, 0], space=far, chan=oc),
            remote(v.rowm.at[k], v.rowm_in.at[k], v.ks.at[k, 1], v.kr.at[k, 1], space=far),
            remote(v.colm.at[k], v.colm_in.at[k], v.ks.at[k, 2], v.kr.at[k, 2], chan=oc),
        ]
        for copy in copies:
            go(copy)
        return copies, total, spread

    def rim_finish(k, copies, total, spread):
        for copy in copies:
            copy.wait_recv()
        parts = [(total, spread)]
        for ref, first in ((v.rowm_in, W), (v.colm_in, 2 * R), (v.corm_in, 1)):
            parts.append((ref[k, first : first + 1, :], ref[k, first + 1 : first + 2, :]))
        whole = parts[0][0] + parts[1][0] + parts[2][0] + parts[3][0]
        wide = lambda row: jnp.broadcast_to(row, (8, LANES))
        center = group_sum(wide(whole))[0:1] * scale
        spreads = jnp.zeros((1, LANES), F32)
        for part_total, part_spread in parts:
            away = part_total * (1.0 / REG) - center
            spreads = spreads + part_spread + away * away * float(REG)
        inverse = lax.rsqrt(group_sum(wide(spreads))[0:1] * scale + EPSILON)
        return center, inverse

    rims1 = rim_exchange(0, v.conv_raw.at[own])
    pack(v.ypack, first, PM)
    near_copy = remote(v.ypack, v.yin.at[0], v.vs.at[0], v.vr.at[0], space=pair)
    go(near_copy)
    side_copy = remote(v.ypack, v.yin.at[2], v.vs.at[1], v.vr.at[1], tm=tx)
    go(side_copy)
    cross_copy = remote(v.yin.at[0], v.yin.at[1], v.vs.at[2], v.vr.at[2], tm=tx)
    relay(1, far2)
    relay(1, pair)
    relay2(1, far)
    center, inverse = rim_finish(0, *rims1)
    v.rl_in[own, 0 : 2 * R, :] = v.colm_in[0, 0 : 2 * R, :]
    v.rl_in[own, 2 * R : 2 * R + 1, :] = v.corm_in[0, 0:1, :]
    v.rl_in[own, 2 * R + 1 : 2 * R + 2, :] = center
    v.rl_in[own, 2 * R + 2 : 2 * R + 3, :] = inverse
    v.rl_in[own, MR : MR + W, :] = v.rowm_in[0, 0:W, :]

    def rl_copy(n, q, **where):
        ref = v.rl_in.at[q]
        return remote(ref, ref, v.ls.at[n], v.lr.at[q], **where)

    go(rl_copy(0, own, space=pair))
    go(rl_copy(1, own, space=pair, tm=tx))
    go(rl_copy(2, own, tm=tx))

    def second_taps(q):
        build_taps(
            1, q, v.conv_raw[q], [(0, 2 * R, v.rl_in[q, 0 : 2 * R, :])],
            v.rl_in[q, 2 * R : 2 * R + 1, :], v.rl_in[q, MR : MR + W, :],
            v.rl_in[q, 2 * R + 1 : 2 * R + 2, :], v.rl_in[q, 2 * R + 2 : 2 * R + 3, :],
        )

    second_taps(own)
    relay2(1, far2)
    near_copy.wait_recv()
    go(cross_copy)
    finish_weights(1, far)
    v.acc[...] = conv_block(1, own)

    def unpack_conv(slot, q):
        at = 0
        for value in unpack(v.yin[slot], REG):
            v.conv_raw[q, at : at + value.shape[0], :] = value
            at += value.shape[0]

    side_copy.wait_recv()
    rl_copy(2, side, tm=tx).wait_recv()
    unpack_conv(2, side)
    second_taps(side)
    relay2(1, pair)
    v.acc[...] += conv_block(1, side)
    rl_copy(0, near, space=pair).wait_recv()
    unpack_conv(0, near)
    second_taps(near)
    cross_copy.wait_recv()
    rl_copy(1, cross, space=pair, tm=tx).wait_recv()
    unpack_conv(1, cross)
    second_taps(cross)
    finish_weights(1, far2)
    v.acc[...] += conv_block(1, far2)
    finish_weights(1, pair)
    v.hid[...] = v.acc[...] + conv_block(1, pair) + v.feat_all[own]
    rims2 = rim_exchange(1, v.hid)

    @pl.when(hh == t)
    def _():
        hw_copy(0, oc, chan=oc).wait_recv()

    @pl.when(hh != t)
    def _():
        for slot in range(C):
            hw_copy(1, slot, space=far).wait_recv()

    bias_copy.wait_recv()
    blank = jnp.zeros((LANES - 3 * Z, LANES), F32)
    for b in range(3):
        rows = [v.hwq[cc, a * 3 + b] for a in range(3) for cc in range(C)] + [blank]
        high, low = split_pair(jnp.concatenate(rows, axis=0))
        for place, value in ((3 * b, high), (3 * b + 1, high), (3 * b + 2, low)):
            v.wh_mat[:, place * LANES : (place + 1) * LANES] = value
    ours, other_bias = v.bias_out[...], v.bias_in[...]
    bias = jnp.where(
        own == 0,
        jnp.concatenate(
            [jnp.where(c == cc, ours, other_bias) for cc in range(C)], axis=0
        ),
        0.0,
    )

    for first, mat in ((0, v.wn_mat), (4 * (Z + 4), wc_out)):
        for b in range(2):
            for a in range(2):
                at = (b * 2 + a) * Z
                for n in range(strips):
                    high, low = split_pair(v.pw_raw[n, pl.ds(first + a * 2 + b, Z, stride=4), :])
                    lanes = slice(n * LANES, (n + 1) * LANES)
                    mat[at : at + Z, lanes] = high
                    mat[4 * Z + at : 4 * Z + at + Z, lanes] = high
                    mat[8 * Z + at : 8 * Z + at + Z, lanes] = low
    mark_sum = jnp.concatenate(
        [
            jnp.sum(v.pw_raw[n, 4 * Z : 4 * (Z + 4), :], axis=0, keepdims=True)
            for n in range(strips)
        ],
        axis=1,
    )

    PR, PC, PP = dims["PR"], dims["PC"], dims["PP"]
    FULLW = W * T
    cells, turned, patch = v.cells, v.turned, v.patch
    cells[...] = jnp.zeros(cells.shape, F32)
    patch[...] = jnp.zeros(patch.shape, F32)

    def build_patches():
        turned[...] = cells[...].T
        for b in range(2):
            picked = turned[pl.ds(b, PC, stride=2), :]
            for i in range(PR):
                patch[i * PP : i * PP + PC, b * 2 * Z : (b + 1) * 2 * Z] = picked[
                    :, i * 2 * Z : (i + 1) * 2 * Z
                ]

    for f in range(FR):
        for i in range(R):
            cells[i * Z : (i + 1) * Z, 0:FULLW] = v.noisy[f, i]
        build_patches()
        got = jnp.dot(split_columns(patch[:, 0 : 4 * Z]), v.wn_mat[...], preferred_element_type=F32)
        opening = (t * FR + f) == 0
        base_out[f] = got + v.patch_b[...].reshape(1, -1) + jnp.where(opening, mark_sum, 0.0)

    center, inverse = rim_finish(1, *rims2)
    build_taps(
        2, own, v.hid[...], [(0, 2 * R, v.colm_in[1, 0 : 2 * R, :])], v.corm_in[1, 0:1, :],
        v.rowm_in[1, 0:W, :], center, inverse,
    )

    columns = []
    for b in range(3):
        high, low = split_pair(v.taps[own, b, AT : AT + v.mixed.shape[0], :])
        columns += [high, low, high]
    v.mixed[...] = lax.dot_general(
        jnp.concatenate(columns, axis=1),
        v.wh_mat[...],
        (((1,), (1,)), ((), ())),
        preferred_element_type=F32,
    )
    for j in range(2):
        shifted = [v.mixed[j * TILE + a * W : j * TILE + a * W + LANES, :] for a in range(3)]
        joined = jnp.where(
            col_id < Z, shifted[0], jnp.where(col_id < 2 * Z, shifted[1], shifted[2])
        ).T
        v.lat_send[j] = joined[0:Z] + joined[Z : 2 * Z] + joined[2 * Z : 3 * Z] + bias
    v.lat_in[c, own] = v.lat_send[p]

    def lat_copy(dp, dt, dc, slot_c, slot_q):
        return remote(
            v.lat_send.at[1 - p if dp else p], v.lat_in.at[slot_c, slot_q],
            v.ts.at[dp, dt, dc], v.tr.at[slot_c, slot_q],
            space=pair if dp else s, tm=tx if dt else t, chan=oc if dc else c,
        )

    hops = [(1, 1, 1), (1, 1, 0), (0, 1, 1), (0, 1, 0), (1, 0, 1), (1, 0, 0), (0, 0, 1)]
    for dp, dt, dc in hops:
        go_if(((tx if dt else t) == 0) | (c == 1), lat_copy(dp, dt, dc, c, own))

    for condition, copy in sent:
        if condition is None:
            copy.wait_send()
        else:
            pl.when(condition)(copy.wait_send)

    for dp, dt, dc in hops:
        from_c = oc if dc else c
        source = 2 * (tx if dt else t) + (1 - p if dp else p)
        pl.when((t == 0) | (from_c == 1))(lat_copy(dp, dt, dc, from_c, source).wait_recv)

    def latent_of(tt):
        return v.lat_in[tt, 0] + v.lat_in[tt, 1] + v.lat_in[tt, 2] + v.lat_in[tt, 3]

    value = latent_of(t)
    for r in range(R):
        latent[r] = value[:, r * W : (r + 1) * W]
    for f in range(FR):
        cells[...] = jnp.zeros(cells.shape, F32)
        opening = (t * FR + f) == 0
        for tt in range(T):
            value = latent_of(tt)
            for i in range(R):
                cells[i * Z : (i + 1) * Z, tt * W : (tt + 1) * W] = value[:, i * W : (i + 1) * W]
        for i in range(R):
            rows = slice(i * Z, (i + 1) * Z)
            cells[rows, 0:FULLW] = jnp.where(opening, cells[rows, 0:FULLW], v.later[f, i])
        build_patches()
        patch_out[f] = patch[...]


def up(value, unit):
    return -(-value // unit) * unit


def packed_rows(rows, width, unit):
    free = LANES - width
    if free <= 0 or width % free or rows % 8:
        return rows
    main = up(-(-rows * width // LANES), unit)
    fits = main < rows and (rows - main) * (width // free) <= main
    return main if fits else rows


def plan(mesh_shape, features, noisy_latents, patch_weight, head_weight):
    S, T, C, G = (mesh_shape[axis] for axis in ("space", "tm", "chan", "groups"))
    R, W, CH = features.shape
    FR, Z = noisy_latents.shape[:2]
    dims = dict(S=S, T=T, C=C, R=R, W=W, CH=CH, Z=Z, FR=FR)
    dims["PR"], dims["PC"] = R // 2, W * T // 2
    dims["PP"] = up(W * T // 2, 8)
    dims["N"] = patch_weight.shape[1]
    CB = CH // S
    TILE = R * W
    dims["AM"] = packed_rows(TILE, CB, 16)
    dims["PM"] = packed_rows(2 * TILE, CB, 8)
    dims["WQ"] = 9 * (CB // 4)
    dims["WM"] = packed_rows(dims["WQ"], CB, 8)
    fits = (
        (S, T, C, G) == (4, 2, 2, 2)
        and CH % S == 0
        and CB <= LANES
        and CB % (4 * 8) == 0
        and CB % (CH // NGROUP) == 0
        and TILE % 8 == 0
        and TILE <= LANES
        and R % 2 == 0
        and R <= 8
        and all(dims[name] % 8 == 0 for name in ("AM", "PM", "WQ", "WM"))
        and dims["WM"] > 8
        and 2 * R + 2 <= up(2 * R + 2, 8)
        and head_weight.shape[3] * C == Z
        and Z % 16 == 0
        and 3 * Z <= LANES
        and R * Z <= LANES
        and W * T <= LANES
        and W * T % 2 == 0
        and 4 * Z <= LANES
        and dims["N"] % LANES == 0
    )
    return dims if fits else None


def fused(dims, args):
    S, T, C = dims["S"], dims["T"], dims["C"]
    R, W, CH = dims["R"], dims["W"], dims["CH"]
    Z, FR, N = dims["Z"], dims["FR"], dims["N"]
    CB, NH = CH // S, CH // C
    TILE, REG = R * W, 2 * R * W
    (f, g1, s1, w1, g2, s2, w2, g3, s3, hw, hb, noisy, later, pw, pb) = args
    flat = lambda v: v.reshape((9,) + v.shape[2:])
    by_row = lambda v: jnp.transpose(v, (0, 2, 1, 3))
    operands = (
        f, g1, s1, flat(w1), g2, s2, flat(w2), g3, s3,
        flat(jnp.transpose(hw, (0, 1, 3, 2))), hb, by_row(noisy), by_row(later), pw, pb,
    )
    vmem = pl.BlockSpec(memory_space=pltpu.VMEM)
    far = pl.BlockSpec(memory_space=pl.ANY)
    dma = lambda *shape: pltpu.SemaphoreType.DMA(shape)
    buf = lambda *shape: pltpu.VMEM(shape, F32)
    half = lambda *shape: pltpu.VMEM(shape, BF16)
    PR, PC, PP = dims["PR"], dims["PC"], dims["PP"]
    MR, RR = up(2 * R + 2, 8), up(W + 2, 8)
    TR = up(8 + 2 * W + TILE + LANES, 8)
    scratch = {
        name: pltpu.VMEM(operands[k].shape, F32)
        for name, k in (
            ("feat", 0), ("gain1", 1), ("shift1", 2), ("w1_raw", 3), ("gain2", 4), ("shift2", 5),
            ("w2_raw", 6), ("gain3", 7), ("shift3", 8), ("head_w", 9), ("head_b", 10),
            ("noisy", 11), ("later", 12), ("patch_b", 14),
        )
    }
    scratch |= {
        "pw_raw": buf(N // LANES, pw.shape[0], LANES),
        "prm": buf(3, S, 8, LANES),
        "tile": buf(S, TILE, LANES),
        "feat_all": buf(S, REG, LANES),
        "a_pack": buf(S, dims["AM"], LANES),
        "a_in": buf(2, S, dims["AM"], LANES),
        "st": buf(8, LANES),
        "st_in": buf(T, S, 8, LANES),
        "colf": buf(S, 8, LANES),
        "colf_in": buf(2, S, 8, LANES),
        "rowf": buf(S, RR, LANES),
        "rowf_in": buf(S, RR, LANES),
        "corf": buf(8, LANES),
        "corf_in": buf(8, LANES),
        "wpack": buf(2, 2, C, dims["WM"], LANES),
        "wown": buf(2, 9 * CB, LANES),
        "bias_out": buf(Z // C, LANES),
        "bias_in": buf(Z // C, LANES),
        "wq": buf(2, S, 4, dims["WM"], LANES),
        "wf": buf(9 * CB, LANES),
        "mat": half(2, S, 9 * LANES, 2 * LANES),
        "taps": buf(S, 3, TR, LANES),
        "acc": buf(REG, LANES),
        "conv_raw": buf(S, REG, LANES),
        "ypack": buf(dims["PM"], LANES),
        "yin": buf(3, dims["PM"], LANES),
        "hid": buf(REG, LANES),
        "colm": buf(2, MR, LANES),
        "colm_in": buf(2, MR, LANES),
        "rowm": buf(2, RR, LANES),
        "rowm_in": buf(2, RR, LANES),
        "corm": buf(2, 8, LANES),
        "corm_in": buf(2, 8, LANES),
        "rl_in": buf(S, MR + RR, LANES),
        "hw_send": buf(9, Z // C, LANES),
        "hwq": buf(C, 9, Z // C, LANES),
        "wh_mat": half(LANES, 9 * LANES),
        "wn_mat": half(12 * Z, N),
        "mixed": buf(TR - 8, LANES),
        "lat_send": buf(2, Z, LANES),
        "lat_in": buf(C, S, Z, LANES),
        "cells": buf(LANES, LANES),
        "turned": buf(LANES, LANES),
        "patch": buf(PR * PP, LANES),
        "load_sem": dma(16 + N // LANES),
        "as_sem": dma(3), "ar_sem": dma(2), "fs": dma(2), "fr": dma(2), "gs": dma(2),
        "ss_sem": dma(T, S), "sr_sem": dma(T, S),
        "cs_sem": dma(3), "cr_sem": dma(2),
        "rs_sem": dma(4), "rr_sem": dma(2),
        "os_sem": dma(4), "or_sem": dma(1),
        "is_sem": dma(1), "ir_sem": dma(1),
        "zs": dma(2, S, C), "zr": dma(2, S),
        "ys": dma(2, S), "yr": dma(2, S),
        "bs": dma(2, S, 2), "br": dma(2, S, 2),
        "es": dma(2), "er": dma(2),
        "ks": dma(2, 3), "kr": dma(2, 3),
        "vs": dma(3), "vr": dma(3),
        "ls": dma(3), "lr": dma(S),
        "hs": dma(3), "hr": dma(C),
        "ts": dma(2, T, C), "tr": dma(C, S),
    }
    patch, base, wc, latent = pl.pallas_call(
        functools.partial(fused_kernel, dims, tuple(scratch)),
        out_shape=(
            jax.ShapeDtypeStruct((FR, PR * PP, LANES), F32),
            jax.ShapeDtypeStruct((FR, PR * PP, N), F32),
            jax.ShapeDtypeStruct((12 * Z, N), BF16),
            jax.ShapeDtypeStruct((R, Z, W), F32),
        ),
        in_specs=[pl.BlockSpec(memory_space=pltpu.HBM)] * 15,
        out_specs=(vmem, vmem, vmem, vmem),
        scratch_shapes=list(scratch.values()),
        compiler_params=pltpu.CompilerParams(
            collective_id=0, has_side_effects=True, vmem_limit_bytes=32 * 2**20
        ),
        name="fused_block",
    )(*[pltpu.with_memory_space_constraint(v, pltpu.HBM) for v in operands])
    NB = 4 if N % (4 * LANES) == 0 else 1
    tokens, latent = pl.pallas_call(
        functools.partial(finish_kernel, dims, NB),
        out_shape=(
            jax.ShapeDtypeStruct((PR, PC, FR, N), F32),
            jax.ShapeDtypeStruct((R, Z, W), F32),
        ),
        in_specs=[vmem] * 4,
        out_specs=(pl.BlockSpec(memory_space=pltpu.HBM), pl.BlockSpec(memory_space=pltpu.HBM)),
        scratch_shapes=[buf(PR, PC, FR, N), dma(NB + 1)],
        compiler_params=pltpu.CompilerParams(vmem_limit_bytes=8 * 2**20),
        name="finish_tokens",
    )(patch, base, wc, latent)
    return jnp.transpose(tokens, (2, 0, 1, 3)), jnp.transpose(latent, (0, 2, 1))


def solution(mesh):
    shape = dict(mesh.shape)

    def step(*args):
        dims = plan(shape, args[0], args[11], args[13], args[9])
        return on_device(*args) if dims is None else fused(dims, args)

    return jax.shard_map(
        step,
        mesh=mesh,
        in_specs=(
            P(("groups", "space"), "tm", None),
            P(),
            P(),
            P(None, None, "space", "chan"),
            P(),
            P(),
            P(None, None, "space", "chan"),
            P(),
            P(),
            P(None, None, "space", "chan"),
            P("chan"),
            P(("groups", "tm"), None, "space", None),
            P(("groups", "tm"), None, "space", None),
            P(None, "chan"),
            P("chan"),
        ),
        out_specs=(P(("groups", "tm"), "space", None, "chan"), P(("groups", "space"), "tm", None)),
        check_vma=False,
    )
```

```python
import functools
import types

import jax
import jax.numpy as jnp
from jax import lax
from jax.experimental import pallas as pl
from jax.experimental.pallas import tpu as pltpu
from jax.sharding import PartitionSpec as P

NGROUP = 32


EPSILON = 1e-06
HIGHEST = lax.Precision.HIGHEST


def padded_2(cells, sides, width):
    for axis, dim in sides:
        count = lax.axis_size(axis)
        ends = count - 1
        head = lax.slice_in_dim(cells, 0, width, axis=dim)
        tail = lax.slice_in_dim(cells, cells.shape[dim] - width, cells.shape[dim], axis=dim)
        cells = jnp.concatenate(
            [
                lax.ppermute(tail, axis, [(i, (i + 1) % count) for i in range(ends)]),
                cells,
                lax.ppermute(head, axis, [((i + 1) % count, i) for i in range(ends)]),
            ],
            axis=dim,
        )
    return cells


def group_stats(inner, count_all):
    grouped = inner.reshape(-1, NGROUP, inner.shape[-1] // NGROUP)
    totals, squares = lax.psum(
        (jnp.sum(grouped, axis=(0, 2)), jnp.sum(grouped * grouped, axis=(0, 2))), ("space", "tm")
    )
    center = totals / count_all
    spread = squares / count_all - center * center
    return (center, lax.rsqrt(spread + EPSILON))


def normalize_act(values, stats, gain, shift):
    center, inverse = stats
    grouped = values.reshape(values.shape[:-1] + (NGROUP, values.shape[-1] // NGROUP))
    scaled = (grouped - center[:, None]) * inverse[:, None]
    return jax.nn.silu(scaled.reshape(values.shape) * gain + shift)


def tap_columns(padded, rows_out, cols_out):
    shifted = [
        padded[row_tap : row_tap + rows_out, col_tap : col_tap + cols_out, :]
        for row_tap in range(3)
        for col_tap in range(3)
    ]
    return jnp.stack(shifted, axis=2).reshape(rows_out * cols_out, 9, padded.shape[-1])


def add_taps(columns, piece):
    depth = piece.shape[2]
    picked = columns.reshape(columns.shape[0], 9 * depth)
    return jnp.dot(
        picked,
        piece.reshape(9 * depth, piece.shape[3]),
        precision=HIGHEST,
        preferred_element_type=jnp.float32,
    )


def wide_conv(padded, weight, rows_out, cols_out):
    columns = tap_columns(padded, rows_out, cols_out)
    summed = add_taps(columns, lax.all_gather(weight, "space", axis=2, tiled=True))
    return lax.all_gather(summed.reshape(rows_out, cols_out, -1), "chan", axis=2, tiled=True)


def border_rim(values):
    return padded_2(values, (("space", 0), ("tm", 1)), 1)


def on_device(
    features,
    norm1_gain,
    norm1_shift,
    conv1_weight,
    norm2_gain,
    norm2_shift,
    conv2_weight,
    head_gain,
    head_shift,
    head_weight,
    head_bias,
    noisy_latents,
    later_cond,
    patch_weight,
    patch_bias,
):
    tile_rows = features.shape[0]
    tile_cols = features.shape[1]
    count_all = float(
        tile_rows
        * tile_cols
        * lax.axis_size("space")
        * lax.axis_size("tm")
        * (features.shape[2] // NGROUP)
    )
    first_stats = group_stats(features, count_all)
    active = normalize_act(features, first_stats, norm1_gain, norm1_shift)
    first_conv = wide_conv(border_rim(active), conv1_weight, tile_rows, tile_cols)
    second_stats = group_stats(first_conv, count_all)
    second_act = normalize_act(first_conv, second_stats, norm2_gain, norm2_shift)
    second_conv = wide_conv(border_rim(second_act), conv2_weight, tile_rows, tile_cols)
    hidden = features + second_conv
    head_stats = group_stats(hidden, count_all)
    head_act = normalize_act(hidden, head_stats, head_gain, head_shift)
    head_pad = padded_2(head_act, (("space", 0), ("tm", 1)), 1)
    head_columns = tap_columns(head_pad, tile_rows, tile_cols)
    latent_part = (
        add_taps(head_columns, lax.all_gather(head_weight, "space", axis=2, tiled=True)) + head_bias
    )
    image_latent = lax.all_gather(
        latent_part.reshape(tile_rows, tile_cols, -1), "chan", axis=2, tiled=True
    )
    latent_row = lax.all_gather(image_latent, "tm", axis=1, tiled=True)
    frame_count = noisy_latents.shape[0]
    full_width = noisy_latents.shape[3]
    frame_ids = lax.axis_index("tm") * frame_count + jnp.arange(frame_count)
    opening = frame_ids == 0
    condition = jnp.where(
        opening[:, None, None, None], jnp.transpose(latent_row, (2, 0, 1))[None], later_cond
    )
    marks = jnp.broadcast_to(
        opening.astype(jnp.float32)[:, None, None, None], (frame_count, 4, tile_rows, full_width)
    )
    stacked = jnp.concatenate([noisy_latents, marks, condition], axis=1)
    channel_count = stacked.shape[1]
    patches = (
        stacked.reshape(frame_count, channel_count, tile_rows // 2, 2, full_width // 2, 2)
        .transpose(0, 2, 4, 1, 3, 5)
        .reshape(-1, channel_count * 4)
    )
    tokens = (
        jnp.dot(patches, patch_weight, precision=HIGHEST, preferred_element_type=jnp.float32)
        + patch_bias
    )
    return (tokens.reshape(frame_count, tile_rows // 2, full_width // 2, -1), image_latent)


MESH = pl.DeviceIdType.MESH
LANES = 128
BF16 = jnp.bfloat16
F32 = jnp.float32


def split_pair(values):
    high = values.astype(BF16)
    return high, (values - high.astype(F32)).astype(BF16)


def split_columns(values):
    high, low = split_pair(values)
    return jnp.concatenate([high, low, high], axis=1)


def finish_kernel(dims, parts, patch, base, wc, latent_in, tokens, latent, tok, sem):
    PC, PP, Z, FR = dims["PC"], dims["PP"], dims["Z"], dims["FR"]
    width = dims["N"] // parts
    copies = [pltpu.make_async_copy(latent_in, latent, sem.at[parts])]
    copies[0].start()
    lhs = [split_columns(patch[f, :, 0 : 4 * Z]) for f in range(FR)]
    for n in range(parts):
        lanes = slice(n * width, (n + 1) * width)
        for f in range(FR):
            got = base[f, :, lanes] + jnp.dot(lhs[f], wc[:, lanes], preferred_element_type=F32)
            for p in range(dims["PR"]):
                tok[p, :, f, lanes] = got[p * PP : p * PP + PC, :]
        view = (slice(None), slice(None), slice(None), pl.ds(n * width, width))
        copies.append(pltpu.make_async_copy(tok.at[view], tokens.at[view], sem.at[n]))
        copies[-1].start()
    for copy in copies:
        copy.wait()


def fused_kernel(dims, names, *refs):
    S, T, C = dims["S"], dims["T"], dims["C"]
    R, W, CH = dims["R"], dims["W"], dims["CH"]
    Z, FR = dims["Z"], dims["FR"]
    CB = CH // S
    TILE = R * W
    REG = 2 * TILE
    per_group = CH // NGROUP
    ZH = Z // C
    AM, PM, WQ, WM = dims["AM"], dims["PM"], dims["WQ"], dims["WM"]
    QR = CB // 4
    AT = 8
    LAST = 2 * R + 1
    MR = up(2 * R + 2, 8)
    (
        feat_hbm, gain1_hbm, shift1_hbm, w1_hbm, gain2_hbm, shift2_hbm, w2_hbm, gain3_hbm,
        shift3_hbm, head_w_hbm, head_b_hbm, noisy_hbm, later_hbm, pw_hbm, patch_b_hbm,
    ) = refs[:15]
    patch_out, base_out, wc_out, latent = refs[15:19]
    v = types.SimpleNamespace(**dict(zip(names, refs[19:])))
    s = lax.axis_index("space")
    t = lax.axis_index("tm")
    c = lax.axis_index("chan")
    g = lax.axis_index("groups")
    p, hh = lax.rem(s, 2), lax.div(s, 2)
    pair, far, far2 = s + 1 - 2 * p, lax.rem(s + 2, 4), 3 - s
    tx, oc, gy = 1 - t, 1 - c, 1 - g
    inner = (p + hh) == 1
    own, side = 2 * t + p, 2 * tx + p
    near, cross = 2 * t + 1 - p, 2 * tx + 1 - p
    home = c == t
    stray = c != t

    def remote(src, dst, ssem, rsem, **where):
        return pltpu.make_async_remote_copy(
            src_ref=src, dst_ref=dst, send_sem=ssem, recv_sem=rsem, device_id=where,
            device_id_type=MESH,
        )

    def go(copy):
        copy.start()

    def go_if(condition, copy):
        @pl.when(condition)
        def _():
            copy.start()

    def rows_of(count):
        return v.wf.at[pl.ds(0, count)]

    def await_bytes(ref, sem):
        pltpu.make_async_copy(ref, ref, sem).wait()

    early = (
        (feat_hbm, v.feat), (w1_hbm, v.w1_raw), (gain1_hbm, v.gain1), (shift1_hbm, v.shift1),
        (w2_hbm, v.w2_raw), (gain2_hbm, v.gain2), (shift2_hbm, v.shift2),
        (gain3_hbm, v.gain3), (shift3_hbm, v.shift3), (head_w_hbm, v.head_w),
        (head_b_hbm, v.head_b), (noisy_hbm, v.noisy), (later_hbm, v.later),
        (patch_b_hbm, v.patch_b),
    )
    loads = [
        pltpu.make_async_copy(src, dst, v.load_sem.at[k]) for k, (src, dst) in enumerate(early)
    ]
    strips = v.pw_raw.shape[0]
    loads += [
        pltpu.make_async_copy(
            pw_hbm.at[:, n * LANES : (n + 1) * LANES], v.pw_raw.at[n], v.load_sem.at[len(early)]
        )
        for n in range(strips)
    ]
    for load in loads:
        load.start()

    v.lat_in[...] = jnp.zeros(v.lat_in.shape, F32)
    barrier = pltpu.get_barrier_semaphore()
    for ds in range(S):
        for dt in range(T):
            for dc in range(C):
                if ds or dt or dc:
                    pl.semaphore_signal(
                        barrier,
                        inc=1,
                        device_id={
                            "space": lax.rem(s + ds, S),
                            "tm": lax.rem(t + dt, T),
                            "chan": lax.rem(c + dc, C),
                        },
                        device_id_type=MESH,
                    )
    pl.semaphore_signal(barrier, inc=1, device_id={"groups": gy}, device_id_type=MESH)

    def padded(values, width=LANES):
        rows = values.shape[0]
        if width == values.shape[1]:
            return values
        return jnp.concatenate([values, jnp.zeros((rows, width - values.shape[1]), values.dtype)], axis=1)

    def pack(dst, value, main):
        rows = value.shape[0]
        dst[...] = value[0:main]
        rest = rows - main
        free = LANES - CB
        for j in range(CB // free if rest else 0):
            dst[j * rest : (j + 1) * rest, CB:LANES] = value[main:rows, j * free : (j + 1) * free]

    def unpack(value, rows):
        main = value.shape[0]
        rest = rows - main
        if not rest:
            return (value,)
        free = LANES - CB
        columns = [value[j * rest : (j + 1) * rest, CB:LANES] for j in range(CB // free)]
        return value, padded(jnp.concatenate(columns, axis=1))

    def channel_stats(values):
        total = jnp.sum(values, axis=0, keepdims=True)
        middle = total * (1.0 / values.shape[0])
        away = values - middle
        return total, jnp.sum(away * away, axis=0, keepdims=True)

    loads[0].wait()
    for r in range(R):
        line = v.feat[r]
        for q in range(S):
            v.tile[q, r * W : (r + 1) * W, :] = padded(line[:, q * CB : (q + 1) * CB])
    own_rows = pl.ds(pl.multiple_of(p * TILE, 8), TILE)
    for q in range(S):
        value = v.tile[q]
        v.feat_all[q, own_rows, :] = value
        pack(v.a_pack.at[q], value, AM)
        total, spread = channel_stats(value)
        v.st[q : q + 1, :] = total
        v.st[S + q : S + q + 1, :] = spread
        edge = jnp.where(
            t == 0, v.tile[q, pl.ds(W - 1, R, stride=W), :], v.tile[q, pl.ds(0, R, stride=W), :]
        )
        v.colf[q, 0:R, :] = edge
        v.rowf[q, 0:W, :] = jnp.where(hh == 0, value[TILE - W : TILE], value[0:W])
        v.corf[q : q + 1, :] = jnp.where(hh == 0, edge[R - 1 : R], edge[0:1])
    v.st_in[t, s] = v.st[...]

    @pl.when(stray)
    def _():
        v.colf_in[p] = v.colf[...]

    def w_pack(k, raw):
        @pl.when(home)
        def _():
            for cc in range(C):
                rows = pl.ds(pl.multiple_of(QR * (2 * g + cc), 8), QR)
                for pp in range(2):
                    pieces = [raw[tap, rows, :][:, pp * CB : (pp + 1) * CB] for tap in range(9)]
                    pack(v.wpack.at[k, pp, cc], padded(jnp.concatenate(pieces, axis=0)), WM)

    loads[1].wait()
    w_pack(0, v.w1_raw)

    def w_own(k, raw):
        @pl.when(home)
        def _():
            for tap in range(9):
                w = raw[tap]
                v.wown[k, tap * CB : (tap + 1) * CB, :] = padded(
                    jnp.where(p == 0, w[:, 0:CB], w[:, CB : 2 * CB])
                )

    w_own(0, v.w1_raw)

    row_id = lax.broadcasted_iota(jnp.int32, (LANES, LANES), 0)
    col_id = lax.broadcasted_iota(jnp.int32, (LANES, LANES), 1)
    same = ((row_id // per_group) == (col_id // per_group)) & (row_id < CB) & (col_id < CB)
    member = jnp.where(same, 1.0, 0.0).astype(F32)

    def group_sum(rows8):
        return jnp.dot(rows8, member, precision=HIGHEST, preferred_element_type=F32)

    def store_mat(k, q, tap, w):
        high, low = split_pair(w)
        v.mat[k, q, tap * LANES : tap * LANES + CB, 0:LANES] = high
        v.mat[k, q, tap * LANES : tap * LANES + CB, LANES : 2 * LANES] = low

    def own_copy(k):
        return remote(v.wown.at[k], v.wown.at[k], v.es.at[0], v.er.at[k], chan=oc)

    def own_mat(k):
        pl.when(stray)(own_copy(k).wait_recv)
        for tap in range(9):
            store_mat(k, s, tap, v.wown[k, tap * CB : (tap + 1) * CB, :])

    gap = jnp.zeros((LANES - CB, 2 * LANES), BF16)
    for k in range(2):
        for q in range(S):
            for tap in range(9):
                v.mat[k, q, tap * LANES + CB : (tap + 1) * LANES, :] = gap

    def z_copy(k, n, peer, slot, cc):
        return remote(
            v.wpack.at[k, lax.rem(peer, 2), cc], v.wq.at[k, slot, 2 * g + cc],
            v.zs.at[0], v.zr.at[k, n], space=peer, chan=cc,
        )

    def y_copy(k, n, z, which):
        ref = v.wq.at[k, z, which]
        return remote(ref, ref, v.ys.at[0], v.yr.at[k, n], groups=gy)

    def b_copy(k, n, z, which):
        ref = v.wq.at[k, z, which]
        return remote(ref, ref, v.bs.at[0], v.br.at[k, n], chan=oc)

    order = (far, far2, pair)

    def z_send(k, n):
        for cc in range(C):
            go_if(home, z_copy(k, n, order[n], s, cc))

    def relay(k, n):
        z = order[n]
        remote(
            v.wpack.at[k, 0, 0], v.wq.at[k, z, 2 * g + c], v.zs.at[0], v.zr.at[k, n],
            space=z, chan=t,
        ).wait_recv()
        y_copy(k, n, z, 2 * g + c).start()
        b_copy(k, n, z, 2 * g + c).start()

    def relay2(k, n, z):
        y_copy(k, n, z, 2 * gy + c).wait_recv()
        b_copy(k, n, z, 2 * gy + c).start()

    def nth_weights(i):
        flip = lax.rem(lax.div(i + 1, 2), 2)
        return 2 * lax.rem(hh + flip, 2) + lax.rem(p + lax.div(i, 2), 2)

    def nth_block(j):
        return 2 * lax.rem(t + lax.rem(j, 2), 2) + lax.rem(p + lax.div(j, 2), 2)

    def finish_weights(k, n, z):
        await_bytes(rows_of(2 * WM), v.br.at[k, n])
        for kk in range(4):
            at = 0
            for value in unpack(v.wq[k, z, kk], WQ):
                for n in range(value.shape[0] // 8):
                    tap, off = divmod(at, QR)
                    to = tap * CB + kk * QR + off
                    v.wf[to : to + 8, :] = value[n * 8 : n * 8 + 8]
                    at += 8
        for tap in range(9):
            store_mat(k, z, tap, v.wf[tap * CB : (tap + 1) * CB, :])

    pl.semaphore_wait(barrier, S * T * C)

    feat_copy = remote(v.a_pack, v.a_in.at[p], v.as_sem.at[0], v.ar_sem.at[0], tm=tx)

    def feat_part(m):
        blocks = pl.ds(2 * m, 2)
        return remote(
            v.a_pack.at[blocks], v.a_in.at[p, blocks], v.fs.at[0], v.fr.at[m], space=pair
        )

    def st_copy(dt, peer, mt, ms):
        return remote(
            v.st, v.st_in.at[mt, ms], v.ss_sem.at[0], v.sr_sem.at[0],
            space=peer, tm=tx if dt else t,
        )

    def col_copy(n, slot, **where):
        return remote(v.colf, v.colf_in.at[slot], v.cs_sem.at[0], v.cr_sem.at[slot], **where)

    hub = inner & home
    row_copy = remote(v.rowf, v.rowf_in, v.rs_sem.at[0], v.rr_sem.at[0], space=far2)

    def row_forward(n, **where):
        return remote(v.rowf_in, v.rowf_in, v.rs_sem.at[1], v.rr_sem.at[1], **where)

    def cor_copy(n, **where):
        return remote(v.corf, v.corf_in, v.os_sem.at[0], v.or_sem.at[0], **where)

    st_peers = [(0, far), (0, far2), (1, far), (1, far2), (0, pair), (1, pair), (1, s)]
    go_if(hub, row_copy)
    for dt, peer in st_peers:
        go(st_copy(dt, peer, t, s))
    for n, (peer, column) in enumerate(((far, t), (far2, t), (far, tx), (far2, tx))):
        go_if(inner & stray, cor_copy(n, space=peer, tm=column))
    go_if(stray, col_copy(0, p, tm=tx))
    go_if(stray, col_copy(1, p, space=pair))
    go_if(stray, col_copy(2, p, space=pair, tm=tx))
    go_if(home, feat_part(0))
    go_if(home, feat_part(1))
    go_if(home, feat_copy)
    z_send(0, 0)
    go_if(home, own_copy(0))
    z_send(0, 1)
    bias_copy = remote(v.bias_out, v.bias_in, v.is_sem.at[0], v.ir_sem.at[0], chan=oc)

    for load in loads[2 : len(early)]:
        load.wait()
    await_bytes(v.pw_raw, v.load_sem.at[len(early)])
    for n, (gain, shift) in enumerate(
        ((v.gain1, v.shift1), (v.gain2, v.shift2), (v.gain3, v.shift3))
    ):
        for j, ref in enumerate((gain, shift)):
            row = ref[...].reshape(1, CH)
            for q in range(S):
                v.prm[n, q, j : j + 1, :] = padded(row[:, q * CB : (q + 1) * CB])
    bias_row = jnp.broadcast_to(v.head_b[...].reshape(1, ZH), (ZH, ZH))
    diagonal = lax.broadcasted_iota(jnp.int32, (ZH, ZH), 0) == lax.broadcasted_iota(
        jnp.int32, (ZH, ZH), 1
    )
    my_bias = jnp.sum(jnp.where(diagonal, bias_row, 0.0), axis=1, keepdims=True)
    v.bias_out[...] = jnp.broadcast_to(my_bias, (ZH, LANES))
    go(bias_copy)
    own_mat(0)
    for tap in range(9):
        v.hw_send[tap] = padded(v.head_w[tap])

    @pl.when(hub)
    def _():
        row_copy.wait_recv()

    for n, where in enumerate((dict(space=pair), dict(tm=tx), dict(space=pair, tm=tx))):
        go_if(hub, row_forward(n, **where))
    z_send(0, 2)
    w_pack(1, v.w2_raw)
    w_own(1, v.w2_raw)
    go_if(home, own_copy(1))
    def feat_pass(m):
        ref = v.a_in.at[1 - p, pl.ds(2 * m, 2)]
        return remote(ref, ref, v.gs.at[0], v.fr.at[m], tm=tx)

    def pass_features(when):
        @pl.when(home & when)
        def _():
            for m in range(2):
                feat_part(m).wait_recv()
                feat_pass(m).start()

    pass_features(inner)
    relay(0, 0)
    pass_features(jnp.logical_not(inner))
    for n in (0, 2, 1):
        z_send(1, n)
    relay(0, 1)

    def hw_copy(n, slot, **where):
        return remote(v.hw_send, v.hwq.at[slot], v.hs.at[0], v.hr.at[slot], **where)

    @pl.when(hh == t)
    def _():
        v.hwq[c] = v.hw_send[...]

    def unpack_features(slot):
        for q in range(S):
            at = 0
            for value in unpack(v.a_in[slot, q], TILE):
                rows = pl.ds(pl.multiple_of(slot * TILE + at, 8), value.shape[0])
                v.feat_all[q, rows, :] = value
                at += value.shape[0]

    @pl.when(stray)
    def _():
        feat_copy.wait_recv()
        unpack_features(p)

    @pl.when(stray)
    def _():
        for m in range(2):
            feat_pass(m).wait_recv()

    unpack_features(1 - p)
    await_bytes(rows_of(8 * len(st_peers)), v.sr_sem.at[0])
    col_copy(1, 1 - p, space=pair).wait_recv()
    pl.when(home)(col_copy(0, p, tm=tx).wait_recv)
    cor_copy(0, space=far).wait_recv()
    pl.when(jnp.logical_not(hub))(row_forward(0, space=pair).wait_recv)

    scale = 1.0 / float(per_group * TILE * S * T)
    everyone = [v.st_in[tt, ss] for tt in range(T) for ss in range(S)]
    total8 = everyone[0]
    for part in everyone[1:]:
        total8 = total8 + part
    summed = group_sum(total8)
    center8 = summed * scale
    gathered = jnp.zeros((8, LANES), F32)
    for part in everyone:
        away = part * (1.0 / TILE) - center8
        gathered = gathered + away * away * float(TILE)
    inverse4 = lax.rsqrt((group_sum(gathered)[0:S] + summed[S : 2 * S]) * scale + EPSILON)

    def build_taps(n, q, value, columns, corner, row, center, inverse):
        gain, shift = v.prm[n, q, 0:1, :], v.prm[n, q, 1:2, :]

        def act(values):
            u = (values - center) * inverse * gain + shift
            return u / (1.0 + jnp.exp(-u))

        inside = act(value)
        line = act(row)
        top, bottom = jnp.where(hh == 1, line, 0.0), jnp.where(hh == 0, line, 0.0)
        tail = jnp.zeros((8, LANES), F32)
        for b in range(3):
            at = AT + 1 - b
            v.taps[q, b, AT + (LAST + 1) * W : AT + (LAST + 1) * W + 8, :] = tail
            v.taps[q, b, at : at + W, :] = top
            v.taps[q, b, at + W : at + W + REG, :] = inside
            v.taps[q, b, at + W + REG : at + 2 * W + REG, :] = bottom
        tip = act(corner)
        sides = [(0, 1, jnp.where(hh == 1, tip, 0.0)), (LAST, 1, jnp.where(hh == 0, tip, 0.0))]
        sides += [(1 + first, count, act(raw)) for first, count, raw in columns]
        for first, count, piece in sides:
            at = AT + first * W
            from_left = jnp.where(c == 1, piece, 0.0)
            from_right = jnp.where(c == 0, piece, 0.0)
            if count == 1:
                v.taps[q, 0, at : at + 1, :] = from_left
                v.taps[q, 2, at + W - 1 : at + W, :] = from_right
            else:
                v.taps[q, 0, pl.ds(at, count, stride=W), :] = from_left
                v.taps[q, 2, pl.ds(at + W - 1, count, stride=W), :] = from_right

    for q in range(S):
        v.nrm[q, 0:1, :] = center8[q : q + 1]
        v.nrm[q, 1:2, :] = inverse4[q : q + 1]
        v.nrm[q, 2:3, :] = v.corf_in[q : q + 1, :]

    def first_taps(q, carry):
        build_taps(
            0, q, v.feat_all[q],
            [(0, R, v.colf_in[0, q, 0:R, :]), (R, R, v.colf_in[1, q, 0:R, :])],
            v.nrm[q, 2:3, :], v.rowf_in[q, 0:W, :], v.nrm[q, 0:1, :], v.nrm[q, 1:2, :],
        )
        return carry

    def operand(q):
        highs, lows = [], []
        for a in range(3):
            for b in range(3):
                high, low = split_pair(v.taps[q, b, AT + a * W : AT + a * W + REG, :])
                highs.append(high)
                lows.append(low)
        return jnp.concatenate(
            [jnp.concatenate(highs, axis=1), jnp.concatenate(lows, axis=1)], axis=0
        )

    def conv_block(k, q):
        part = jnp.dot(operand(q), v.mat[k, q], preferred_element_type=F32)
        return part[0:REG, 0:LANES] + part[0:REG, LANES:] + part[REG:, 0:LANES]

    lax.fori_loop(0, S, first_taps, 0)
    relay2(0, 0, far)
    relay(0, 2)
    go_if(hh == t, hw_copy(0, c, chan=oc))
    go_if(hh == t, hw_copy(1, c, space=far))
    go_if(hh == t, hw_copy(2, c, space=far, chan=oc))
    v.acc[...] = jnp.zeros(v.acc.shape, F32)

    def first_step(i, carry):
        z = nth_weights(i)

        @pl.when(i > 0)
        def _():
            finish_weights(0, i - 1, z)

        v.acc[...] += conv_block(0, z)

        @pl.when(i < 2)
        def _():
            relay2(0, i + 1, nth_weights(i + 2))

        return carry

    lax.fori_loop(0, 4, first_step, 0)
    first = v.acc[...]
    v.conv_raw[own] = first

    def rim_exchange(k, full):
        value = full[...]
        total, spread = channel_stats(value)
        column = jnp.where(
            c == 0, full[pl.ds(W - 1, 2 * R, stride=W), :], full[pl.ds(0, 2 * R, stride=W), :]
        )
        row = jnp.where(hh == 0, value[REG - W : REG], value[0:W])
        corner = jnp.where(hh == 0, column[2 * R - 1 : 2 * R], column[0:1])
        for ref, first, rows in ((v.rowm, W, row), (v.colm, 2 * R, column), (v.corm, 1, corner)):
            ref[k, 0:first, :] = rows
            ref[k, first : first + 1, :] = total
            ref[k, first + 1 : first + 2, :] = spread
        copies = [
            remote(v.corm.at[k], v.corm_in.at[k], v.ks.at[0], v.kr.at[k], space=far, chan=oc),
            remote(v.rowm.at[k], v.rowm_in.at[k], v.ks.at[0], v.kr.at[k], space=far),
            remote(v.colm.at[k], v.colm_in.at[k], v.ks.at[0], v.kr.at[k], chan=oc),
        ]
        for copy in copies:
            go(copy)
        return total, spread

    def rim_finish(k, total, spread):
        await_bytes(rows_of(MR + up(W + 2, 8) + 8), v.kr.at[k])
        parts = [(total, spread)]
        for ref, first in ((v.rowm_in, W), (v.colm_in, 2 * R), (v.corm_in, 1)):
            parts.append((ref[k, first : first + 1, :], ref[k, first + 1 : first + 2, :]))
        whole = parts[0][0] + parts[1][0] + parts[2][0] + parts[3][0]
        wide = lambda row: jnp.broadcast_to(row, (8, LANES))
        center = group_sum(wide(whole))[0:1] * scale
        spreads = jnp.zeros((1, LANES), F32)
        for part_total, part_spread in parts:
            away = part_total * (1.0 / REG) - center
            spreads = spreads + part_spread + away * away * float(REG)
        inverse = lax.rsqrt(group_sum(wide(spreads))[0:1] * scale + EPSILON)
        return center, inverse

    rims1 = rim_exchange(0, v.conv_raw.at[own])
    pack(v.ypack, first, PM)
    near_copy = remote(v.ypack, v.yin.at[0], v.vs.at[0], v.vr.at[0], space=pair)
    go(near_copy)
    side_copy = remote(v.ypack, v.yin.at[2], v.vs.at[0], v.vr.at[1], tm=tx)
    go(side_copy)
    cross_copy = remote(v.yin.at[0], v.yin.at[1], v.vs.at[0], v.vr.at[2], tm=tx)
    own_mat(1)
    relay(1, 0)
    relay(1, 2)
    relay(1, 1)
    center, inverse = rim_finish(0, *rims1)
    v.rl_in[own, 0 : 2 * R, :] = v.colm_in[0, 0 : 2 * R, :]
    v.rl_in[own, 2 * R : 2 * R + 1, :] = v.corm_in[0, 0:1, :]
    v.rl_in[own, 2 * R + 1 : 2 * R + 2, :] = center
    v.rl_in[own, 2 * R + 2 : 2 * R + 3, :] = inverse
    v.rl_in[own, MR : MR + W, :] = v.rowm_in[0, 0:W, :]

    def rl_copy(n, q, **where):
        ref = v.rl_in.at[q]
        return remote(ref, ref, v.ls.at[0], v.lr.at[q], **where)

    go(rl_copy(0, own, space=pair))
    go(rl_copy(1, own, space=pair, tm=tx))
    go(rl_copy(2, own, tm=tx))

    def second_taps(q):
        build_taps(
            1, q, v.conv_raw[q], [(0, 2 * R, v.rl_in[q, 0 : 2 * R, :])],
            v.rl_in[q, 2 * R : 2 * R + 1, :], v.rl_in[q, MR : MR + W, :],
            v.rl_in[q, 2 * R + 1 : 2 * R + 2, :], v.rl_in[q, 2 * R + 2 : 2 * R + 3, :],
        )

    def second_step(j, carry):
        q = nth_block(j)

        @pl.when(j == 1)
        def _():
            side_copy.wait_recv()
            rl_copy(2, side, tm=tx).wait_recv()

        @pl.when(j == 2)
        def _():
            rl_copy(0, near, space=pair).wait_recv()

        @pl.when(j == 3)
        def _():
            cross_copy.wait_recv()
            rl_copy(1, cross, space=pair, tm=tx).wait_recv()

        @pl.when(j > 0)
        def _():
            at = 0
            for value in unpack(v.yin[lax.rem(j + 1, 3)], REG):
                v.conv_raw[q, at : at + value.shape[0], :] = value
                at += value.shape[0]

        second_taps(q)

        @pl.when(j == 0)
        def _():
            relay2(1, 0, far)
            near_copy.wait_recv()
            cross_copy.start()
            relay2(1, 2, pair)
            finish_weights(1, 0, far)

        @pl.when(j == 1)
        def _():
            relay2(1, 1, far2)

        @pl.when(j == 2)
        def _():
            finish_weights(1, 2, pair)
            finish_weights(1, 1, far2)

        v.acc[...] += conv_block(1, q)
        return carry

    v.acc[...] = v.feat_all[own]
    lax.fori_loop(0, S, second_step, 0)
    v.hid[...] = v.acc[...]
    rims2 = rim_exchange(1, v.hid)

    @pl.when(hh == t)
    def _():
        hw_copy(0, oc, chan=oc).wait_recv()

    @pl.when(hh != t)
    def _():
        for slot in range(C):
            hw_copy(1, slot, space=far).wait_recv()

    bias_copy.wait_recv()
    blank = jnp.zeros((LANES - 3 * Z, LANES), F32)
    for b in range(3):
        rows = [v.hwq[cc, a * 3 + b] for a in range(3) for cc in range(C)] + [blank]
        high, low = split_pair(jnp.concatenate(rows, axis=0))
        for place, value in ((3 * b, high), (3 * b + 1, high), (3 * b + 2, low)):
            v.wh_mat[:, place * LANES : (place + 1) * LANES] = value
    ours, other_bias = v.bias_out[...], v.bias_in[...]
    bias = jnp.where(
        own == 0,
        jnp.concatenate(
            [jnp.where(c == cc, ours, other_bias) for cc in range(C)], axis=0
        ),
        0.0,
    )

    for first, mat in ((0, v.wn_mat), (4 * (Z + 4), wc_out)):
        for b in range(2):
            for a in range(2):
                at = (b * 2 + a) * Z
                for n in range(strips):
                    high, low = split_pair(v.pw_raw[n, pl.ds(first + a * 2 + b, Z, stride=4), :])
                    lanes = slice(n * LANES, (n + 1) * LANES)
                    mat[at : at + Z, lanes] = high
                    mat[4 * Z + at : 4 * Z + at + Z, lanes] = high
                    mat[8 * Z + at : 8 * Z + at + Z, lanes] = low
    mark_sum = jnp.concatenate(
        [
            jnp.sum(v.pw_raw[n, 4 * Z : 4 * (Z + 4), :], axis=0, keepdims=True)
            for n in range(strips)
        ],
        axis=1,
    )

    PR, PC, PP = dims["PR"], dims["PC"], dims["PP"]
    FULLW = W * T
    cells, turned, patch = v.cells, v.turned, v.patch
    cells[...] = jnp.zeros(cells.shape, F32)
    patch[...] = jnp.zeros(patch.shape, F32)

    def build_patches():
        turned[...] = cells[...].T
        for b in range(2):
            picked = turned[pl.ds(b, PC, stride=2), :]
            for i in range(PR):
                patch[i * PP : i * PP + PC, b * 2 * Z : (b + 1) * 2 * Z] = picked[
                    :, i * 2 * Z : (i + 1) * 2 * Z
                ]

    for f in range(FR):
        for i in range(R):
            cells[i * Z : (i + 1) * Z, 0:FULLW] = v.noisy[f, i]
        build_patches()
        got = jnp.dot(split_columns(patch[:, 0 : 4 * Z]), v.wn_mat[...], preferred_element_type=F32)
        opening = (t * FR + f) == 0
        base_out[f] = got + v.patch_b[...].reshape(1, -1) + jnp.where(opening, mark_sum, 0.0)

    center, inverse = rim_finish(1, *rims2)
    build_taps(
        2, own, v.hid[...], [(0, 2 * R, v.colm_in[1, 0 : 2 * R, :])], v.corm_in[1, 0:1, :],
        v.rowm_in[1, 0:W, :], center, inverse,
    )

    columns = []
    for b in range(3):
        high, low = split_pair(v.taps[own, b, AT : AT + v.mixed.shape[0], :])
        columns += [high, low, high]
    v.mixed[...] = lax.dot_general(
        jnp.concatenate(columns, axis=1),
        v.wh_mat[...],
        (((1,), (1,)), ((), ())),
        preferred_element_type=F32,
    )
    for j in range(2):
        shifted = [v.mixed[j * TILE + a * W : j * TILE + a * W + LANES, :] for a in range(3)]
        joined = jnp.where(
            col_id < Z, shifted[0], jnp.where(col_id < 2 * Z, shifted[1], shifted[2])
        ).T
        v.lat_send[j] = joined[0:Z] + joined[Z : 2 * Z] + joined[2 * Z : 3 * Z] + bias
    v.lat_in[c, own] = v.lat_send[p]

    def lat_copy(dp, dt, dc, slot_c, slot_q):
        return remote(
            v.lat_send.at[1 - p if dp else p], v.lat_in.at[slot_c, slot_q],
            v.ts.at[0], v.tr.at[0],
            space=pair if dp else s, tm=tx if dt else t, chan=oc if dc else c,
        )

    hops = [(1, 1, 1), (1, 1, 0), (0, 1, 1), (0, 1, 0), (1, 0, 1), (1, 0, 0), (0, 0, 1)]
    for dp, dt, dc in hops:
        go_if(((tx if dt else t) == 0) | (c == 1), lat_copy(dp, dt, dc, c, own))

    pl.when(t == 0)(functools.partial(await_bytes, rows_of(7 * Z), v.tr.at[0]))
    pl.when((t == 1) & (c == 1))(functools.partial(await_bytes, rows_of(3 * Z), v.tr.at[0]))
    pl.when((t == 1) & (c == 0))(functools.partial(await_bytes, rows_of(4 * Z), v.tr.at[0]))

    def latent_of(tt):
        return v.lat_in[tt, 0] + v.lat_in[tt, 1] + v.lat_in[tt, 2] + v.lat_in[tt, 3]

    value = latent_of(t)
    for r in range(R):
        latent[r] = value[:, r * W : (r + 1) * W]
    for f in range(FR):
        cells[...] = jnp.zeros(cells.shape, F32)
        opening = (t * FR + f) == 0
        for tt in range(T):
            value = latent_of(tt)
            for i in range(R):
                cells[i * Z : (i + 1) * Z, tt * W : (tt + 1) * W] = value[:, i * W : (i + 1) * W]
        for i in range(R):
            rows = slice(i * Z, (i + 1) * Z)
            cells[rows, 0:FULLW] = jnp.where(opening, cells[rows, 0:FULLW], v.later[f, i])
        build_patches()
        patch_out[f] = patch[...]
    RR = up(W + 2, 8)
    drains = (
        (home, rows_of(S * AM), v.as_sem), (home, rows_of(S * AM), v.fs),
        (home, rows_of(S * AM), v.gs), (None, rows_of(8 * len(st_peers)), v.ss_sem),
        (stray, rows_of(3 * S * 8), v.cs_sem), (hub, rows_of(S * RR), v.rs_sem),
        (inner & stray, rows_of(4 * 8), v.os_sem), (None, rows_of(ZH), v.is_sem),
        (home, v.wq.at[0, pl.ds(0, 3)], v.zs), (None, v.wq.at[0, pl.ds(0, 3), pl.ds(0, 2)], v.ys),
        (None, v.wq.at[0, pl.ds(0, 3)], v.bs), (home, v.wown, v.es),
        (None, rows_of(2 * (MR + RR + 8)), v.ks), (None, v.yin, v.vs),
        (None, rows_of(3 * (MR + RR)), v.ls), (hh == t, rows_of(3 * 9 * ZH), v.hs),
        (c == 1, rows_of(7 * Z), v.ts), ((c == 0) & (t == 0), rows_of(3 * Z), v.ts),
        ((c == 0) & (t == 1), rows_of(4 * Z), v.ts),
    )
    for condition, ref, sem in drains:
        wait = functools.partial(await_bytes, ref, sem.at[0])
        wait() if condition is None else pl.when(condition)(wait)
    pl.when(hub)(functools.partial(await_bytes, rows_of(3 * S * RR), v.rs_sem.at[1]))


def up(value, unit):
    return -(-value // unit) * unit


def packed_rows(rows, width, unit):
    free = LANES - width
    if free <= 0 or width % free or rows % 8:
        return rows
    main = up(-(-rows * width // LANES), unit)
    fits = main < rows and (rows - main) * (width // free) <= main
    return main if fits else rows


def plan(mesh_shape, features, noisy_latents, patch_weight, head_weight):
    S, T, C, G = (mesh_shape[axis] for axis in ("space", "tm", "chan", "groups"))
    R, W, CH = features.shape
    FR, Z = noisy_latents.shape[:2]
    dims = dict(S=S, T=T, C=C, R=R, W=W, CH=CH, Z=Z, FR=FR)
    dims["PR"], dims["PC"] = R // 2, W * T // 2
    dims["PP"] = up(W * T // 2, 8)
    dims["N"] = patch_weight.shape[1]
    CB = CH // S
    TILE = R * W
    dims["AM"] = packed_rows(TILE, CB, 16)
    dims["PM"] = packed_rows(2 * TILE, CB, 8)
    dims["WQ"] = 9 * (CB // 4)
    dims["WM"] = packed_rows(dims["WQ"], CB, 8)
    fits = (
        (S, T, C, G) == (4, 2, 2, 2)
        and CH % S == 0
        and CB <= LANES
        and CB % (4 * 8) == 0
        and CB % (CH // NGROUP) == 0
        and TILE % 8 == 0
        and TILE <= LANES
        and R % 2 == 0
        and R <= 8
        and all(dims[name] % 8 == 0 for name in ("AM", "PM", "WQ", "WM"))
        and dims["WM"] > 8
        and 2 * R + 2 <= up(2 * R + 2, 8)
        and head_weight.shape[3] * C == Z
        and Z % 16 == 0
        and 3 * Z <= LANES
        and R * Z <= LANES
        and W * T <= LANES
        and W * T % 2 == 0
        and 4 * Z <= LANES
        and dims["N"] % LANES == 0
    )
    return dims if fits else None


def fused(dims, args):
    S, T, C = dims["S"], dims["T"], dims["C"]
    R, W, CH = dims["R"], dims["W"], dims["CH"]
    Z, FR, N = dims["Z"], dims["FR"], dims["N"]
    CB, NH = CH // S, CH // C
    TILE, REG = R * W, 2 * R * W
    (f, g1, s1, w1, g2, s2, w2, g3, s3, hw, hb, noisy, later, pw, pb) = args
    flat = lambda v: v.reshape((9,) + v.shape[2:])
    by_row = lambda v: jnp.transpose(v, (0, 2, 1, 3))
    operands = (
        f, g1, s1, flat(w1), g2, s2, flat(w2), g3, s3,
        flat(jnp.transpose(hw, (0, 1, 3, 2))), hb, by_row(noisy), by_row(later), pw, pb,
    )
    vmem = pl.BlockSpec(memory_space=pltpu.VMEM)
    far = pl.BlockSpec(memory_space=pl.ANY)
    dma = lambda *shape: pltpu.SemaphoreType.DMA(shape)
    buf = lambda *shape: pltpu.VMEM(shape, F32)
    half = lambda *shape: pltpu.VMEM(shape, BF16)
    PR, PC, PP = dims["PR"], dims["PC"], dims["PP"]
    MR, RR = up(2 * R + 2, 8), up(W + 2, 8)
    TR = up(8 + 2 * W + TILE + LANES, 8)
    scratch = {
        name: pltpu.VMEM(operands[k].shape, F32)
        for name, k in (
            ("feat", 0), ("gain1", 1), ("shift1", 2), ("w1_raw", 3), ("gain2", 4), ("shift2", 5),
            ("w2_raw", 6), ("gain3", 7), ("shift3", 8), ("head_w", 9), ("head_b", 10),
            ("noisy", 11), ("later", 12), ("patch_b", 14),
        )
    }
    scratch |= {
        "pw_raw": buf(N // LANES, pw.shape[0], LANES),
        "prm": buf(3, S, 8, LANES),
        "tile": buf(S, TILE, LANES),
        "feat_all": buf(S, REG, LANES),
        "a_pack": buf(S, dims["AM"], LANES),
        "a_in": buf(2, S, dims["AM"], LANES),
        "st": buf(8, LANES),
        "st_in": buf(T, S, 8, LANES),
        "colf": buf(S, 8, LANES),
        "colf_in": buf(2, S, 8, LANES),
        "rowf": buf(S, RR, LANES),
        "rowf_in": buf(S, RR, LANES),
        "corf": buf(8, LANES),
        "corf_in": buf(8, LANES),
        "wpack": buf(2, 2, C, dims["WM"], LANES),
        "wown": buf(2, 9 * CB, LANES),
        "bias_out": buf(Z // C, LANES),
        "bias_in": buf(Z // C, LANES),
        "wq": buf(2, S, 4, dims["WM"], LANES),
        "wf": buf(9 * CB, LANES),
        "mat": half(2, S, 9 * LANES, 2 * LANES),
        "taps": buf(S, 3, TR, LANES),
        "nrm": buf(S, 8, LANES),
        "acc": buf(REG, LANES),
        "conv_raw": buf(S, REG, LANES),
        "ypack": buf(dims["PM"], LANES),
        "yin": buf(3, dims["PM"], LANES),
        "hid": buf(REG, LANES),
        "colm": buf(2, MR, LANES),
        "colm_in": buf(2, MR, LANES),
        "rowm": buf(2, RR, LANES),
        "rowm_in": buf(2, RR, LANES),
        "corm": buf(2, 8, LANES),
        "corm_in": buf(2, 8, LANES),
        "rl_in": buf(S, MR + RR, LANES),
        "hw_send": buf(9, Z // C, LANES),
        "hwq": buf(C, 9, Z // C, LANES),
        "wh_mat": half(LANES, 9 * LANES),
        "wn_mat": half(12 * Z, N),
        "mixed": buf(TR - 8, LANES),
        "lat_send": buf(2, Z, LANES),
        "lat_in": buf(C, S, Z, LANES),
        "cells": buf(LANES, LANES),
        "turned": buf(LANES, LANES),
        "patch": buf(PR * PP, LANES),
        "load_sem": dma(15),
        "as_sem": dma(1), "ar_sem": dma(1), "fs": dma(1), "fr": dma(2), "gs": dma(1),
        "ss_sem": dma(1), "sr_sem": dma(1),
        "cs_sem": dma(1), "cr_sem": dma(2),
        "rs_sem": dma(2), "rr_sem": dma(2),
        "os_sem": dma(1), "or_sem": dma(1),
        "is_sem": dma(1), "ir_sem": dma(1),
        "zs": dma(1), "zr": dma(2, 3),
        "ys": dma(1), "yr": dma(2, 3),
        "bs": dma(1), "br": dma(2, 3),
        "es": dma(1), "er": dma(2),
        "ks": dma(1), "kr": dma(2),
        "vs": dma(1), "vr": dma(3),
        "ls": dma(1), "lr": dma(S),
        "hs": dma(1), "hr": dma(C),
        "ts": dma(1), "tr": dma(1),
    }
    patch, base, wc, latent = pl.pallas_call(
        functools.partial(fused_kernel, dims, tuple(scratch)),
        out_shape=(
            jax.ShapeDtypeStruct((FR, PR * PP, LANES), F32),
            jax.ShapeDtypeStruct((FR, PR * PP, N), F32),
            jax.ShapeDtypeStruct((12 * Z, N), BF16),
            jax.ShapeDtypeStruct((R, Z, W), F32),
        ),
        in_specs=[pl.BlockSpec(memory_space=pltpu.HBM)] * 15,
        out_specs=(vmem, vmem, vmem, vmem),
        scratch_shapes=list(scratch.values()),
        compiler_params=pltpu.CompilerParams(
            collective_id=0, has_side_effects=True, vmem_limit_bytes=32 * 2**20
        ),
        name="fused_block",
    )(*[pltpu.with_memory_space_constraint(v, pltpu.HBM) for v in operands])
    NB = 4 if N % (4 * LANES) == 0 else 1
    tokens, latent = pl.pallas_call(
        functools.partial(finish_kernel, dims, NB),
        out_shape=(
            jax.ShapeDtypeStruct((PR, PC, FR, N), F32),
            jax.ShapeDtypeStruct((R, Z, W), F32),
        ),
        in_specs=[vmem] * 4,
        out_specs=(pl.BlockSpec(memory_space=pltpu.HBM), pl.BlockSpec(memory_space=pltpu.HBM)),
        scratch_shapes=[buf(PR, PC, FR, N), dma(NB + 1)],
        compiler_params=pltpu.CompilerParams(vmem_limit_bytes=8 * 2**20),
        name="finish_tokens",
    )(patch, base, wc, latent)
    return jnp.transpose(tokens, (2, 0, 1, 3)), jnp.transpose(latent, (0, 2, 1))


def solution(mesh):
    shape = dict(mesh.shape)

    def step(*args):
        dims = plan(shape, args[0], args[11], args[13], args[9])
        return on_device(*args) if dims is None else fused(dims, args)

    return jax.shard_map(
        step,
        mesh=mesh,
        in_specs=(
            P(("groups", "space"), "tm", None),
            P(),
            P(),
            P(None, None, "space", "chan"),
            P(),
            P(),
            P(None, None, "space", "chan"),
            P(),
            P(),
            P(None, None, "space", "chan"),
            P("chan"),
            P(("groups", "tm"), None, "space", None),
            P(("groups", "tm"), None, "space", None),
            P(None, "chan"),
            P("chan"),
        ),
        out_specs=(P(("groups", "tm"), "space", None, "chan"), P(("groups", "space"), "tm", None)),
        check_vma=False,
    )
```

```python
import functools
import types

import jax
import jax.numpy as jnp
from jax import lax
from jax.experimental import pallas as pl
from jax.experimental.pallas import tpu as pltpu
from jax.sharding import PartitionSpec as P

NGROUP = 32


EPSILON = 1e-06
HIGHEST = lax.Precision.HIGHEST


def padded_2(cells, sides, width):
    for axis, dim in sides:
        count = lax.axis_size(axis)
        ends = count - 1
        head = lax.slice_in_dim(cells, 0, width, axis=dim)
        tail = lax.slice_in_dim(cells, cells.shape[dim] - width, cells.shape[dim], axis=dim)
        cells = jnp.concatenate(
            [
                lax.ppermute(tail, axis, [(i, (i + 1) % count) for i in range(ends)]),
                cells,
                lax.ppermute(head, axis, [((i + 1) % count, i) for i in range(ends)]),
            ],
            axis=dim,
        )
    return cells


def group_stats(inner, count_all):
    grouped = inner.reshape(-1, NGROUP, inner.shape[-1] // NGROUP)
    totals, squares = lax.psum(
        (jnp.sum(grouped, axis=(0, 2)), jnp.sum(grouped * grouped, axis=(0, 2))), ("space", "tm")
    )
    center = totals / count_all
    spread = squares / count_all - center * center
    return (center, lax.rsqrt(spread + EPSILON))


def normalize_act(values, stats, gain, shift):
    center, inverse = stats
    grouped = values.reshape(values.shape[:-1] + (NGROUP, values.shape[-1] // NGROUP))
    scaled = (grouped - center[:, None]) * inverse[:, None]
    return jax.nn.silu(scaled.reshape(values.shape) * gain + shift)


def tap_columns(padded, rows_out, cols_out):
    shifted = [
        padded[row_tap : row_tap + rows_out, col_tap : col_tap + cols_out, :]
        for row_tap in range(3)
        for col_tap in range(3)
    ]
    return jnp.stack(shifted, axis=2).reshape(rows_out * cols_out, 9, padded.shape[-1])


def add_taps(columns, piece):
    depth = piece.shape[2]
    picked = columns.reshape(columns.shape[0], 9 * depth)
    return jnp.dot(
        picked,
        piece.reshape(9 * depth, piece.shape[3]),
        precision=HIGHEST,
        preferred_element_type=jnp.float32,
    )


def wide_conv(padded, weight, rows_out, cols_out):
    columns = tap_columns(padded, rows_out, cols_out)
    summed = add_taps(columns, lax.all_gather(weight, "space", axis=2, tiled=True))
    return lax.all_gather(summed.reshape(rows_out, cols_out, -1), "chan", axis=2, tiled=True)


def border_rim(values):
    return padded_2(values, (("space", 0), ("tm", 1)), 1)


def on_device(
    features,
    norm1_gain,
    norm1_shift,
    conv1_weight,
    norm2_gain,
    norm2_shift,
    conv2_weight,
    head_gain,
    head_shift,
    head_weight,
    head_bias,
    noisy_latents,
    later_cond,
    patch_weight,
    patch_bias,
):
    tile_rows = features.shape[0]
    tile_cols = features.shape[1]
    count_all = float(
        tile_rows
        * tile_cols
        * lax.axis_size("space")
        * lax.axis_size("tm")
        * (features.shape[2] // NGROUP)
    )
    first_stats = group_stats(features, count_all)
    active = normalize_act(features, first_stats, norm1_gain, norm1_shift)
    first_conv = wide_conv(border_rim(active), conv1_weight, tile_rows, tile_cols)
    second_stats = group_stats(first_conv, count_all)
    second_act = normalize_act(first_conv, second_stats, norm2_gain, norm2_shift)
    second_conv = wide_conv(border_rim(second_act), conv2_weight, tile_rows, tile_cols)
    hidden = features + second_conv
    head_stats = group_stats(hidden, count_all)
    head_act = normalize_act(hidden, head_stats, head_gain, head_shift)
    head_pad = padded_2(head_act, (("space", 0), ("tm", 1)), 1)
    head_columns = tap_columns(head_pad, tile_rows, tile_cols)
    latent_part = (
        add_taps(head_columns, lax.all_gather(head_weight, "space", axis=2, tiled=True)) + head_bias
    )
    image_latent = lax.all_gather(
        latent_part.reshape(tile_rows, tile_cols, -1), "chan", axis=2, tiled=True
    )
    latent_row = lax.all_gather(image_latent, "tm", axis=1, tiled=True)
    frame_count = noisy_latents.shape[0]
    full_width = noisy_latents.shape[3]
    frame_ids = lax.axis_index("tm") * frame_count + jnp.arange(frame_count)
    opening = frame_ids == 0
    condition = jnp.where(
        opening[:, None, None, None], jnp.transpose(latent_row, (2, 0, 1))[None], later_cond
    )
    marks = jnp.broadcast_to(
        opening.astype(jnp.float32)[:, None, None, None], (frame_count, 4, tile_rows, full_width)
    )
    stacked = jnp.concatenate([noisy_latents, marks, condition], axis=1)
    channel_count = stacked.shape[1]
    patches = (
        stacked.reshape(frame_count, channel_count, tile_rows // 2, 2, full_width // 2, 2)
        .transpose(0, 2, 4, 1, 3, 5)
        .reshape(-1, channel_count * 4)
    )
    tokens = (
        jnp.dot(patches, patch_weight, precision=HIGHEST, preferred_element_type=jnp.float32)
        + patch_bias
    )
    return (tokens.reshape(frame_count, tile_rows // 2, full_width // 2, -1), image_latent)


MESH = pl.DeviceIdType.MESH
LANES = 128
BF16 = jnp.bfloat16
F32 = jnp.float32


def split_pair(values):
    high = values.astype(BF16)
    return high, (values - high.astype(F32)).astype(BF16)


def split_columns(values):
    high, low = split_pair(values)
    return jnp.concatenate([high, low, high], axis=1)


def finish_kernel(dims, parts, patch, base, wc, latent_in, tokens, latent, tok, sem):
    PC, PP, Z, FR = dims["PC"], dims["PP"], dims["Z"], dims["FR"]
    width = dims["N"] // parts
    copies = [pltpu.make_async_copy(latent_in, latent, sem.at[parts])]
    copies[0].start()
    lhs = [split_columns(patch[f, :, 0 : 4 * Z]) for f in range(FR)]
    for n in range(parts):
        lanes = slice(n * width, (n + 1) * width)
        for f in range(FR):
            got = base[f, :, lanes] + jnp.dot(lhs[f], wc[:, lanes], preferred_element_type=F32)
            for p in range(dims["PR"]):
                tok[p, :, f, lanes] = got[p * PP : p * PP + PC, :]
        view = (slice(None), slice(None), slice(None), pl.ds(n * width, width))
        copies.append(pltpu.make_async_copy(tok.at[view], tokens.at[view], sem.at[n]))
        copies[-1].start()
    for copy in copies:
        copy.wait()


def fused_kernel(dims, names, *refs):
    S, T, C = dims["S"], dims["T"], dims["C"]
    R, W, CH = dims["R"], dims["W"], dims["CH"]
    Z, FR = dims["Z"], dims["FR"]
    CB = CH // S
    TILE = R * W
    REG = 2 * TILE
    per_group = CH // NGROUP
    ZH = Z // C
    AM, PM, WQ, WM = dims["AM"], dims["PM"], dims["WQ"], dims["WM"]
    QR = CB // 4
    AT = 8
    LAST = 2 * R + 1
    MR = up(2 * R + 2, 8)
    (
        feat_hbm, gain1_hbm, shift1_hbm, w1_hbm, gain2_hbm, shift2_hbm, w2_hbm, gain3_hbm,
        shift3_hbm, head_w_hbm, head_b_hbm, noisy_hbm, later_hbm, pw_hbm, patch_b_hbm,
    ) = refs[:15]
    patch_out, base_out, wc_out, latent = refs[15:19]
    v = types.SimpleNamespace(**dict(zip(names, refs[19:])))
    s = lax.axis_index("space")
    t = lax.axis_index("tm")
    c = lax.axis_index("chan")
    g = lax.axis_index("groups")
    p, hh = lax.rem(s, 2), lax.div(s, 2)
    pair, far, far2 = s + 1 - 2 * p, lax.rem(s + 2, 4), 3 - s
    tx, oc, gy = 1 - t, 1 - c, 1 - g
    inner = (p + hh) == 1
    own, side = 2 * t + p, 2 * tx + p
    near, cross = 2 * t + 1 - p, 2 * tx + 1 - p
    home = c == t
    stray = c != t

    def remote(src, dst, ssem, rsem, **where):
        return pltpu.make_async_remote_copy(
            src_ref=src, dst_ref=dst, send_sem=ssem, recv_sem=rsem, device_id=where,
            device_id_type=MESH,
        )

    def go(copy):
        copy.start()

    def go_if(condition, copy):
        @pl.when(condition)
        def _():
            copy.start()

    def rows_of(count):
        return v.wf.at[pl.ds(0, count)]

    def await_bytes(ref, sem):
        pltpu.make_async_copy(ref, ref, sem).wait()

    v.lat_in[...] = jnp.zeros(v.lat_in.shape, F32)
    barrier = pltpu.get_barrier_semaphore()
    for ds in range(S):
        for dt in range(T):
            for dc in range(C):
                if ds or dt or dc:
                    pl.semaphore_signal(
                        barrier,
                        inc=1,
                        device_id={
                            "space": lax.rem(s + ds, S),
                            "tm": lax.rem(t + dt, T),
                            "chan": lax.rem(c + dc, C),
                        },
                        device_id_type=MESH,
                    )
    pl.semaphore_signal(barrier, inc=1, device_id={"groups": gy}, device_id_type=MESH)

    early = (
        (feat_hbm, v.feat), (w1_hbm, v.w1_raw), (gain1_hbm, v.gain1), (shift1_hbm, v.shift1),
        (w2_hbm, v.w2_raw), (gain2_hbm, v.gain2), (shift2_hbm, v.shift2),
        (gain3_hbm, v.gain3), (shift3_hbm, v.shift3), (head_w_hbm, v.head_w),
        (head_b_hbm, v.head_b), (noisy_hbm, v.noisy), (later_hbm, v.later),
        (patch_b_hbm, v.patch_b),
    )
    loads = [
        pltpu.make_async_copy(src, dst, v.load_sem.at[k]) for k, (src, dst) in enumerate(early)
    ]
    strips = v.pw_raw.shape[0]
    loads += [
        pltpu.make_async_copy(
            pw_hbm.at[:, n * LANES : (n + 1) * LANES], v.pw_raw.at[n], v.load_sem.at[len(early)]
        )
        for n in range(strips)
    ]
    for load in loads:
        load.start()

    def padded(values, width=LANES):
        rows = values.shape[0]
        if width == values.shape[1]:
            return values
        return jnp.concatenate([values, jnp.zeros((rows, width - values.shape[1]), values.dtype)], axis=1)

    def pack(dst, value, main):
        rows = value.shape[0]
        dst[...] = value[0:main]
        rest = rows - main
        free = LANES - CB
        for j in range(CB // free if rest else 0):
            dst[j * rest : (j + 1) * rest, CB:LANES] = value[main:rows, j * free : (j + 1) * free]

    def unpack(value, rows):
        main = value.shape[0]
        rest = rows - main
        if not rest:
            return (value,)
        free = LANES - CB
        columns = [value[j * rest : (j + 1) * rest, CB:LANES] for j in range(CB // free)]
        return value, padded(jnp.concatenate(columns, axis=1))

    def channel_stats(values):
        total = jnp.sum(values, axis=0, keepdims=True)
        middle = total * (1.0 / values.shape[0])
        away = values - middle
        return total, jnp.sum(away * away, axis=0, keepdims=True)

    loads[0].wait()
    for r in range(R):
        line = v.feat[r]
        for q in range(S):
            v.tile[q, r * W : (r + 1) * W, :] = padded(line[:, q * CB : (q + 1) * CB])
    own_rows = pl.ds(pl.multiple_of(p * TILE, 8), TILE)
    for q in range(S):
        value = v.tile[q]
        v.feat_all[q, own_rows, :] = value
        pack(v.a_pack.at[q], value, AM)
        total, spread = channel_stats(value)
        v.st[q : q + 1, :] = total
        v.st[S + q : S + q + 1, :] = spread
        edge = jnp.where(
            t == 0, v.tile[q, pl.ds(W - 1, R, stride=W), :], v.tile[q, pl.ds(0, R, stride=W), :]
        )
        v.colf[q, 0:R, :] = edge
        v.rowf[q, 0:W, :] = jnp.where(hh == 0, value[TILE - W : TILE], value[0:W])
        v.corf[q : q + 1, :] = jnp.where(hh == 0, edge[R - 1 : R], edge[0:1])
    v.st_in[t, s] = v.st[...]

    @pl.when(stray)
    def _():
        v.colf_in[p] = v.colf[...]

    def w_pack(k, raw):
        @pl.when(home)
        def _():
            for cc in range(C):
                rows = pl.ds(pl.multiple_of(QR * (2 * g + cc), 8), QR)
                for pp in range(2):
                    pieces = [raw[tap, rows, :][:, pp * CB : (pp + 1) * CB] for tap in range(9)]
                    pack(v.wpack.at[k, pp, cc], padded(jnp.concatenate(pieces, axis=0)), WM)

    loads[1].wait()
    w_pack(0, v.w1_raw)

    def w_own(k, raw):
        @pl.when(home)
        def _():
            for tap in range(9):
                w = raw[tap]
                v.wown[k, tap * CB : (tap + 1) * CB, :] = padded(
                    jnp.where(p == 0, w[:, 0:CB], w[:, CB : 2 * CB])
                )


    row_id = lax.broadcasted_iota(jnp.int32, (LANES, LANES), 0)
    col_id = lax.broadcasted_iota(jnp.int32, (LANES, LANES), 1)
    same = ((row_id // per_group) == (col_id // per_group)) & (row_id < CB) & (col_id < CB)
    member = jnp.where(same, 1.0, 0.0).astype(F32)

    def group_sum(rows8):
        return jnp.dot(rows8, member, precision=HIGHEST, preferred_element_type=F32)

    def store_mat(k, q, tap, w):
        high, low = split_pair(w)
        v.mat[k, q, tap * LANES : tap * LANES + CB, 0:LANES] = high
        v.mat[k, q, tap * LANES : tap * LANES + CB, LANES : 2 * LANES] = low

    def own_copy(k):
        return remote(v.wown.at[k], v.wown.at[k], v.es.at[0], v.er.at[k], chan=oc)

    def own_mat(k):
        pl.when(stray)(own_copy(k).wait_recv)
        for tap in range(9):
            store_mat(k, s, tap, v.wown[k, tap * CB : (tap + 1) * CB, :])

    gap = jnp.zeros((LANES - CB, 2 * LANES), BF16)
    for k in range(2):
        for q in range(S):
            for tap in range(9):
                v.mat[k, q, tap * LANES + CB : (tap + 1) * LANES, :] = gap

    def z_copy(k, n, peer, slot, cc):
        return remote(
            v.wpack.at[k, lax.rem(peer, 2), cc], v.wq.at[k, slot, 2 * g + cc],
            v.zs.at[0], v.zr.at[k, n], space=peer, chan=cc,
        )

    def y_copy(k, n, z, which):
        ref = v.wq.at[k, z, which]
        return remote(ref, ref, v.ys.at[0], v.yr.at[k, n], groups=gy)

    def b_copy(k, n, z, which):
        ref = v.wq.at[k, z, which]
        return remote(ref, ref, v.bs.at[0], v.br.at[k, n], chan=oc)

    order = (far, far2, pair)

    def z_send(k, n):
        for cc in range(C):
            go_if(home, z_copy(k, n, order[n], s, cc))

    def relay(k, n):
        z = order[n]
        remote(
            v.wpack.at[k, 0, 0], v.wq.at[k, z, 2 * g + c], v.zs.at[0], v.zr.at[k, n],
            space=z, chan=t,
        ).wait_recv()
        y_copy(k, n, z, 2 * g + c).start()
        b_copy(k, n, z, 2 * g + c).start()

    def relay2(k, n, z):
        y_copy(k, n, z, 2 * gy + c).wait_recv()
        b_copy(k, n, z, 2 * gy + c).start()

    def nth_weights(i):
        flip = lax.rem(lax.div(i + 1, 2), 2)
        return 2 * lax.rem(hh + flip, 2) + lax.rem(p + lax.div(i, 2), 2)

    def nth_block(j):
        return 2 * lax.rem(t + lax.rem(j, 2), 2) + lax.rem(p + lax.div(j, 2), 2)

    def finish_weights(k, n, z):
        await_bytes(rows_of(2 * WM), v.br.at[k, n])
        for kk in range(4):
            at = 0
            for value in unpack(v.wq[k, z, kk], WQ):
                for n in range(value.shape[0] // 8):
                    tap, off = divmod(at, QR)
                    to = tap * CB + kk * QR + off
                    v.wf[to : to + 8, :] = value[n * 8 : n * 8 + 8]
                    at += 8
        for tap in range(9):
            store_mat(k, z, tap, v.wf[tap * CB : (tap + 1) * CB, :])

    pl.semaphore_wait(barrier, S * T * C)

    feat_copy = remote(v.a_pack, v.a_in.at[p], v.as_sem.at[0], v.ar_sem.at[0], tm=tx)

    def feat_part(m):
        blocks = pl.ds(2 * m, 2)
        return remote(
            v.a_pack.at[blocks], v.a_in.at[p, blocks], v.fs.at[0], v.fr.at[m], space=pair
        )

    def st_copy(dt, peer, mt, ms):
        return remote(
            v.st, v.st_in.at[mt, ms], v.ss_sem.at[0], v.sr_sem.at[0],
            space=peer, tm=tx if dt else t,
        )

    def col_copy(n, slot, **where):
        return remote(v.colf, v.colf_in.at[slot], v.cs_sem.at[0], v.cr_sem.at[slot], **where)

    hub = inner & home
    row_copy = remote(v.rowf, v.rowf_in, v.rs_sem.at[0], v.rr_sem.at[0], space=far2)

    def row_forward(n, **where):
        return remote(v.rowf_in, v.rowf_in, v.rs_sem.at[1], v.rr_sem.at[1], **where)

    def cor_copy(n, **where):
        return remote(v.corf, v.corf_in, v.os_sem.at[0], v.or_sem.at[0], **where)

    st_peers = [(0, far), (0, far2), (1, far), (1, far2), (0, pair), (1, pair), (1, s)]
    go_if(hub, row_copy)
    for dt, peer in st_peers:
        go(st_copy(dt, peer, t, s))
    for n, (peer, column) in enumerate(((far, t), (far2, t), (far, tx), (far2, tx))):
        go_if(inner & stray, cor_copy(n, space=peer, tm=column))
    go_if(stray, col_copy(0, p, tm=tx))
    go_if(stray, col_copy(1, p, space=pair))
    go_if(stray, col_copy(2, p, space=pair, tm=tx))
    go_if(home, feat_part(0))
    go_if(home, feat_part(1))
    go_if(home, feat_copy)
    z_send(0, 0)
    z_send(0, 1)
    w_own(0, v.w1_raw)
    go_if(home, own_copy(0))
    bias_copy = remote(v.bias_out, v.bias_in, v.is_sem.at[0], v.ir_sem.at[0], chan=oc)

    for load in loads[2 : len(early)]:
        load.wait()
    await_bytes(v.pw_raw, v.load_sem.at[len(early)])
    for n, (gain, shift) in enumerate(
        ((v.gain1, v.shift1), (v.gain2, v.shift2), (v.gain3, v.shift3))
    ):
        for j, ref in enumerate((gain, shift)):
            row = ref[...].reshape(1, CH)
            for q in range(S):
                v.prm[n, q, j : j + 1, :] = padded(row[:, q * CB : (q + 1) * CB])
    bias_row = jnp.broadcast_to(v.head_b[...].reshape(1, ZH), (ZH, ZH))
    diagonal = lax.broadcasted_iota(jnp.int32, (ZH, ZH), 0) == lax.broadcasted_iota(
        jnp.int32, (ZH, ZH), 1
    )
    my_bias = jnp.sum(jnp.where(diagonal, bias_row, 0.0), axis=1, keepdims=True)
    v.bias_out[...] = jnp.broadcast_to(my_bias, (ZH, LANES))
    go(bias_copy)
    for tap in range(9):
        v.hw_send[tap] = padded(v.head_w[tap])

    @pl.when(hub)
    def _():
        row_copy.wait_recv()

    for n, where in enumerate((dict(space=pair), dict(tm=tx), dict(space=pair, tm=tx))):
        go_if(hub, row_forward(n, **where))
    z_send(0, 2)
    own_mat(0)
    w_pack(1, v.w2_raw)
    w_own(1, v.w2_raw)
    go_if(home, own_copy(1))
    def feat_pass(m):
        ref = v.a_in.at[1 - p, pl.ds(2 * m, 2)]
        return remote(ref, ref, v.gs.at[0], v.fr.at[m], tm=tx)

    def pass_features(when):
        @pl.when(home & when)
        def _():
            for m in range(2):
                feat_part(m).wait_recv()
                feat_pass(m).start()

    pass_features(inner)
    relay(0, 0)
    pass_features(jnp.logical_not(inner))
    for n in (0, 2, 1):
        z_send(1, n)
    relay(0, 1)

    def hw_copy(n, slot, **where):
        return remote(v.hw_send, v.hwq.at[slot], v.hs.at[0], v.hr.at[slot], **where)

    @pl.when(hh == t)
    def _():
        v.hwq[c] = v.hw_send[...]

    def unpack_features(slot):
        for q in range(S):
            at = 0
            for value in unpack(v.a_in[slot, q], TILE):
                rows = pl.ds(pl.multiple_of(slot * TILE + at, 8), value.shape[0])
                v.feat_all[q, rows, :] = value
                at += value.shape[0]

    @pl.when(stray)
    def _():
        feat_copy.wait_recv()
        unpack_features(p)

    @pl.when(stray)
    def _():
        for m in range(2):
            feat_pass(m).wait_recv()

    unpack_features(1 - p)
    await_bytes(rows_of(8 * len(st_peers)), v.sr_sem.at[0])
    col_copy(1, 1 - p, space=pair).wait_recv()
    pl.when(home)(col_copy(0, p, tm=tx).wait_recv)
    cor_copy(0, space=far).wait_recv()
    pl.when(jnp.logical_not(hub))(row_forward(0, space=pair).wait_recv)

    scale = 1.0 / float(per_group * TILE * S * T)
    everyone = [v.st_in[tt, ss] for tt in range(T) for ss in range(S)]
    total8 = everyone[0]
    for part in everyone[1:]:
        total8 = total8 + part
    summed = group_sum(total8)
    center8 = summed * scale
    gathered = jnp.zeros((8, LANES), F32)
    for part in everyone:
        away = part * (1.0 / TILE) - center8
        gathered = gathered + away * away * float(TILE)
    inverse4 = lax.rsqrt((group_sum(gathered)[0:S] + summed[S : 2 * S]) * scale + EPSILON)

    def build_taps(n, q, value, columns, corner, row, center, inverse):
        gain, shift = v.prm[n, q, 0:1, :], v.prm[n, q, 1:2, :]

        def act(values):
            u = (values - center) * inverse * gain + shift
            return u / (1.0 + jnp.exp(-u))

        inside = act(value)
        line = act(row)
        top, bottom = jnp.where(hh == 1, line, 0.0), jnp.where(hh == 0, line, 0.0)
        tail = jnp.zeros((8, LANES), F32)
        for b in range(3):
            at = AT + 1 - b
            v.taps[q, b, AT + (LAST + 1) * W : AT + (LAST + 1) * W + 8, :] = tail
            v.taps[q, b, at : at + W, :] = top
            v.taps[q, b, at + W : at + W + REG, :] = inside
            v.taps[q, b, at + W + REG : at + 2 * W + REG, :] = bottom
        tip = act(corner)
        sides = [(0, 1, jnp.where(hh == 1, tip, 0.0)), (LAST, 1, jnp.where(hh == 0, tip, 0.0))]
        sides += [(1 + first, count, act(raw)) for first, count, raw in columns]
        for first, count, piece in sides:
            at = AT + first * W
            from_left = jnp.where(c == 1, piece, 0.0)
            from_right = jnp.where(c == 0, piece, 0.0)
            if count == 1:
                v.taps[q, 0, at : at + 1, :] = from_left
                v.taps[q, 2, at + W - 1 : at + W, :] = from_right
            else:
                v.taps[q, 0, pl.ds(at, count, stride=W), :] = from_left
                v.taps[q, 2, pl.ds(at + W - 1, count, stride=W), :] = from_right

    for q in range(S):
        v.nrm[q, 0:1, :] = center8[q : q + 1]
        v.nrm[q, 1:2, :] = inverse4[q : q + 1]
        v.nrm[q, 2:3, :] = v.corf_in[q : q + 1, :]

    def first_taps(q, carry):
        build_taps(
            0, q, v.feat_all[q],
            [(0, R, v.colf_in[0, q, 0:R, :]), (R, R, v.colf_in[1, q, 0:R, :])],
            v.nrm[q, 2:3, :], v.rowf_in[q, 0:W, :], v.nrm[q, 0:1, :], v.nrm[q, 1:2, :],
        )
        return carry

    def operand(q):
        highs, lows = [], []
        for a in range(3):
            for b in range(3):
                high, low = split_pair(v.taps[q, b, AT + a * W : AT + a * W + REG, :])
                highs.append(high)
                lows.append(low)
        return jnp.concatenate(
            [jnp.concatenate(highs, axis=1), jnp.concatenate(lows, axis=1)], axis=0
        )

    def conv_block(k, q):
        part = jnp.dot(operand(q), v.mat[k, q], preferred_element_type=F32)
        return part[0:REG, 0:LANES] + part[0:REG, LANES:] + part[REG:, 0:LANES]

    lax.fori_loop(0, S, first_taps, 0)
    relay2(0, 0, far)
    relay(0, 2)
    v.acc[...] = jnp.zeros(v.acc.shape, F32)

    def first_step(i, carry):
        z = nth_weights(i)

        @pl.when(i > 0)
        def _():
            finish_weights(0, i - 1, z)

        v.acc[...] += conv_block(0, z)

        @pl.when(i < 2)
        def _():
            relay2(0, i + 1, nth_weights(i + 2))

        @pl.when(i == 2)
        def _():
            relay(1, 0)

        return carry

    lax.fori_loop(0, 4, first_step, 0)
    first = v.acc[...]
    v.conv_raw[own] = first

    def rim_exchange(k, full):
        value = full[...]
        total, spread = channel_stats(value)
        column = jnp.where(
            c == 0, full[pl.ds(W - 1, 2 * R, stride=W), :], full[pl.ds(0, 2 * R, stride=W), :]
        )
        row = jnp.where(hh == 0, value[REG - W : REG], value[0:W])
        corner = jnp.where(hh == 0, column[2 * R - 1 : 2 * R], column[0:1])
        for ref, first, rows in ((v.rowm, W, row), (v.colm, 2 * R, column), (v.corm, 1, corner)):
            ref[k, 0:first, :] = rows
            ref[k, first : first + 1, :] = total
            ref[k, first + 1 : first + 2, :] = spread
        copies = [
            remote(v.corm.at[k], v.corm_in.at[k], v.ks.at[0], v.kr.at[k], space=far, chan=oc),
            remote(v.rowm.at[k], v.rowm_in.at[k], v.ks.at[0], v.kr.at[k], space=far),
            remote(v.colm.at[k], v.colm_in.at[k], v.ks.at[0], v.kr.at[k], chan=oc),
        ]
        for copy in copies:
            go(copy)
        return total, spread

    def rim_finish(k, total, spread):
        await_bytes(rows_of(MR + up(W + 2, 8) + 8), v.kr.at[k])
        parts = [(total, spread)]
        for ref, first in ((v.rowm_in, W), (v.colm_in, 2 * R), (v.corm_in, 1)):
            parts.append((ref[k, first : first + 1, :], ref[k, first + 1 : first + 2, :]))
        whole = parts[0][0] + parts[1][0] + parts[2][0] + parts[3][0]
        wide = lambda row: jnp.broadcast_to(row, (8, LANES))
        center = group_sum(wide(whole))[0:1] * scale
        spreads = jnp.zeros((1, LANES), F32)
        for part_total, part_spread in parts:
            away = part_total * (1.0 / REG) - center
            spreads = spreads + part_spread + away * away * float(REG)
        inverse = lax.rsqrt(group_sum(wide(spreads))[0:1] * scale + EPSILON)
        return center, inverse

    rims1 = rim_exchange(0, v.conv_raw.at[own])
    pack(v.ypack, first, PM)
    near_copy = remote(v.ypack, v.yin.at[0], v.vs.at[0], v.vr.at[0], space=pair)
    go(near_copy)
    side_copy = remote(v.ypack, v.yin.at[2], v.vs.at[0], v.vr.at[1], tm=tx)
    go(side_copy)
    PH = up(PM // 2, 8)
    upper, lower = pl.ds(0, PH), pl.ds(PH, PM - PH)
    cross_x = remote(
        v.yin.at[0, upper], v.yin.at[1, upper], v.vs.at[0], v.vr.at[2], tm=tx
    )
    cross_z = remote(
        v.yin.at[2, lower], v.yin.at[1, lower], v.vs.at[0], v.vr.at[2], space=pair
    )
    own_mat(1)
    relay(1, 2)
    relay(1, 1)
    center, inverse = rim_finish(0, *rims1)
    v.rl_in[own, 0 : 2 * R, :] = v.colm_in[0, 0 : 2 * R, :]
    v.rl_in[own, 2 * R : 2 * R + 1, :] = v.corm_in[0, 0:1, :]
    v.rl_in[own, 2 * R + 1 : 2 * R + 2, :] = center
    v.rl_in[own, 2 * R + 2 : 2 * R + 3, :] = inverse
    v.rl_in[own, MR : MR + W, :] = v.rowm_in[0, 0:W, :]

    def rl_copy(n, q, **where):
        ref = v.rl_in.at[q]
        return remote(ref, ref, v.ls.at[0], v.lr.at[q], **where)

    go(rl_copy(0, own, space=pair))
    go(rl_copy(1, own, space=pair, tm=tx))
    go(rl_copy(2, own, tm=tx))
    go_if(hh == t, hw_copy(0, c, chan=oc))
    go_if(hh == t, hw_copy(1, c, space=far))

    def second_taps(q):
        build_taps(
            1, q, v.conv_raw[q], [(0, 2 * R, v.rl_in[q, 0 : 2 * R, :])],
            v.rl_in[q, 2 * R : 2 * R + 1, :], v.rl_in[q, MR : MR + W, :],
            v.rl_in[q, 2 * R + 1 : 2 * R + 2, :], v.rl_in[q, 2 * R + 2 : 2 * R + 3, :],
        )

    def second_step(j, carry):
        q = nth_block(j)

        @pl.when(j == 1)
        def _():
            relay2(1, 2, pair)
            rl_copy(2, side, tm=tx).wait_recv()

        @pl.when(j == 2)
        def _():
            relay2(1, 1, far2)

        @pl.when(j == 2)
        def _():
            rl_copy(0, near, space=pair).wait_recv()

        @pl.when(j == 3)
        def _():
            await_bytes(rows_of(PM), v.vr.at[2])
            rl_copy(1, cross, space=pair, tm=tx).wait_recv()

        @pl.when((j == 3) & (hh != t))
        def _():
            hw_copy(1, c, space=far).wait_recv()
            remote(v.hwq.at[c], v.hwq.at[c], v.hs.at[0], v.hr.at[c], chan=oc).start()

        @pl.when(j > 0)
        def _():
            at = 0
            for value in unpack(v.yin[lax.rem(j + 1, 3)], REG):
                v.conv_raw[q, at : at + value.shape[0], :] = value
                at += value.shape[0]

        second_taps(q)

        @pl.when(j == 0)
        def _():
            relay2(1, 0, far)

        @pl.when(j == jnp.where(t == hh, 1, 0))
        def _():
            finish_weights(1, 0, far)

        @pl.when(j == 2)
        def _():
            finish_weights(1, 2 - lax.rem(t + hh, 2), near)

        @pl.when(j == 3)
        def _():
            finish_weights(1, 1 + lax.rem(t + hh, 2), cross)

        v.acc[...] += conv_block(1, q)

        @pl.when(j == 0)
        def _():
            side_copy.wait_recv()
            cross_z.start()
            near_copy.wait_recv()
            cross_x.start()

        return carry

    v.acc[...] = v.feat_all[own]
    lax.fori_loop(0, S, second_step, 0)
    v.hid[...] = v.acc[...]
    rims2 = rim_exchange(1, v.hid)

    hw_copy(0, oc, chan=oc).wait_recv()
    bias_copy.wait_recv()
    blank = jnp.zeros((LANES - 3 * Z, LANES), F32)
    for b in range(3):
        rows = [v.hwq[cc, a * 3 + b] for a in range(3) for cc in range(C)] + [blank]
        high, low = split_pair(jnp.concatenate(rows, axis=0))
        for place, value in ((3 * b, high), (3 * b + 1, high), (3 * b + 2, low)):
            v.wh_mat[:, place * LANES : (place + 1) * LANES] = value
    ours, other_bias = v.bias_out[...], v.bias_in[...]
    bias = jnp.where(
        own == 0,
        jnp.concatenate(
            [jnp.where(c == cc, ours, other_bias) for cc in range(C)], axis=0
        ),
        0.0,
    )

    for first, mat in ((0, v.wn_mat), (4 * (Z + 4), wc_out)):
        for b in range(2):
            for a in range(2):
                at = (b * 2 + a) * Z
                for n in range(strips):
                    high, low = split_pair(v.pw_raw[n, pl.ds(first + a * 2 + b, Z, stride=4), :])
                    lanes = slice(n * LANES, (n + 1) * LANES)
                    mat[at : at + Z, lanes] = high
                    mat[4 * Z + at : 4 * Z + at + Z, lanes] = high
                    mat[8 * Z + at : 8 * Z + at + Z, lanes] = low
    mark_sum = jnp.concatenate(
        [
            jnp.sum(v.pw_raw[n, 4 * Z : 4 * (Z + 4), :], axis=0, keepdims=True)
            for n in range(strips)
        ],
        axis=1,
    )

    PR, PC, PP = dims["PR"], dims["PC"], dims["PP"]
    FULLW = W * T
    cells, turned, patch = v.cells, v.turned, v.patch
    cells[...] = jnp.zeros(cells.shape, F32)
    patch[...] = jnp.zeros(patch.shape, F32)

    def build_patches():
        turned[...] = cells[...].T
        for b in range(2):
            picked = turned[pl.ds(b, PC, stride=2), :]
            for i in range(PR):
                patch[i * PP : i * PP + PC, b * 2 * Z : (b + 1) * 2 * Z] = picked[
                    :, i * 2 * Z : (i + 1) * 2 * Z
                ]

    for f in range(FR):
        for i in range(R):
            cells[i * Z : (i + 1) * Z, 0:FULLW] = v.noisy[f, i]
        build_patches()
        got = jnp.dot(split_columns(patch[:, 0 : 4 * Z]), v.wn_mat[...], preferred_element_type=F32)
        opening = (t * FR + f) == 0
        base_out[f] = got + v.patch_b[...].reshape(1, -1) + jnp.where(opening, mark_sum, 0.0)

    center, inverse = rim_finish(1, *rims2)
    build_taps(
        2, own, v.hid[...], [(0, 2 * R, v.colm_in[1, 0 : 2 * R, :])], v.corm_in[1, 0:1, :],
        v.rowm_in[1, 0:W, :], center, inverse,
    )

    columns = []
    for b in range(3):
        high, low = split_pair(v.taps[own, b, AT : AT + v.mixed.shape[0], :])
        columns += [high, low, high]
    v.mixed[...] = lax.dot_general(
        jnp.concatenate(columns, axis=1),
        v.wh_mat[...],
        (((1,), (1,)), ((), ())),
        preferred_element_type=F32,
    )
    for j in range(2):
        shifted = [v.mixed[j * TILE + a * W : j * TILE + a * W + LANES, :] for a in range(3)]
        joined = jnp.where(
            col_id < Z, shifted[0], jnp.where(col_id < 2 * Z, shifted[1], shifted[2])
        ).T
        v.lat_send[j] = joined[0:Z] + joined[Z : 2 * Z] + joined[2 * Z : 3 * Z] + bias
    v.lat_in[c, own] = v.lat_send[p]

    def lat_copy(dp, dt, dc, slot_c, slot_q):
        return remote(
            v.lat_send.at[1 - p if dp else p], v.lat_in.at[slot_c, slot_q],
            v.ts.at[0], v.tr.at[0],
            space=pair if dp else s, tm=tx if dt else t, chan=oc if dc else c,
        )

    hops = [(1, 1, 1), (1, 1, 0), (0, 1, 1), (0, 1, 0), (1, 0, 1), (1, 0, 0), (0, 0, 1)]
    for dp, dt, dc in hops:
        go_if(((tx if dt else t) == 0) | (c == 1), lat_copy(dp, dt, dc, c, own))

    pl.when(t == 0)(functools.partial(await_bytes, rows_of(7 * Z), v.tr.at[0]))
    pl.when((t == 1) & (c == 1))(functools.partial(await_bytes, rows_of(3 * Z), v.tr.at[0]))
    pl.when((t == 1) & (c == 0))(functools.partial(await_bytes, rows_of(4 * Z), v.tr.at[0]))

    def latent_of(tt):
        return v.lat_in[tt, 0] + v.lat_in[tt, 1] + v.lat_in[tt, 2] + v.lat_in[tt, 3]

    value = latent_of(t)
    for r in range(R):
        latent[r] = value[:, r * W : (r + 1) * W]
    for f in range(FR):
        cells[...] = jnp.zeros(cells.shape, F32)
        opening = (t * FR + f) == 0
        for tt in range(T):
            value = latent_of(tt)
            for i in range(R):
                cells[i * Z : (i + 1) * Z, tt * W : (tt + 1) * W] = value[:, i * W : (i + 1) * W]
        for i in range(R):
            rows = slice(i * Z, (i + 1) * Z)
            cells[rows, 0:FULLW] = jnp.where(opening, cells[rows, 0:FULLW], v.later[f, i])
        build_patches()
        patch_out[f] = patch[...]
    RR = up(W + 2, 8)
    drains = (
        (home, rows_of(S * AM), v.as_sem), (home, rows_of(S * AM), v.fs),
        (home, rows_of(S * AM), v.gs), (None, rows_of(8 * len(st_peers)), v.ss_sem),
        (stray, rows_of(3 * S * 8), v.cs_sem), (hub, rows_of(S * RR), v.rs_sem),
        (inner & stray, rows_of(4 * 8), v.os_sem), (None, rows_of(ZH), v.is_sem),
        (home, v.wq.at[0, pl.ds(0, 3)], v.zs), (None, v.wq.at[0, pl.ds(0, 3), pl.ds(0, 2)], v.ys),
        (None, v.wq.at[0, pl.ds(0, 3)], v.bs), (home, v.wown, v.es),
        (None, rows_of(2 * (MR + RR + 8)), v.ks), (None, v.yin, v.vs),
        (None, rows_of(3 * (MR + RR)), v.ls), (hh == t, rows_of(2 * 9 * ZH), v.hs),
        (hh != t, rows_of(9 * ZH), v.hs),
        (c == 1, rows_of(7 * Z), v.ts), ((c == 0) & (t == 0), rows_of(3 * Z), v.ts),
        ((c == 0) & (t == 1), rows_of(4 * Z), v.ts),
    )
    for condition, ref, sem in drains:
        wait = functools.partial(await_bytes, ref, sem.at[0])
        wait() if condition is None else pl.when(condition)(wait)
    pl.when(hub)(functools.partial(await_bytes, rows_of(3 * S * RR), v.rs_sem.at[1]))


def up(value, unit):
    return -(-value // unit) * unit


def packed_rows(rows, width, unit):
    free = LANES - width
    if free <= 0 or width % free or rows % 8:
        return rows
    main = up(-(-rows * width // LANES), unit)
    fits = main < rows and (rows - main) * (width // free) <= main
    return main if fits else rows


def plan(mesh_shape, features, noisy_latents, patch_weight, head_weight):
    S, T, C, G = (mesh_shape[axis] for axis in ("space", "tm", "chan", "groups"))
    R, W, CH = features.shape
    FR, Z = noisy_latents.shape[:2]
    dims = dict(S=S, T=T, C=C, R=R, W=W, CH=CH, Z=Z, FR=FR)
    dims["PR"], dims["PC"] = R // 2, W * T // 2
    dims["PP"] = up(W * T // 2, 8)
    dims["N"] = patch_weight.shape[1]
    CB = CH // S
    TILE = R * W
    dims["AM"] = packed_rows(TILE, CB, 16)
    dims["PM"] = packed_rows(2 * TILE, CB, 8)
    dims["WQ"] = 9 * (CB // 4)
    dims["WM"] = packed_rows(dims["WQ"], CB, 8)
    fits = (
        (S, T, C, G) == (4, 2, 2, 2)
        and CH % S == 0
        and CB <= LANES
        and CB % (4 * 8) == 0
        and CB % (CH // NGROUP) == 0
        and TILE % 8 == 0
        and TILE <= LANES
        and R % 2 == 0
        and R <= 8
        and all(dims[name] % 8 == 0 for name in ("AM", "PM", "WQ", "WM"))
        and dims["WM"] > 8
        and 2 * R + 2 <= up(2 * R + 2, 8)
        and head_weight.shape[3] * C == Z
        and Z % 16 == 0
        and 3 * Z <= LANES
        and R * Z <= LANES
        and W * T <= LANES
        and W * T % 2 == 0
        and 4 * Z <= LANES
        and dims["N"] % LANES == 0
    )
    return dims if fits else None


def fused(dims, args):
    S, T, C = dims["S"], dims["T"], dims["C"]
    R, W, CH = dims["R"], dims["W"], dims["CH"]
    Z, FR, N = dims["Z"], dims["FR"], dims["N"]
    CB, NH = CH // S, CH // C
    TILE, REG = R * W, 2 * R * W
    (f, g1, s1, w1, g2, s2, w2, g3, s3, hw, hb, noisy, later, pw, pb) = args
    flat = lambda v: v.reshape((9,) + v.shape[2:])
    by_row = lambda v: jnp.transpose(v, (0, 2, 1, 3))
    operands = (
        f, g1, s1, flat(w1), g2, s2, flat(w2), g3, s3,
        flat(jnp.transpose(hw, (0, 1, 3, 2))), hb, by_row(noisy), by_row(later), pw, pb,
    )
    vmem = pl.BlockSpec(memory_space=pltpu.VMEM)
    far = pl.BlockSpec(memory_space=pl.ANY)
    dma = lambda *shape: pltpu.SemaphoreType.DMA(shape)
    buf = lambda *shape: pltpu.VMEM(shape, F32)
    half = lambda *shape: pltpu.VMEM(shape, BF16)
    PR, PC, PP = dims["PR"], dims["PC"], dims["PP"]
    MR, RR = up(2 * R + 2, 8), up(W + 2, 8)
    TR = up(8 + 2 * W + TILE + LANES, 8)
    scratch = {
        name: pltpu.VMEM(operands[k].shape, F32)
        for name, k in (
            ("feat", 0), ("gain1", 1), ("shift1", 2), ("w1_raw", 3), ("gain2", 4), ("shift2", 5),
            ("w2_raw", 6), ("gain3", 7), ("shift3", 8), ("head_w", 9), ("head_b", 10),
            ("noisy", 11), ("later", 12), ("patch_b", 14),
        )
    }
    scratch |= {
        "pw_raw": buf(N // LANES, pw.shape[0], LANES),
        "prm": buf(3, S, 8, LANES),
        "tile": buf(S, TILE, LANES),
        "feat_all": buf(S, REG, LANES),
        "a_pack": buf(S, dims["AM"], LANES),
        "a_in": buf(2, S, dims["AM"], LANES),
        "st": buf(8, LANES),
        "st_in": buf(T, S, 8, LANES),
        "colf": buf(S, 8, LANES),
        "colf_in": buf(2, S, 8, LANES),
        "rowf": buf(S, RR, LANES),
        "rowf_in": buf(S, RR, LANES),
        "corf": buf(8, LANES),
        "corf_in": buf(8, LANES),
        "wpack": buf(2, 2, C, dims["WM"], LANES),
        "wown": buf(2, 9 * CB, LANES),
        "bias_out": buf(Z // C, LANES),
        "bias_in": buf(Z // C, LANES),
        "wq": buf(2, S, 4, dims["WM"], LANES),
        "wf": buf(9 * CB, LANES),
        "mat": half(2, S, 9 * LANES, 2 * LANES),
        "taps": buf(S, 3, TR, LANES),
        "nrm": buf(S, 8, LANES),
        "acc": buf(REG, LANES),
        "conv_raw": buf(S, REG, LANES),
        "ypack": buf(dims["PM"], LANES),
        "yin": buf(3, dims["PM"], LANES),
        "hid": buf(REG, LANES),
        "colm": buf(2, MR, LANES),
        "colm_in": buf(2, MR, LANES),
        "rowm": buf(2, RR, LANES),
        "rowm_in": buf(2, RR, LANES),
        "corm": buf(2, 8, LANES),
        "corm_in": buf(2, 8, LANES),
        "rl_in": buf(S, MR + RR, LANES),
        "hw_send": buf(9, Z // C, LANES),
        "hwq": buf(C, 9, Z // C, LANES),
        "wh_mat": half(LANES, 9 * LANES),
        "wn_mat": half(12 * Z, N),
        "mixed": buf(TR - 8, LANES),
        "lat_send": buf(2, Z, LANES),
        "lat_in": buf(C, S, Z, LANES),
        "cells": buf(LANES, LANES),
        "turned": buf(LANES, LANES),
        "patch": buf(PR * PP, LANES),
        "load_sem": dma(15),
        "as_sem": dma(1), "ar_sem": dma(1), "fs": dma(1), "fr": dma(2), "gs": dma(1),
        "ss_sem": dma(1), "sr_sem": dma(1),
        "cs_sem": dma(1), "cr_sem": dma(2),
        "rs_sem": dma(2), "rr_sem": dma(2),
        "os_sem": dma(1), "or_sem": dma(1),
        "is_sem": dma(1), "ir_sem": dma(1),
        "zs": dma(1), "zr": dma(2, 3),
        "ys": dma(1), "yr": dma(2, 3),
        "bs": dma(1), "br": dma(2, 3),
        "es": dma(1), "er": dma(2),
        "ks": dma(1), "kr": dma(2),
        "vs": dma(1), "vr": dma(3),
        "ls": dma(1), "lr": dma(S),
        "hs": dma(1), "hr": dma(C),
        "ts": dma(1), "tr": dma(1),
    }
    patch, base, wc, latent = pl.pallas_call(
        functools.partial(fused_kernel, dims, tuple(scratch)),
        out_shape=(
            jax.ShapeDtypeStruct((FR, PR * PP, LANES), F32),
            jax.ShapeDtypeStruct((FR, PR * PP, N), F32),
            jax.ShapeDtypeStruct((12 * Z, N), BF16),
            jax.ShapeDtypeStruct((R, Z, W), F32),
        ),
        in_specs=[pl.BlockSpec(memory_space=pltpu.HBM)] * 15,
        out_specs=(vmem, vmem, vmem, vmem),
        scratch_shapes=list(scratch.values()),
        compiler_params=pltpu.CompilerParams(
            collective_id=0, has_side_effects=True, vmem_limit_bytes=32 * 2**20
        ),
        name="fused_block",
    )(*[pltpu.with_memory_space_constraint(v, pltpu.HBM) for v in operands])
    NB = 4 if N % (4 * LANES) == 0 else 1
    tokens, latent = pl.pallas_call(
        functools.partial(finish_kernel, dims, NB),
        out_shape=(
            jax.ShapeDtypeStruct((PR, PC, FR, N), F32),
            jax.ShapeDtypeStruct((R, Z, W), F32),
        ),
        in_specs=[vmem] * 4,
        out_specs=(pl.BlockSpec(memory_space=pltpu.HBM), pl.BlockSpec(memory_space=pltpu.HBM)),
        scratch_shapes=[buf(PR, PC, FR, N), dma(NB + 1)],
        compiler_params=pltpu.CompilerParams(vmem_limit_bytes=8 * 2**20),
        name="finish_tokens",
    )(patch, base, wc, latent)
    return jnp.transpose(tokens, (2, 0, 1, 3)), jnp.transpose(latent, (0, 2, 1))


def solution(mesh):
    shape = dict(mesh.shape)

    def step(*args):
        dims = plan(shape, args[0], args[11], args[13], args[9])
        return on_device(*args) if dims is None else fused(dims, args)

    return jax.shard_map(
        step,
        mesh=mesh,
        in_specs=(
            P(("groups", "space"), "tm", None),
            P(),
            P(),
            P(None, None, "space", "chan"),
            P(),
            P(),
            P(None, None, "space", "chan"),
            P(),
            P(),
            P(None, None, "space", "chan"),
            P("chan"),
            P(("groups", "tm"), None, "space", None),
            P(("groups", "tm"), None, "space", None),
            P(None, "chan"),
            P("chan"),
        ),
        out_specs=(P(("groups", "tm"), "space", None, "chan"), P(("groups", "space"), "tm", None)),
        check_vma=False,
    )
```

```python
import functools
import types

import jax
import jax.numpy as jnp
from jax import lax
from jax.experimental import pallas as pl
from jax.experimental.pallas import tpu as pltpu
from jax.sharding import PartitionSpec as P

NGROUP = 32


EPSILON = 1e-06
HIGHEST = lax.Precision.HIGHEST


def padded_2(cells, sides, width):
    for axis, dim in sides:
        count = lax.axis_size(axis)
        ends = count - 1
        head = lax.slice_in_dim(cells, 0, width, axis=dim)
        tail = lax.slice_in_dim(cells, cells.shape[dim] - width, cells.shape[dim], axis=dim)
        cells = jnp.concatenate(
            [
                lax.ppermute(tail, axis, [(i, (i + 1) % count) for i in range(ends)]),
                cells,
                lax.ppermute(head, axis, [((i + 1) % count, i) for i in range(ends)]),
            ],
            axis=dim,
        )
    return cells


def group_stats(inner, count_all):
    grouped = inner.reshape(-1, NGROUP, inner.shape[-1] // NGROUP)
    totals, squares = lax.psum(
        (jnp.sum(grouped, axis=(0, 2)), jnp.sum(grouped * grouped, axis=(0, 2))), ("space", "tm")
    )
    center = totals / count_all
    spread = squares / count_all - center * center
    return (center, lax.rsqrt(spread + EPSILON))


def normalize_act(values, stats, gain, shift):
    center, inverse = stats
    grouped = values.reshape(values.shape[:-1] + (NGROUP, values.shape[-1] // NGROUP))
    scaled = (grouped - center[:, None]) * inverse[:, None]
    return jax.nn.silu(scaled.reshape(values.shape) * gain + shift)


def tap_columns(padded, rows_out, cols_out):
    shifted = [
        padded[row_tap : row_tap + rows_out, col_tap : col_tap + cols_out, :]
        for row_tap in range(3)
        for col_tap in range(3)
    ]
    return jnp.stack(shifted, axis=2).reshape(rows_out * cols_out, 9, padded.shape[-1])


def add_taps(columns, piece):
    depth = piece.shape[2]
    picked = columns.reshape(columns.shape[0], 9 * depth)
    return jnp.dot(
        picked,
        piece.reshape(9 * depth, piece.shape[3]),
        precision=HIGHEST,
        preferred_element_type=jnp.float32,
    )


def wide_conv(padded, weight, rows_out, cols_out):
    columns = tap_columns(padded, rows_out, cols_out)
    summed = add_taps(columns, lax.all_gather(weight, "space", axis=2, tiled=True))
    return lax.all_gather(summed.reshape(rows_out, cols_out, -1), "chan", axis=2, tiled=True)


def border_rim(values):
    return padded_2(values, (("space", 0), ("tm", 1)), 1)


def on_device(
    features,
    norm1_gain,
    norm1_shift,
    conv1_weight,
    norm2_gain,
    norm2_shift,
    conv2_weight,
    head_gain,
    head_shift,
    head_weight,
    head_bias,
    noisy_latents,
    later_cond,
    patch_weight,
    patch_bias,
):
    tile_rows = features.shape[0]
    tile_cols = features.shape[1]
    count_all = float(
        tile_rows
        * tile_cols
        * lax.axis_size("space")
        * lax.axis_size("tm")
        * (features.shape[2] // NGROUP)
    )
    first_stats = group_stats(features, count_all)
    active = normalize_act(features, first_stats, norm1_gain, norm1_shift)
    first_conv = wide_conv(border_rim(active), conv1_weight, tile_rows, tile_cols)
    second_stats = group_stats(first_conv, count_all)
    second_act = normalize_act(first_conv, second_stats, norm2_gain, norm2_shift)
    second_conv = wide_conv(border_rim(second_act), conv2_weight, tile_rows, tile_cols)
    hidden = features + second_conv
    head_stats = group_stats(hidden, count_all)
    head_act = normalize_act(hidden, head_stats, head_gain, head_shift)
    head_pad = padded_2(head_act, (("space", 0), ("tm", 1)), 1)
    head_columns = tap_columns(head_pad, tile_rows, tile_cols)
    latent_part = (
        add_taps(head_columns, lax.all_gather(head_weight, "space", axis=2, tiled=True)) + head_bias
    )
    image_latent = lax.all_gather(
        latent_part.reshape(tile_rows, tile_cols, -1), "chan", axis=2, tiled=True
    )
    latent_row = lax.all_gather(image_latent, "tm", axis=1, tiled=True)
    frame_count = noisy_latents.shape[0]
    full_width = noisy_latents.shape[3]
    frame_ids = lax.axis_index("tm") * frame_count + jnp.arange(frame_count)
    opening = frame_ids == 0
    condition = jnp.where(
        opening[:, None, None, None], jnp.transpose(latent_row, (2, 0, 1))[None], later_cond
    )
    marks = jnp.broadcast_to(
        opening.astype(jnp.float32)[:, None, None, None], (frame_count, 4, tile_rows, full_width)
    )
    stacked = jnp.concatenate([noisy_latents, marks, condition], axis=1)
    channel_count = stacked.shape[1]
    patches = (
        stacked.reshape(frame_count, channel_count, tile_rows // 2, 2, full_width // 2, 2)
        .transpose(0, 2, 4, 1, 3, 5)
        .reshape(-1, channel_count * 4)
    )
    tokens = (
        jnp.dot(patches, patch_weight, precision=HIGHEST, preferred_element_type=jnp.float32)
        + patch_bias
    )
    return (tokens.reshape(frame_count, tile_rows // 2, full_width // 2, -1), image_latent)


MESH = pl.DeviceIdType.MESH
LANES = 128
BF16 = jnp.bfloat16
F32 = jnp.float32


def split_pair(values):
    high = values.astype(BF16)
    return high, (values - high.astype(F32)).astype(BF16)


def split_columns(values):
    high, low = split_pair(values)
    return jnp.concatenate([high, low, high], axis=1)


def finish_kernel(dims, parts, patch, base, wc, latent_in, tokens, latent, tok, sem):
    PC, PP, Z, FR = dims["PC"], dims["PP"], dims["Z"], dims["FR"]
    width = dims["N"] // parts
    copies = [pltpu.make_async_copy(latent_in, latent, sem.at[parts])]
    copies[0].start()
    lhs = [split_columns(patch[f, :, 0 : 4 * Z]) for f in range(FR)]
    for n in range(parts):
        lanes = slice(n * width, (n + 1) * width)
        for f in range(FR):
            got = base[f, :, lanes] + jnp.dot(lhs[f], wc[:, lanes], preferred_element_type=F32)
            for p in range(dims["PR"]):
                tok[p, :, f, lanes] = got[p * PP : p * PP + PC, :]
        view = (slice(None), slice(None), slice(None), pl.ds(n * width, width))
        copies.append(pltpu.make_async_copy(tok.at[view], tokens.at[view], sem.at[n]))
        copies[-1].start()
    for copy in copies:
        copy.wait()


def fused_kernel(dims, names, *refs):
    S, T, C = dims["S"], dims["T"], dims["C"]
    R, W, CH = dims["R"], dims["W"], dims["CH"]
    Z, FR = dims["Z"], dims["FR"]
    CB = CH // S
    TILE = R * W
    REG = 2 * TILE
    per_group = CH // NGROUP
    ZH = Z // C
    AM, PM, WQ, WM = dims["AM"], dims["PM"], dims["WQ"], dims["WM"]
    QR = CB // 4
    AT = 8
    LAST = 2 * R + 1
    MR = up(2 * R + 2, 8)
    (
        feat_hbm, gain1_hbm, shift1_hbm, w1_hbm, gain2_hbm, shift2_hbm, w2_hbm, gain3_hbm,
        shift3_hbm, head_w_hbm, head_b_hbm, noisy_hbm, later_hbm, pw_hbm, patch_b_hbm,
    ) = refs[:15]
    patch_out, base_out, wc_out, latent = refs[15:19]
    v = types.SimpleNamespace(**dict(zip(names, refs[19:])))
    s = lax.axis_index("space")
    t = lax.axis_index("tm")
    c = lax.axis_index("chan")
    g = lax.axis_index("groups")
    p, hh = lax.rem(s, 2), lax.div(s, 2)
    pair, far, far2 = s + 1 - 2 * p, lax.rem(s + 2, 4), 3 - s
    tx, oc, gy = 1 - t, 1 - c, 1 - g
    inner = (p + hh) == 1
    own, side = 2 * t + p, 2 * tx + p
    near, cross = 2 * t + 1 - p, 2 * tx + 1 - p
    home = c == t
    stray = c != t

    def remote(src, dst, ssem, rsem, **where):
        return pltpu.make_async_remote_copy(
            src_ref=src, dst_ref=dst, send_sem=ssem, recv_sem=rsem, device_id=where,
            device_id_type=MESH,
        )

    def go(copy):
        copy.start()

    def go_if(condition, copy):
        @pl.when(condition)
        def _():
            copy.start()

    def rows_of(count):
        return v.wf.at[pl.ds(0, count)]

    def await_bytes(ref, sem):
        pltpu.make_async_copy(ref, ref, sem).wait()

    v.lat_in[...] = jnp.zeros(v.lat_in.shape, F32)
    barrier = pltpu.get_barrier_semaphore()
    for ds in range(S):
        for dt in range(T):
            for dc in range(C):
                if ds or dt or dc:
                    pl.semaphore_signal(
                        barrier,
                        inc=1,
                        device_id={
                            "space": lax.rem(s + ds, S),
                            "tm": lax.rem(t + dt, T),
                            "chan": lax.rem(c + dc, C),
                        },
                        device_id_type=MESH,
                    )
    pl.semaphore_signal(barrier, inc=1, device_id={"groups": gy}, device_id_type=MESH)

    early = (
        (feat_hbm, v.feat), (w1_hbm, v.w1_raw), (gain1_hbm, v.gain1), (shift1_hbm, v.shift1),
        (w2_hbm, v.w2_raw), (gain2_hbm, v.gain2), (shift2_hbm, v.shift2),
        (gain3_hbm, v.gain3), (shift3_hbm, v.shift3), (head_w_hbm, v.head_w),
        (head_b_hbm, v.head_b), (noisy_hbm, v.noisy), (later_hbm, v.later),
        (patch_b_hbm, v.patch_b),
    )
    loads = [
        pltpu.make_async_copy(src, dst, v.load_sem.at[k]) for k, (src, dst) in enumerate(early)
    ]
    strips = v.pw_raw.shape[0]
    loads += [
        pltpu.make_async_copy(
            pw_hbm.at[:, n * LANES : (n + 1) * LANES], v.pw_raw.at[n], v.load_sem.at[len(early)]
        )
        for n in range(strips)
    ]
    for load in loads:
        load.start()

    def padded(values, width=LANES):
        rows = values.shape[0]
        if width == values.shape[1]:
            return values
        return jnp.concatenate([values, jnp.zeros((rows, width - values.shape[1]), values.dtype)], axis=1)

    def pack(dst, value, main):
        rows = value.shape[0]
        dst[...] = value[0:main]
        rest = rows - main
        free = LANES - CB
        for j in range(CB // free if rest else 0):
            dst[j * rest : (j + 1) * rest, CB:LANES] = value[main:rows, j * free : (j + 1) * free]

    def unpack(value, rows):
        main = value.shape[0]
        rest = rows - main
        if not rest:
            return (value,)
        free = LANES - CB
        columns = [value[j * rest : (j + 1) * rest, CB:LANES] for j in range(CB // free)]
        return value, padded(jnp.concatenate(columns, axis=1))

    def channel_stats(values):
        total = jnp.sum(values, axis=0, keepdims=True)
        middle = total * (1.0 / values.shape[0])
        away = values - middle
        return total, jnp.sum(away * away, axis=0, keepdims=True)

    loads[0].wait()
    for r in range(R):
        line = v.feat[r]
        for q in range(S):
            v.tile[q, r * W : (r + 1) * W, :] = padded(line[:, q * CB : (q + 1) * CB])
    own_rows = pl.ds(pl.multiple_of(p * TILE, 8), TILE)
    for q in range(S):
        value = v.tile[q]
        v.feat_all[q, own_rows, :] = value
        pack(v.a_pack.at[q], value, AM)
        total, spread = channel_stats(value)
        v.st[q : q + 1, :] = total
        v.st[S + q : S + q + 1, :] = spread
        edge = jnp.where(
            t == 0, v.tile[q, pl.ds(W - 1, R, stride=W), :], v.tile[q, pl.ds(0, R, stride=W), :]
        )
        v.colf[q, 0:R, :] = edge
        v.rowf[q, 0:W, :] = jnp.where(hh == 0, value[TILE - W : TILE], value[0:W])
        v.corf[q : q + 1, :] = jnp.where(hh == 0, edge[R - 1 : R], edge[0:1])
    v.st_in[t, s] = v.st[...]

    @pl.when(stray)
    def _():
        v.colf_in[p] = v.colf[...]

    def w_pack(k, raw):
        @pl.when(home)
        def _():
            for cc in range(C):
                rows = pl.ds(pl.multiple_of(QR * (2 * g + cc), 8), QR)
                for pp in range(2):
                    pieces = [raw[tap, rows, :][:, pp * CB : (pp + 1) * CB] for tap in range(9)]
                    pack(v.wpack.at[k, pp, cc], padded(jnp.concatenate(pieces, axis=0)), WM)

    loads[1].wait()
    w_pack(0, v.w1_raw)

    def w_own(k, raw):
        @pl.when(home)
        def _():
            for tap in range(9):
                w = raw[tap]
                v.wown[k, tap * CB : (tap + 1) * CB, :] = padded(
                    jnp.where(p == 0, w[:, 0:CB], w[:, CB : 2 * CB])
                )


    row_id = lax.broadcasted_iota(jnp.int32, (LANES, LANES), 0)
    col_id = lax.broadcasted_iota(jnp.int32, (LANES, LANES), 1)
    same = ((row_id // per_group) == (col_id // per_group)) & (row_id < CB) & (col_id < CB)
    member = jnp.where(same, 1.0, 0.0).astype(F32)

    def group_sum(rows8):
        return jnp.dot(rows8, member, precision=HIGHEST, preferred_element_type=F32)

    def store_mat(k, q, tap, w):
        high, low = split_pair(w)
        v.mat[k, q, tap * LANES : tap * LANES + CB, 0:LANES] = high
        v.mat[k, q, tap * LANES : tap * LANES + CB, LANES : 2 * LANES] = low

    def own_copy(k):
        return remote(v.wown.at[k], v.wown.at[k], v.es.at[0], v.er.at[k], chan=oc)

    def own_mat(k):
        pl.when(stray)(own_copy(k).wait_recv)
        for tap in range(9):
            store_mat(k, s, tap, v.wown[k, tap * CB : (tap + 1) * CB, :])

    gap = jnp.zeros((LANES - CB, 2 * LANES), BF16)
    for k in range(2):
        for q in range(S):
            for tap in range(9):
                v.mat[k, q, tap * LANES + CB : (tap + 1) * LANES, :] = gap

    WH = up(WM // 2, 8)
    pieces_of = (pl.ds(0, WH), pl.ds(WH, WM - WH))
    order = (far, far2, pair)

    def z_copy(k, n, peer, slot, cc, h):
        return remote(
            v.wpack.at[k, lax.rem(peer, 2), cc, pieces_of[h]],
            v.wq.at[k, slot, 2 * g + cc, pieces_of[h]],
            v.zs.at[0], v.zr.at[k, n, h], space=peer, chan=cc,
        )

    def y_copy(k, n, z, which, h):
        ref = v.wq.at[k, z, which, pieces_of[h]]
        return remote(ref, ref, v.ys.at[0], v.yr.at[k, n, h], groups=gy)

    def b_copy(k, n, z, which, h):
        ref = v.wq.at[k, z, which, pieces_of[h]]
        return remote(ref, ref, v.bs.at[0], v.br.at[k, n], chan=oc)

    def z_send(k, n):
        for h in range(2):
            for cc in range(C):
                go_if(home, z_copy(k, n, order[n], s, cc, h))

    def relay(k, n):
        z = order[n]
        for h in range(2):
            remote(
                v.wpack.at[k, 0, 0, pieces_of[h]], v.wq.at[k, z, 2 * g + c, pieces_of[h]],
                v.zs.at[0], v.zr.at[k, n, h], space=z, chan=t,
            ).wait_recv()
            y_copy(k, n, z, 2 * g + c, h).start()
            b_copy(k, n, z, 2 * g + c, h).start()

    def relay2(k, n, z):
        for h in range(2):
            y_copy(k, n, z, 2 * gy + c, h).wait_recv()
            b_copy(k, n, z, 2 * gy + c, h).start()

    def nth_weights(i):
        flip = lax.rem(lax.div(i + 1, 2), 2)
        return 2 * lax.rem(hh + flip, 2) + lax.rem(p + lax.div(i, 2), 2)

    def nth_block(j):
        return 2 * lax.rem(t + lax.rem(j, 2), 2) + lax.rem(p + lax.div(j, 2), 2)

    def finish_weights(k, n, z):
        await_bytes(rows_of(2 * WM), v.br.at[k, n])
        for kk in range(4):
            at = 0
            for value in unpack(v.wq[k, z, kk], WQ):
                for n in range(value.shape[0] // 8):
                    tap, off = divmod(at, QR)
                    to = tap * CB + kk * QR + off
                    v.wf[to : to + 8, :] = value[n * 8 : n * 8 + 8]
                    at += 8
        for tap in range(9):
            store_mat(k, z, tap, v.wf[tap * CB : (tap + 1) * CB, :])

    pl.semaphore_wait(barrier, S * T * C)

    feat_copy = remote(v.a_pack, v.a_in.at[p], v.as_sem.at[0], v.ar_sem.at[0], tm=tx)

    def feat_part(m):
        blocks = pl.ds(2 * m, 2)
        return remote(
            v.a_pack.at[blocks], v.a_in.at[p, blocks], v.fs.at[0], v.fr.at[m], space=pair
        )

    def st_copy(dt, peer, mt, ms):
        return remote(
            v.st, v.st_in.at[mt, ms], v.ss_sem.at[0], v.sr_sem.at[0],
            space=peer, tm=tx if dt else t,
        )

    def col_copy(n, slot, **where):
        return remote(v.colf, v.colf_in.at[slot], v.cs_sem.at[0], v.cr_sem.at[slot], **where)

    hub = inner & home
    row_copy = remote(v.rowf, v.rowf_in, v.rs_sem.at[0], v.rr_sem.at[0], space=far2)

    def row_forward(n, **where):
        return remote(v.rowf_in, v.rowf_in, v.rs_sem.at[1], v.rr_sem.at[1], **where)

    def cor_copy(n, **where):
        return remote(v.corf, v.corf_in, v.os_sem.at[0], v.or_sem.at[0], **where)

    st_peers = [(0, far), (0, far2), (1, far), (1, far2), (0, pair), (1, pair), (1, s)]
    go_if(hub, row_copy)
    for dt, peer in st_peers:
        go(st_copy(dt, peer, t, s))
    for n, (peer, column) in enumerate(((far, t), (far2, t), (far, tx), (far2, tx))):
        go_if(inner & stray, cor_copy(n, space=peer, tm=column))
    go_if(stray, col_copy(0, p, tm=tx))
    go_if(stray, col_copy(1, p, space=pair))
    go_if(stray, col_copy(2, p, space=pair, tm=tx))
    go_if(home, feat_part(0))
    go_if(home, feat_part(1))
    go_if(home, feat_copy)
    z_send(0, 0)
    z_send(0, 1)
    w_own(0, v.w1_raw)
    go_if(home, own_copy(0))
    bias_copy = remote(v.bias_out, v.bias_in, v.is_sem.at[0], v.ir_sem.at[0], chan=oc)

    for load in loads[2 : len(early)]:
        load.wait()
    await_bytes(v.pw_raw, v.load_sem.at[len(early)])
    for n, (gain, shift) in enumerate(
        ((v.gain1, v.shift1), (v.gain2, v.shift2), (v.gain3, v.shift3))
    ):
        for j, ref in enumerate((gain, shift)):
            row = ref[...].reshape(1, CH)
            for q in range(S):
                v.prm[n, q, j : j + 1, :] = padded(row[:, q * CB : (q + 1) * CB])
    bias_row = jnp.broadcast_to(v.head_b[...].reshape(1, ZH), (ZH, ZH))
    diagonal = lax.broadcasted_iota(jnp.int32, (ZH, ZH), 0) == lax.broadcasted_iota(
        jnp.int32, (ZH, ZH), 1
    )
    my_bias = jnp.sum(jnp.where(diagonal, bias_row, 0.0), axis=1, keepdims=True)
    v.bias_out[...] = jnp.broadcast_to(my_bias, (ZH, LANES))
    go(bias_copy)
    for tap in range(9):
        v.hw_send[tap] = padded(v.head_w[tap])

    @pl.when(hub)
    def _():
        row_copy.wait_recv()

    for n, where in enumerate((dict(space=pair), dict(tm=tx), dict(space=pair, tm=tx))):
        go_if(hub, row_forward(n, **where))
    z_send(0, 2)
    own_mat(0)
    w_pack(1, v.w2_raw)
    w_own(1, v.w2_raw)
    go_if(home, own_copy(1))
    def feat_pass(m):
        ref = v.a_in.at[1 - p, pl.ds(2 * m, 2)]
        return remote(ref, ref, v.gs.at[0], v.fr.at[m], tm=tx)

    def pass_features(when):
        @pl.when(home & when)
        def _():
            for m in range(2):
                feat_part(m).wait_recv()
                feat_pass(m).start()

    pass_features(inner)
    relay(0, 0)
    pass_features(jnp.logical_not(inner))
    for n in (0, 2, 1):
        z_send(1, n)
    relay(0, 1)

    def hw_copy(n, slot, **where):
        return remote(v.hw_send, v.hwq.at[slot], v.hs.at[0], v.hr.at[slot], **where)

    @pl.when(hh == t)
    def _():
        v.hwq[c] = v.hw_send[...]

    def unpack_features(slot):
        for q in range(S):
            at = 0
            for value in unpack(v.a_in[slot, q], TILE):
                rows = pl.ds(pl.multiple_of(slot * TILE + at, 8), value.shape[0])
                v.feat_all[q, rows, :] = value
                at += value.shape[0]

    @pl.when(stray)
    def _():
        feat_copy.wait_recv()
        unpack_features(p)

    @pl.when(stray)
    def _():
        for m in range(2):
            feat_pass(m).wait_recv()

    unpack_features(1 - p)
    await_bytes(rows_of(8 * len(st_peers)), v.sr_sem.at[0])
    col_copy(1, 1 - p, space=pair).wait_recv()
    pl.when(home)(col_copy(0, p, tm=tx).wait_recv)
    cor_copy(0, space=far).wait_recv()
    pl.when(jnp.logical_not(hub))(row_forward(0, space=pair).wait_recv)

    scale = 1.0 / float(per_group * TILE * S * T)
    everyone = [v.st_in[tt, ss] for tt in range(T) for ss in range(S)]
    total8 = everyone[0]
    for part in everyone[1:]:
        total8 = total8 + part
    summed = group_sum(total8)
    center8 = summed * scale
    gathered = jnp.zeros((8, LANES), F32)
    for part in everyone:
        away = part * (1.0 / TILE) - center8
        gathered = gathered + away * away * float(TILE)
    inverse4 = lax.rsqrt((group_sum(gathered)[0:S] + summed[S : 2 * S]) * scale + EPSILON)

    def build_taps(n, q, value, columns, corner, row, center, inverse):
        gain, shift = v.prm[n, q, 0:1, :], v.prm[n, q, 1:2, :]

        def act(values):
            u = (values - center) * inverse * gain + shift
            return u / (1.0 + jnp.exp(-u))

        inside = act(value)
        line = act(row)
        top, bottom = jnp.where(hh == 1, line, 0.0), jnp.where(hh == 0, line, 0.0)
        tail = jnp.zeros((8, LANES), F32)
        for b in range(3):
            at = AT + 1 - b
            v.taps[q, b, AT + (LAST + 1) * W : AT + (LAST + 1) * W + 8, :] = tail
            v.taps[q, b, at : at + W, :] = top
            v.taps[q, b, at + W : at + W + REG, :] = inside
            v.taps[q, b, at + W + REG : at + 2 * W + REG, :] = bottom
        tip = act(corner)
        sides = [(0, 1, jnp.where(hh == 1, tip, 0.0)), (LAST, 1, jnp.where(hh == 0, tip, 0.0))]
        sides += [(1 + first, count, act(raw)) for first, count, raw in columns]
        for first, count, piece in sides:
            at = AT + first * W
            from_left = jnp.where(c == 1, piece, 0.0)
            from_right = jnp.where(c == 0, piece, 0.0)
            if count == 1:
                v.taps[q, 0, at : at + 1, :] = from_left
                v.taps[q, 2, at + W - 1 : at + W, :] = from_right
            else:
                v.taps[q, 0, pl.ds(at, count, stride=W), :] = from_left
                v.taps[q, 2, pl.ds(at + W - 1, count, stride=W), :] = from_right

    for q in range(S):
        v.nrm[q, 0:1, :] = center8[q : q + 1]
        v.nrm[q, 1:2, :] = inverse4[q : q + 1]
        v.nrm[q, 2:3, :] = v.corf_in[q : q + 1, :]

    def first_taps(q, carry):
        build_taps(
            0, q, v.feat_all[q],
            [(0, R, v.colf_in[0, q, 0:R, :]), (R, R, v.colf_in[1, q, 0:R, :])],
            v.nrm[q, 2:3, :], v.rowf_in[q, 0:W, :], v.nrm[q, 0:1, :], v.nrm[q, 1:2, :],
        )
        return carry

    def operand(q):
        highs, lows = [], []
        for a in range(3):
            for b in range(3):
                high, low = split_pair(v.taps[q, b, AT + a * W : AT + a * W + REG, :])
                highs.append(high)
                lows.append(low)
        return jnp.concatenate(
            [jnp.concatenate(highs, axis=1), jnp.concatenate(lows, axis=1)], axis=0
        )

    def conv_block(k, q):
        part = jnp.dot(operand(q), v.mat[k, q], preferred_element_type=F32)
        return part[0:REG, 0:LANES] + part[0:REG, LANES:] + part[REG:, 0:LANES]

    lax.fori_loop(0, S, first_taps, 0)
    relay2(0, 0, far)
    relay(0, 2)
    v.acc[...] = jnp.zeros(v.acc.shape, F32)

    def first_step(i, carry):
        z = nth_weights(i)

        @pl.when(i > 0)
        def _():
            finish_weights(0, i - 1, z)

        v.acc[...] += conv_block(0, z)

        @pl.when(i < 2)
        def _():
            relay2(0, i + 1, nth_weights(i + 2))

        @pl.when(i == 1)
        def _():
            relay(1, 0)

        return carry

    lax.fori_loop(0, 4, first_step, 0)
    first = v.acc[...]
    v.conv_raw[own] = first

    def rim_exchange(k, full):
        value = full[...]
        total, spread = channel_stats(value)
        column = jnp.where(
            c == 0, full[pl.ds(W - 1, 2 * R, stride=W), :], full[pl.ds(0, 2 * R, stride=W), :]
        )
        row = jnp.where(hh == 0, value[REG - W : REG], value[0:W])
        corner = jnp.where(hh == 0, column[2 * R - 1 : 2 * R], column[0:1])
        for ref, first, rows in ((v.rowm, W, row), (v.colm, 2 * R, column), (v.corm, 1, corner)):
            ref[k, 0:first, :] = rows
            ref[k, first : first + 1, :] = total
            ref[k, first + 1 : first + 2, :] = spread
        copies = [
            remote(v.corm.at[k], v.corm_in.at[k], v.ks.at[0], v.kr.at[k], space=far, chan=oc),
            remote(v.rowm.at[k], v.rowm_in.at[k], v.ks.at[0], v.kr.at[k], space=far),
            remote(v.colm.at[k], v.colm_in.at[k], v.ks.at[0], v.kr.at[k], chan=oc),
        ]
        for copy in copies:
            go(copy)
        return total, spread

    def rim_finish(k, total, spread):
        await_bytes(rows_of(MR + up(W + 2, 8) + 8), v.kr.at[k])
        parts = [(total, spread)]
        for ref, first in ((v.rowm_in, W), (v.colm_in, 2 * R), (v.corm_in, 1)):
            parts.append((ref[k, first : first + 1, :], ref[k, first + 1 : first + 2, :]))
        whole = parts[0][0] + parts[1][0] + parts[2][0] + parts[3][0]
        wide = lambda row: jnp.broadcast_to(row, (8, LANES))
        center = group_sum(wide(whole))[0:1] * scale
        spreads = jnp.zeros((1, LANES), F32)
        for part_total, part_spread in parts:
            away = part_total * (1.0 / REG) - center
            spreads = spreads + part_spread + away * away * float(REG)
        inverse = lax.rsqrt(group_sum(wide(spreads))[0:1] * scale + EPSILON)
        return center, inverse

    rims1 = rim_exchange(0, v.conv_raw.at[own])
    pack(v.ypack, first, PM)
    near_copy = remote(v.ypack, v.yin.at[0], v.vs.at[0], v.vr.at[0], space=pair)
    go(near_copy)
    side_copy = remote(v.ypack, v.yin.at[2], v.vs.at[0], v.vr.at[1], tm=tx)
    go(side_copy)
    PH = up(PM // 2, 8)
    upper, lower = pl.ds(0, PH), pl.ds(PH, PM - PH)
    cross_x = remote(
        v.yin.at[0, upper], v.yin.at[1, upper], v.vs.at[0], v.vr.at[2], tm=tx
    )
    cross_z = remote(
        v.yin.at[2, lower], v.yin.at[1, lower], v.vs.at[0], v.vr.at[2], space=pair
    )
    own_mat(1)
    relay(1, 2)
    relay(1, 1)
    relay2(1, 0, far)
    center, inverse = rim_finish(0, *rims1)
    v.rl_in[own, 0 : 2 * R, :] = v.colm_in[0, 0 : 2 * R, :]
    v.rl_in[own, 2 * R : 2 * R + 1, :] = v.corm_in[0, 0:1, :]
    v.rl_in[own, 2 * R + 1 : 2 * R + 2, :] = center
    v.rl_in[own, 2 * R + 2 : 2 * R + 3, :] = inverse
    v.rl_in[own, MR : MR + W, :] = v.rowm_in[0, 0:W, :]

    def rl_copy(n, q, **where):
        ref = v.rl_in.at[q]
        return remote(ref, ref, v.ls.at[0], v.lr.at[q], **where)

    go(rl_copy(0, own, space=pair))
    go(rl_copy(1, own, space=pair, tm=tx))
    go(rl_copy(2, own, tm=tx))
    go_if(hh == t, hw_copy(0, c, chan=oc))
    go_if(hh == t, hw_copy(1, c, space=far))

    def second_taps(q):
        build_taps(
            1, q, v.conv_raw[q], [(0, 2 * R, v.rl_in[q, 0 : 2 * R, :])],
            v.rl_in[q, 2 * R : 2 * R + 1, :], v.rl_in[q, MR : MR + W, :],
            v.rl_in[q, 2 * R + 1 : 2 * R + 2, :], v.rl_in[q, 2 * R + 2 : 2 * R + 3, :],
        )

    def second_step(j, carry):
        q = nth_block(j)

        @pl.when(j == 1)
        def _():
            relay2(1, 1, far2)

        @pl.when(j == 2)
        def _():
            finish_weights(1, 2 - lax.rem(t + hh, 2), near)

        @pl.when(j == 3)
        def _():
            finish_weights(1, 1 + lax.rem(t + hh, 2), cross)

        @pl.when((j == 1) & (t == hh))
        def _():
            finish_weights(1, 0, far)

        @pl.when(j == 1)
        def _():
            rl_copy(2, side, tm=tx).wait_recv()

        @pl.when(j == 2)
        def _():
            rl_copy(0, near, space=pair).wait_recv()

        @pl.when(j == 3)
        def _():
            await_bytes(rows_of(PM), v.vr.at[2])
            rl_copy(1, cross, space=pair, tm=tx).wait_recv()

        @pl.when((j == 3) & (hh != t))
        def _():
            hw_copy(1, c, space=far).wait_recv()
            remote(v.hwq.at[c], v.hwq.at[c], v.hs.at[0], v.hr.at[c], chan=oc).start()

        @pl.when(j > 0)
        def _():
            at = 0
            for value in unpack(v.yin[lax.rem(j + 1, 3)], REG):
                v.conv_raw[q, at : at + value.shape[0], :] = value
                at += value.shape[0]

        second_taps(q)

        @pl.when((j == 0) & (t != hh))
        def _():
            finish_weights(1, 0, far)

        v.acc[...] += conv_block(1, q)

        @pl.when(j == 0)
        def _():
            relay2(1, 2, pair)
            side_copy.wait_recv()
            cross_z.start()
            near_copy.wait_recv()
            cross_x.start()

        return carry

    v.acc[...] = v.feat_all[own]
    lax.fori_loop(0, S, second_step, 0)
    v.hid[...] = v.acc[...]
    rims2 = rim_exchange(1, v.hid)

    hw_copy(0, oc, chan=oc).wait_recv()
    bias_copy.wait_recv()
    blank = jnp.zeros((LANES - 3 * Z, LANES), F32)
    for b in range(3):
        rows = [v.hwq[cc, a * 3 + b] for a in range(3) for cc in range(C)] + [blank]
        high, low = split_pair(jnp.concatenate(rows, axis=0))
        for place, value in ((3 * b, high), (3 * b + 1, high), (3 * b + 2, low)):
            v.wh_mat[:, place * LANES : (place + 1) * LANES] = value
    ours, other_bias = v.bias_out[...], v.bias_in[...]
    bias = jnp.where(
        own == 0,
        jnp.concatenate(
            [jnp.where(c == cc, ours, other_bias) for cc in range(C)], axis=0
        ),
        0.0,
    )

    for first, mat in ((0, v.wn_mat), (4 * (Z + 4), wc_out)):
        for b in range(2):
            for a in range(2):
                at = (b * 2 + a) * Z
                for n in range(strips):
                    high, low = split_pair(v.pw_raw[n, pl.ds(first + a * 2 + b, Z, stride=4), :])
                    lanes = slice(n * LANES, (n + 1) * LANES)
                    mat[at : at + Z, lanes] = high
                    mat[4 * Z + at : 4 * Z + at + Z, lanes] = high
                    mat[8 * Z + at : 8 * Z + at + Z, lanes] = low
    mark_sum = jnp.concatenate(
        [
            jnp.sum(v.pw_raw[n, 4 * Z : 4 * (Z + 4), :], axis=0, keepdims=True)
            for n in range(strips)
        ],
        axis=1,
    )

    PR, PC, PP = dims["PR"], dims["PC"], dims["PP"]
    FULLW = W * T
    cells, turned, patch = v.cells, v.turned, v.patch
    cells[...] = jnp.zeros(cells.shape, F32)
    patch[...] = jnp.zeros(patch.shape, F32)

    def build_patches():
        turned[...] = cells[...].T
        for b in range(2):
            picked = turned[pl.ds(b, PC, stride=2), :]
            for i in range(PR):
                patch[i * PP : i * PP + PC, b * 2 * Z : (b + 1) * 2 * Z] = picked[
                    :, i * 2 * Z : (i + 1) * 2 * Z
                ]

    for f in range(FR):
        for i in range(R):
            cells[i * Z : (i + 1) * Z, 0:FULLW] = v.noisy[f, i]
        build_patches()
        got = jnp.dot(split_columns(patch[:, 0 : 4 * Z]), v.wn_mat[...], preferred_element_type=F32)
        opening = (t * FR + f) == 0
        base_out[f] = got + v.patch_b[...].reshape(1, -1) + jnp.where(opening, mark_sum, 0.0)

    center, inverse = rim_finish(1, *rims2)
    build_taps(
        2, own, v.hid[...], [(0, 2 * R, v.colm_in[1, 0 : 2 * R, :])], v.corm_in[1, 0:1, :],
        v.rowm_in[1, 0:W, :], center, inverse,
    )

    columns = []
    for b in range(3):
        high, low = split_pair(v.taps[own, b, AT : AT + v.mixed.shape[0], :])
        columns += [high, low, high]
    v.mixed[...] = lax.dot_general(
        jnp.concatenate(columns, axis=1),
        v.wh_mat[...],
        (((1,), (1,)), ((), ())),
        preferred_element_type=F32,
    )
    for j in range(2):
        shifted = [v.mixed[j * TILE + a * W : j * TILE + a * W + LANES, :] for a in range(3)]
        joined = jnp.where(
            col_id < Z, shifted[0], jnp.where(col_id < 2 * Z, shifted[1], shifted[2])
        ).T
        v.lat_send[j] = joined[0:Z] + joined[Z : 2 * Z] + joined[2 * Z : 3 * Z] + bias
    v.lat_in[c, own] = v.lat_send[p]

    def lat_copy(dp, dt, dc, slot_c, slot_q):
        return remote(
            v.lat_send.at[1 - p if dp else p], v.lat_in.at[slot_c, slot_q],
            v.ts.at[0], v.tr.at[0],
            space=pair if dp else s, tm=tx if dt else t, chan=oc if dc else c,
        )

    hops = [(1, 1, 1), (1, 1, 0), (0, 1, 1), (0, 1, 0), (1, 0, 1), (1, 0, 0), (0, 0, 1)]
    for dp, dt, dc in hops:
        go_if(((tx if dt else t) == 0) | (c == 1), lat_copy(dp, dt, dc, c, own))

    pl.when(t == 0)(functools.partial(await_bytes, rows_of(7 * Z), v.tr.at[0]))
    pl.when((t == 1) & (c == 1))(functools.partial(await_bytes, rows_of(3 * Z), v.tr.at[0]))
    pl.when((t == 1) & (c == 0))(functools.partial(await_bytes, rows_of(4 * Z), v.tr.at[0]))

    def latent_of(tt):
        return v.lat_in[tt, 0] + v.lat_in[tt, 1] + v.lat_in[tt, 2] + v.lat_in[tt, 3]

    value = latent_of(t)
    for r in range(R):
        latent[r] = value[:, r * W : (r + 1) * W]
    for f in range(FR):
        cells[...] = jnp.zeros(cells.shape, F32)
        opening = (t * FR + f) == 0
        for tt in range(T):
            value = latent_of(tt)
            for i in range(R):
                cells[i * Z : (i + 1) * Z, tt * W : (tt + 1) * W] = value[:, i * W : (i + 1) * W]
        for i in range(R):
            rows = slice(i * Z, (i + 1) * Z)
            cells[rows, 0:FULLW] = jnp.where(opening, cells[rows, 0:FULLW], v.later[f, i])
        build_patches()
        patch_out[f] = patch[...]
    RR = up(W + 2, 8)
    drains = (
        (home, rows_of(S * AM), v.as_sem), (home, rows_of(S * AM), v.fs),
        (home, rows_of(S * AM), v.gs), (None, rows_of(8 * len(st_peers)), v.ss_sem),
        (stray, rows_of(3 * S * 8), v.cs_sem), (hub, rows_of(S * RR), v.rs_sem),
        (inner & stray, rows_of(4 * 8), v.os_sem), (None, rows_of(ZH), v.is_sem),
        (home, v.wq.at[0, pl.ds(0, 3)], v.zs), (None, v.wq.at[0, pl.ds(0, 3), pl.ds(0, 2)], v.ys),
        (None, v.wq.at[0, pl.ds(0, 3)], v.bs), (home, v.wown, v.es),
        (None, rows_of(2 * (MR + RR + 8)), v.ks), (None, v.yin, v.vs),
        (None, rows_of(3 * (MR + RR)), v.ls), (hh == t, rows_of(2 * 9 * ZH), v.hs),
        (hh != t, rows_of(9 * ZH), v.hs),
        (c == 1, rows_of(7 * Z), v.ts), ((c == 0) & (t == 0), rows_of(3 * Z), v.ts),
        ((c == 0) & (t == 1), rows_of(4 * Z), v.ts),
    )
    for condition, ref, sem in drains:
        wait = functools.partial(await_bytes, ref, sem.at[0])
        wait() if condition is None else pl.when(condition)(wait)
    pl.when(hub)(functools.partial(await_bytes, rows_of(3 * S * RR), v.rs_sem.at[1]))


def up(value, unit):
    return -(-value // unit) * unit


def packed_rows(rows, width, unit):
    free = LANES - width
    if free <= 0 or width % free or rows % 8:
        return rows
    main = up(-(-rows * width // LANES), unit)
    fits = main < rows and (rows - main) * (width // free) <= main
    return main if fits else rows


def plan(mesh_shape, features, noisy_latents, patch_weight, head_weight):
    S, T, C, G = (mesh_shape[axis] for axis in ("space", "tm", "chan", "groups"))
    R, W, CH = features.shape
    FR, Z = noisy_latents.shape[:2]
    dims = dict(S=S, T=T, C=C, R=R, W=W, CH=CH, Z=Z, FR=FR)
    dims["PR"], dims["PC"] = R // 2, W * T // 2
    dims["PP"] = up(W * T // 2, 8)
    dims["N"] = patch_weight.shape[1]
    CB = CH // S
    TILE = R * W
    dims["AM"] = packed_rows(TILE, CB, 16)
    dims["PM"] = packed_rows(2 * TILE, CB, 8)
    dims["WQ"] = 9 * (CB // 4)
    dims["WM"] = packed_rows(dims["WQ"], CB, 8)
    fits = (
        (S, T, C, G) == (4, 2, 2, 2)
        and CH % S == 0
        and CB <= LANES
        and CB % (4 * 8) == 0
        and CB % (CH // NGROUP) == 0
        and TILE % 8 == 0
        and TILE <= LANES
        and R % 2 == 0
        and R <= 8
        and all(dims[name] % 8 == 0 for name in ("AM", "PM", "WQ", "WM"))
        and dims["WM"] > 8
        and 2 * R + 2 <= up(2 * R + 2, 8)
        and head_weight.shape[3] * C == Z
        and Z % 16 == 0
        and 3 * Z <= LANES
        and R * Z <= LANES
        and W * T <= LANES
        and W * T % 2 == 0
        and 4 * Z <= LANES
        and dims["N"] % LANES == 0
    )
    return dims if fits else None


def fused(dims, args):
    S, T, C = dims["S"], dims["T"], dims["C"]
    R, W, CH = dims["R"], dims["W"], dims["CH"]
    Z, FR, N = dims["Z"], dims["FR"], dims["N"]
    CB, NH = CH // S, CH // C
    TILE, REG = R * W, 2 * R * W
    (f, g1, s1, w1, g2, s2, w2, g3, s3, hw, hb, noisy, later, pw, pb) = args
    flat = lambda v: v.reshape((9,) + v.shape[2:])
    by_row = lambda v: jnp.transpose(v, (0, 2, 1, 3))
    operands = (
        f, g1, s1, flat(w1), g2, s2, flat(w2), g3, s3,
        flat(jnp.transpose(hw, (0, 1, 3, 2))), hb, by_row(noisy), by_row(later), pw, pb,
    )
    vmem = pl.BlockSpec(memory_space=pltpu.VMEM)
    far = pl.BlockSpec(memory_space=pl.ANY)
    dma = lambda *shape: pltpu.SemaphoreType.DMA(shape)
    buf = lambda *shape: pltpu.VMEM(shape, F32)
    half = lambda *shape: pltpu.VMEM(shape, BF16)
    PR, PC, PP = dims["PR"], dims["PC"], dims["PP"]
    MR, RR = up(2 * R + 2, 8), up(W + 2, 8)
    TR = up(8 + 2 * W + TILE + LANES, 8)
    scratch = {
        name: pltpu.VMEM(operands[k].shape, F32)
        for name, k in (
            ("feat", 0), ("gain1", 1), ("shift1", 2), ("w1_raw", 3), ("gain2", 4), ("shift2", 5),
            ("w2_raw", 6), ("gain3", 7), ("shift3", 8), ("head_w", 9), ("head_b", 10),
            ("noisy", 11), ("later", 12), ("patch_b", 14),
        )
    }
    scratch |= {
        "pw_raw": buf(N // LANES, pw.shape[0], LANES),
        "prm": buf(3, S, 8, LANES),
        "tile": buf(S, TILE, LANES),
        "feat_all": buf(S, REG, LANES),
        "a_pack": buf(S, dims["AM"], LANES),
        "a_in": buf(2, S, dims["AM"], LANES),
        "st": buf(8, LANES),
        "st_in": buf(T, S, 8, LANES),
        "colf": buf(S, 8, LANES),
        "colf_in": buf(2, S, 8, LANES),
        "rowf": buf(S, RR, LANES),
        "rowf_in": buf(S, RR, LANES),
        "corf": buf(8, LANES),
        "corf_in": buf(8, LANES),
        "wpack": buf(2, 2, C, dims["WM"], LANES),
        "wown": buf(2, 9 * CB, LANES),
        "bias_out": buf(Z // C, LANES),
        "bias_in": buf(Z // C, LANES),
        "wq": buf(2, S, 4, dims["WM"], LANES),
        "wf": buf(9 * CB, LANES),
        "mat": half(2, S, 9 * LANES, 2 * LANES),
        "taps": buf(S, 3, TR, LANES),
        "nrm": buf(S, 8, LANES),
        "acc": buf(REG, LANES),
        "conv_raw": buf(S, REG, LANES),
        "ypack": buf(dims["PM"], LANES),
        "yin": buf(3, dims["PM"], LANES),
        "hid": buf(REG, LANES),
        "colm": buf(2, MR, LANES),
        "colm_in": buf(2, MR, LANES),
        "rowm": buf(2, RR, LANES),
        "rowm_in": buf(2, RR, LANES),
        "corm": buf(2, 8, LANES),
        "corm_in": buf(2, 8, LANES),
        "rl_in": buf(S, MR + RR, LANES),
        "hw_send": buf(9, Z // C, LANES),
        "hwq": buf(C, 9, Z // C, LANES),
        "wh_mat": half(LANES, 9 * LANES),
        "wn_mat": half(12 * Z, N),
        "mixed": buf(TR - 8, LANES),
        "lat_send": buf(2, Z, LANES),
        "lat_in": buf(C, S, Z, LANES),
        "cells": buf(LANES, LANES),
        "turned": buf(LANES, LANES),
        "patch": buf(PR * PP, LANES),
        "load_sem": dma(15),
        "as_sem": dma(1), "ar_sem": dma(1), "fs": dma(1), "fr": dma(2), "gs": dma(1),
        "ss_sem": dma(1), "sr_sem": dma(1),
        "cs_sem": dma(1), "cr_sem": dma(2),
        "rs_sem": dma(2), "rr_sem": dma(2),
        "os_sem": dma(1), "or_sem": dma(1),
        "is_sem": dma(1), "ir_sem": dma(1),
        "zs": dma(1), "zr": dma(2, 3, 2),
        "ys": dma(1), "yr": dma(2, 3, 2),
        "bs": dma(1), "br": dma(2, 3),
        "es": dma(1), "er": dma(2),
        "ks": dma(1), "kr": dma(2),
        "vs": dma(1), "vr": dma(3),
        "ls": dma(1), "lr": dma(S),
        "hs": dma(1), "hr": dma(C),
        "ts": dma(1), "tr": dma(1),
    }
    patch, base, wc, latent = pl.pallas_call(
        functools.partial(fused_kernel, dims, tuple(scratch)),
        out_shape=(
            jax.ShapeDtypeStruct((FR, PR * PP, LANES), F32),
            jax.ShapeDtypeStruct((FR, PR * PP, N), F32),
            jax.ShapeDtypeStruct((12 * Z, N), BF16),
            jax.ShapeDtypeStruct((R, Z, W), F32),
        ),
        in_specs=[pl.BlockSpec(memory_space=pltpu.HBM)] * 15,
        out_specs=(vmem, vmem, vmem, vmem),
        scratch_shapes=list(scratch.values()),
        compiler_params=pltpu.CompilerParams(
            collective_id=0, has_side_effects=True, vmem_limit_bytes=32 * 2**20
        ),
        name="fused_block",
    )(*[pltpu.with_memory_space_constraint(v, pltpu.HBM) for v in operands])
    NB = 4 if N % (4 * LANES) == 0 else 1
    tokens, latent = pl.pallas_call(
        functools.partial(finish_kernel, dims, NB),
        out_shape=(
            jax.ShapeDtypeStruct((PR, PC, FR, N), F32),
            jax.ShapeDtypeStruct((R, Z, W), F32),
        ),
        in_specs=[vmem] * 4,
        out_specs=(pl.BlockSpec(memory_space=pltpu.HBM), pl.BlockSpec(memory_space=pltpu.HBM)),
        scratch_shapes=[buf(PR, PC, FR, N), dma(NB + 1)],
        compiler_params=pltpu.CompilerParams(vmem_limit_bytes=8 * 2**20),
        name="finish_tokens",
    )(patch, base, wc, latent)
    return jnp.transpose(tokens, (2, 0, 1, 3)), jnp.transpose(latent, (0, 2, 1))


def solution(mesh):
    shape = dict(mesh.shape)

    def step(*args):
        dims = plan(shape, args[0], args[11], args[13], args[9])
        return on_device(*args) if dims is None else fused(dims, args)

    return jax.shard_map(
        step,
        mesh=mesh,
        in_specs=(
            P(("groups", "space"), "tm", None),
            P(),
            P(),
            P(None, None, "space", "chan"),
            P(),
            P(),
            P(None, None, "space", "chan"),
            P(),
            P(),
            P(None, None, "space", "chan"),
            P("chan"),
            P(("groups", "tm"), None, "space", None),
            P(("groups", "tm"), None, "space", None),
            P(None, "chan"),
            P("chan"),
        ),
        out_specs=(P(("groups", "tm"), "space", None, "chan"), P(("groups", "space"), "tm", None)),
        check_vma=False,
    )
```

```python
import functools
import types

import jax
import jax.numpy as jnp
from jax import lax
from jax.experimental import pallas as pl
from jax.experimental.pallas import tpu as pltpu
from jax.sharding import PartitionSpec as P

NGROUP = 32


EPSILON = 1e-06
HIGHEST = lax.Precision.HIGHEST


def padded_2(cells, sides, width):
    for axis, dim in sides:
        count = lax.axis_size(axis)
        ends = count - 1
        head = lax.slice_in_dim(cells, 0, width, axis=dim)
        tail = lax.slice_in_dim(cells, cells.shape[dim] - width, cells.shape[dim], axis=dim)
        cells = jnp.concatenate(
            [
                lax.ppermute(tail, axis, [(i, (i + 1) % count) for i in range(ends)]),
                cells,
                lax.ppermute(head, axis, [((i + 1) % count, i) for i in range(ends)]),
            ],
            axis=dim,
        )
    return cells


def group_stats(inner, count_all):
    grouped = inner.reshape(-1, NGROUP, inner.shape[-1] // NGROUP)
    totals, squares = lax.psum(
        (jnp.sum(grouped, axis=(0, 2)), jnp.sum(grouped * grouped, axis=(0, 2))), ("space", "tm")
    )
    center = totals / count_all
    spread = squares / count_all - center * center
    return (center, lax.rsqrt(spread + EPSILON))


def normalize_act(values, stats, gain, shift):
    center, inverse = stats
    grouped = values.reshape(values.shape[:-1] + (NGROUP, values.shape[-1] // NGROUP))
    scaled = (grouped - center[:, None]) * inverse[:, None]
    return jax.nn.silu(scaled.reshape(values.shape) * gain + shift)


def tap_columns(padded, rows_out, cols_out):
    shifted = [
        padded[row_tap : row_tap + rows_out, col_tap : col_tap + cols_out, :]
        for row_tap in range(3)
        for col_tap in range(3)
    ]
    return jnp.stack(shifted, axis=2).reshape(rows_out * cols_out, 9, padded.shape[-1])


def add_taps(columns, piece):
    depth = piece.shape[2]
    picked = columns.reshape(columns.shape[0], 9 * depth)
    return jnp.dot(
        picked,
        piece.reshape(9 * depth, piece.shape[3]),
        precision=HIGHEST,
        preferred_element_type=jnp.float32,
    )


def wide_conv(padded, weight, rows_out, cols_out):
    columns = tap_columns(padded, rows_out, cols_out)
    summed = add_taps(columns, lax.all_gather(weight, "space", axis=2, tiled=True))
    return lax.all_gather(summed.reshape(rows_out, cols_out, -1), "chan", axis=2, tiled=True)


def border_rim(values):
    return padded_2(values, (("space", 0), ("tm", 1)), 1)


def on_device(
    features,
    norm1_gain,
    norm1_shift,
    conv1_weight,
    norm2_gain,
    norm2_shift,
    conv2_weight,
    head_gain,
    head_shift,
    head_weight,
    head_bias,
    noisy_latents,
    later_cond,
    patch_weight,
    patch_bias,
):
    tile_rows = features.shape[0]
    tile_cols = features.shape[1]
    count_all = float(
        tile_rows
        * tile_cols
        * lax.axis_size("space")
        * lax.axis_size("tm")
        * (features.shape[2] // NGROUP)
    )
    first_stats = group_stats(features, count_all)
    active = normalize_act(features, first_stats, norm1_gain, norm1_shift)
    first_conv = wide_conv(border_rim(active), conv1_weight, tile_rows, tile_cols)
    second_stats = group_stats(first_conv, count_all)
    second_act = normalize_act(first_conv, second_stats, norm2_gain, norm2_shift)
    second_conv = wide_conv(border_rim(second_act), conv2_weight, tile_rows, tile_cols)
    hidden = features + second_conv
    head_stats = group_stats(hidden, count_all)
    head_act = normalize_act(hidden, head_stats, head_gain, head_shift)
    head_pad = padded_2(head_act, (("space", 0), ("tm", 1)), 1)
    head_columns = tap_columns(head_pad, tile_rows, tile_cols)
    latent_part = (
        add_taps(head_columns, lax.all_gather(head_weight, "space", axis=2, tiled=True)) + head_bias
    )
    image_latent = lax.all_gather(
        latent_part.reshape(tile_rows, tile_cols, -1), "chan", axis=2, tiled=True
    )
    latent_row = lax.all_gather(image_latent, "tm", axis=1, tiled=True)
    frame_count = noisy_latents.shape[0]
    full_width = noisy_latents.shape[3]
    frame_ids = lax.axis_index("tm") * frame_count + jnp.arange(frame_count)
    opening = frame_ids == 0
    condition = jnp.where(
        opening[:, None, None, None], jnp.transpose(latent_row, (2, 0, 1))[None], later_cond
    )
    marks = jnp.broadcast_to(
        opening.astype(jnp.float32)[:, None, None, None], (frame_count, 4, tile_rows, full_width)
    )
    stacked = jnp.concatenate([noisy_latents, marks, condition], axis=1)
    channel_count = stacked.shape[1]
    patches = (
        stacked.reshape(frame_count, channel_count, tile_rows // 2, 2, full_width // 2, 2)
        .transpose(0, 2, 4, 1, 3, 5)
        .reshape(-1, channel_count * 4)
    )
    tokens = (
        jnp.dot(patches, patch_weight, precision=HIGHEST, preferred_element_type=jnp.float32)
        + patch_bias
    )
    return (tokens.reshape(frame_count, tile_rows // 2, full_width // 2, -1), image_latent)


MESH = pl.DeviceIdType.MESH
LANES = 128
BF16 = jnp.bfloat16
F32 = jnp.float32


def split_pair(values):
    high = values.astype(BF16)
    return high, (values - high.astype(F32)).astype(BF16)


def split_columns(values):
    high, low = split_pair(values)
    return jnp.concatenate([high, low, high], axis=1)


def finish_kernel(dims, parts, patch, base, wc, latent_in, tokens, latent, tok, sem):
    PC, PP, Z, FR = dims["PC"], dims["PP"], dims["Z"], dims["FR"]
    width = dims["N"] // parts
    copies = [pltpu.make_async_copy(latent_in, latent, sem.at[parts])]
    copies[0].start()
    lhs = [split_columns(patch[f, :, 0 : 4 * Z]) for f in range(FR)]
    for n in range(parts):
        lanes = slice(n * width, (n + 1) * width)
        for f in range(FR):
            got = base[f, :, lanes] + jnp.dot(lhs[f], wc[:, lanes], preferred_element_type=F32)
            for p in range(dims["PR"]):
                tok[p, :, f, lanes] = got[p * PP : p * PP + PC, :]
        view = (slice(None), slice(None), slice(None), pl.ds(n * width, width))
        copies.append(pltpu.make_async_copy(tok.at[view], tokens.at[view], sem.at[n]))
        copies[-1].start()
    for copy in copies:
        copy.wait()


def fused_kernel(dims, names, *refs):
    S, T, C = dims["S"], dims["T"], dims["C"]
    R, W, CH = dims["R"], dims["W"], dims["CH"]
    Z, FR = dims["Z"], dims["FR"]
    CB = CH // S
    TILE = R * W
    REG = 2 * TILE
    per_group = CH // NGROUP
    ZH = Z // C
    AM, PM, WQ, WM = dims["AM"], dims["PM"], dims["WQ"], dims["WM"]
    QR = CB // 4
    AT = 8
    LAST = 2 * R + 1
    MR = up(2 * R + 2, 8)
    (
        feat_hbm, gain1_hbm, shift1_hbm, w1_hbm, gain2_hbm, shift2_hbm, w2_hbm, gain3_hbm,
        shift3_hbm, head_w_hbm, head_b_hbm, noisy_hbm, later_hbm, pw_hbm, patch_b_hbm,
    ) = refs[:15]
    patch_out, base_out, wc_out, latent = refs[15:19]
    v = types.SimpleNamespace(**dict(zip(names, refs[19:])))
    s = lax.axis_index("space")
    t = lax.axis_index("tm")
    c = lax.axis_index("chan")
    g = lax.axis_index("groups")
    p, hh = lax.rem(s, 2), lax.div(s, 2)
    pair, far, far2 = s + 1 - 2 * p, lax.rem(s + 2, 4), 3 - s
    tx, oc, gy = 1 - t, 1 - c, 1 - g
    inner = (p + hh) == 1
    own, side = 2 * t + p, 2 * tx + p
    near, cross = 2 * t + 1 - p, 2 * tx + 1 - p
    home = c == t
    stray = c != t

    def remote(src, dst, ssem, rsem, **where):
        return pltpu.make_async_remote_copy(
            src_ref=src, dst_ref=dst, send_sem=ssem, recv_sem=rsem, device_id=where,
            device_id_type=MESH,
        )

    def go(copy):
        copy.start()

    def go_if(condition, copy):
        @pl.when(condition)
        def _():
            copy.start()

    def rows_of(count):
        return v.wf.at[pl.ds(0, count)]

    def await_bytes(ref, sem):
        pltpu.make_async_copy(ref, ref, sem).wait()

    v.lat_in[...] = jnp.zeros(v.lat_in.shape, F32)
    barrier = pltpu.get_barrier_semaphore()
    for ds in range(S):
        for dt in range(T):
            for dc in range(C):
                if ds or dt or dc:
                    pl.semaphore_signal(
                        barrier,
                        inc=1,
                        device_id={
                            "space": lax.rem(s + ds, S),
                            "tm": lax.rem(t + dt, T),
                            "chan": lax.rem(c + dc, C),
                        },
                        device_id_type=MESH,
                    )
    pl.semaphore_signal(barrier, inc=1, device_id={"groups": gy}, device_id_type=MESH)

    early = (
        (feat_hbm, v.feat), (w1_hbm, v.w1_raw), (gain1_hbm, v.gain1), (shift1_hbm, v.shift1),
        (w2_hbm, v.w2_raw), (gain2_hbm, v.gain2), (shift2_hbm, v.shift2),
        (gain3_hbm, v.gain3), (shift3_hbm, v.shift3), (head_w_hbm, v.head_w),
        (head_b_hbm, v.head_b), (noisy_hbm, v.noisy), (later_hbm, v.later),
        (patch_b_hbm, v.patch_b),
    )
    loads = [
        pltpu.make_async_copy(src, dst, v.load_sem.at[k]) for k, (src, dst) in enumerate(early)
    ]
    strips = v.pw_raw.shape[0]
    loads += [
        pltpu.make_async_copy(
            pw_hbm.at[:, n * LANES : (n + 1) * LANES], v.pw_raw.at[n], v.load_sem.at[len(early)]
        )
        for n in range(strips)
    ]
    for load in loads:
        load.start()

    def padded(values, width=LANES):
        rows = values.shape[0]
        if width == values.shape[1]:
            return values
        return jnp.concatenate([values, jnp.zeros((rows, width - values.shape[1]), values.dtype)], axis=1)

    def pack(dst, value, main):
        rows = value.shape[0]
        dst[...] = value[0:main]
        rest = rows - main
        free = LANES - CB
        for j in range(CB // free if rest else 0):
            dst[j * rest : (j + 1) * rest, CB:LANES] = value[main:rows, j * free : (j + 1) * free]

    def unpack(value, rows):
        main = value.shape[0]
        rest = rows - main
        if not rest:
            return (value,)
        free = LANES - CB
        columns = [value[j * rest : (j + 1) * rest, CB:LANES] for j in range(CB // free)]
        return value, padded(jnp.concatenate(columns, axis=1))

    def channel_stats(values):
        total = jnp.sum(values, axis=0, keepdims=True)
        middle = total * (1.0 / values.shape[0])
        away = values - middle
        return total, jnp.sum(away * away, axis=0, keepdims=True)

    loads[0].wait()
    for r in range(R):
        line = v.feat[r]
        for q in range(S):
            v.tile[q, r * W : (r + 1) * W, :] = padded(line[:, q * CB : (q + 1) * CB])
    own_rows = pl.ds(pl.multiple_of(p * TILE, 8), TILE)
    for q in range(S):
        value = v.tile[q]
        v.feat_all[q, own_rows, :] = value
        pack(v.a_pack.at[q], value, AM)
        total, spread = channel_stats(value)
        v.st[q : q + 1, :] = total
        v.st[S + q : S + q + 1, :] = spread
        edge = jnp.where(
            t == 0, v.tile[q, pl.ds(W - 1, R, stride=W), :], v.tile[q, pl.ds(0, R, stride=W), :]
        )
        v.colf[q, 0:R, :] = edge
        v.rowf[q, 0:W, :] = jnp.where(hh == 0, value[TILE - W : TILE], value[0:W])
        v.corf[q : q + 1, :] = jnp.where(hh == 0, edge[R - 1 : R], edge[0:1])
    v.st_in[t, s] = v.st[...]

    @pl.when(stray)
    def _():
        v.colf_in[p] = v.colf[...]

    def w_pack(k, raw):
        @pl.when(home)
        def _():
            for cc in range(C):
                rows = pl.ds(pl.multiple_of(QR * (2 * g + cc), 8), QR)
                for pp in range(2):
                    pieces = [raw[tap, rows, :][:, pp * CB : (pp + 1) * CB] for tap in range(9)]
                    pack(v.wpack.at[k, pp, cc], padded(jnp.concatenate(pieces, axis=0)), WM)

    loads[1].wait()
    w_pack(0, v.w1_raw)

    def w_own(k, raw):
        @pl.when(home)
        def _():
            for tap in range(9):
                w = raw[tap]
                v.wown[k, tap * CB : (tap + 1) * CB, :] = padded(
                    jnp.where(p == 0, w[:, 0:CB], w[:, CB : 2 * CB])
                )


    row_id = lax.broadcasted_iota(jnp.int32, (LANES, LANES), 0)
    col_id = lax.broadcasted_iota(jnp.int32, (LANES, LANES), 1)
    same = ((row_id // per_group) == (col_id // per_group)) & (row_id < CB) & (col_id < CB)
    member = jnp.where(same, 1.0, 0.0).astype(F32)

    def group_sum(rows8):
        return jnp.dot(rows8, member, precision=HIGHEST, preferred_element_type=F32)

    def store_mat(k, q, tap, w):
        high, low = split_pair(w)
        v.mat[k, q, tap * LANES : tap * LANES + CB, 0:LANES] = high
        v.mat[k, q, tap * LANES : tap * LANES + CB, LANES : 2 * LANES] = low

    def own_copy(k):
        return remote(v.wown.at[k], v.wown.at[k], v.es.at[0], v.er.at[k], chan=oc)

    def own_mat(k):
        pl.when(stray)(own_copy(k).wait_recv)
        for tap in range(9):
            store_mat(k, s, tap, v.wown[k, tap * CB : (tap + 1) * CB, :])

    gap = jnp.zeros((LANES - CB, 2 * LANES), BF16)
    for k in range(2):
        for q in range(S):
            for tap in range(9):
                v.mat[k, q, tap * LANES + CB : (tap + 1) * LANES, :] = gap

    WH = up(WM // 2, 8)
    pieces_of = (pl.ds(0, WH), pl.ds(WH, WM - WH))
    order = (far, far2, pair)

    def z_copy(k, n, peer, slot, cc, h):
        return remote(
            v.wpack.at[k, lax.rem(peer, 2), cc, pieces_of[h]],
            v.wq.at[k, slot, 2 * g + cc, pieces_of[h]],
            v.zs.at[0], v.zr.at[k, n, h], space=peer, chan=cc,
        )

    def y_copy(k, n, z, which, h):
        ref = v.wq.at[k, z, which, pieces_of[h]]
        return remote(ref, ref, v.ys.at[0], v.yr.at[k, n, h], groups=gy)

    def b_copy(k, n, z, which, h):
        ref = v.wq.at[k, z, which, pieces_of[h]]
        return remote(ref, ref, v.bs.at[0], v.br.at[k, n], chan=oc)

    def z_send(k, n):
        for h in range(2):
            for cc in range(C):
                go_if(home, z_copy(k, n, order[n], s, cc, h))

    def relay(k, n):
        z = order[n]
        for h in range(2):
            remote(
                v.wpack.at[k, 0, 0, pieces_of[h]], v.wq.at[k, z, 2 * g + c, pieces_of[h]],
                v.zs.at[0], v.zr.at[k, n, h], space=z, chan=t,
            ).wait_recv()
            y_copy(k, n, z, 2 * g + c, h).start()
            b_copy(k, n, z, 2 * g + c, h).start()

    def relay2(k, n, z):
        for h in range(2):
            y_copy(k, n, z, 2 * gy + c, h).wait_recv()
            b_copy(k, n, z, 2 * gy + c, h).start()

    def nth_weights(i):
        flip = lax.rem(lax.div(i + 1, 2), 2)
        return 2 * lax.rem(hh + flip, 2) + lax.rem(p + lax.div(i, 2), 2)

    def nth_block(j):
        return 2 * lax.rem(t + lax.rem(j, 2), 2) + lax.rem(p + lax.div(j, 2), 2)

    def finish_weights(k, n, z):
        await_bytes(rows_of(2 * WM), v.br.at[k, n])
        for kk in range(4):
            at = 0
            for value in unpack(v.wq[k, z, kk], WQ):
                for n in range(value.shape[0] // 8):
                    tap, off = divmod(at, QR)
                    to = tap * CB + kk * QR + off
                    v.wf[to : to + 8, :] = value[n * 8 : n * 8 + 8]
                    at += 8
        for tap in range(9):
            store_mat(k, z, tap, v.wf[tap * CB : (tap + 1) * CB, :])

    pl.semaphore_wait(barrier, S * T * C)

    feat_copy = remote(v.a_pack, v.a_in.at[p], v.as_sem.at[0], v.ar_sem.at[0], tm=tx)

    def feat_part(m):
        blocks = pl.ds(2 * m, 2)
        return remote(
            v.a_pack.at[blocks], v.a_in.at[p, blocks], v.fs.at[0], v.fr.at[m], space=pair
        )

    def st_copy(peer):
        return remote(v.st, v.st_in.at[t, s], v.ss_sem.at[0], v.sr_sem.at[0], space=peer)

    st_forward = remote(
        v.st_in.at[t], v.st_in.at[t], v.ss_sem.at[0], v.sr_sem.at[1], tm=tx
    )

    def col_copy(n, slot, **where):
        return remote(v.colf, v.colf_in.at[slot], v.cs_sem.at[0], v.cr_sem.at[slot], **where)

    hub = inner & home
    row_copy = remote(v.rowf, v.rowf_in, v.rs_sem.at[0], v.rr_sem.at[0], space=far2)

    def row_forward(n, **where):
        return remote(v.rowf_in, v.rowf_in, v.rs_sem.at[1], v.rr_sem.at[1], **where)

    def cor_copy(n, **where):
        return remote(v.corf, v.corf_in, v.os_sem.at[0], v.or_sem.at[0], **where)

    go_if(hub, row_copy)
    for peer in order:
        go(st_copy(peer))
    for n, (peer, column) in enumerate(((far, t), (far2, t), (far, tx), (far2, tx))):
        go_if(inner & stray, cor_copy(n, space=peer, tm=column))
    go_if(stray, col_copy(0, p, tm=tx))
    go_if(stray, col_copy(1, p, space=pair))
    go_if(stray, col_copy(2, p, space=pair, tm=tx))
    go_if(home, feat_part(0))
    go_if(home, feat_part(1))
    go_if(home, feat_copy)
    z_send(0, 0)
    z_send(0, 1)
    w_own(0, v.w1_raw)
    go_if(home, own_copy(0))
    bias_copy = remote(v.bias_out, v.bias_in, v.is_sem.at[0], v.ir_sem.at[0], chan=oc)

    for load in loads[2 : len(early)]:
        load.wait()
    await_bytes(v.pw_raw, v.load_sem.at[len(early)])
    for n, (gain, shift) in enumerate(
        ((v.gain1, v.shift1), (v.gain2, v.shift2), (v.gain3, v.shift3))
    ):
        for j, ref in enumerate((gain, shift)):
            row = ref[...].reshape(1, CH)
            for q in range(S):
                v.prm[n, q, j : j + 1, :] = padded(row[:, q * CB : (q + 1) * CB])
    bias_row = jnp.broadcast_to(v.head_b[...].reshape(1, ZH), (ZH, ZH))
    diagonal = lax.broadcasted_iota(jnp.int32, (ZH, ZH), 0) == lax.broadcasted_iota(
        jnp.int32, (ZH, ZH), 1
    )
    my_bias = jnp.sum(jnp.where(diagonal, bias_row, 0.0), axis=1, keepdims=True)
    v.bias_out[...] = jnp.broadcast_to(my_bias, (ZH, LANES))
    go(bias_copy)
    for tap in range(9):
        v.hw_send[tap] = padded(v.head_w[tap])

    @pl.when(hub)
    def _():
        row_copy.wait_recv()

    for n, where in enumerate((dict(space=pair), dict(tm=tx), dict(space=pair, tm=tx))):
        go_if(hub, row_forward(n, **where))
    z_send(0, 2)
    own_mat(0)
    w_pack(1, v.w2_raw)
    w_own(1, v.w2_raw)
    go_if(home, own_copy(1))
    def feat_pass(m):
        ref = v.a_in.at[1 - p, pl.ds(2 * m, 2)]
        return remote(ref, ref, v.gs.at[0], v.fr.at[m], tm=tx)

    def pass_features(when):
        @pl.when(home & when)
        def _():
            for m in range(2):
                feat_part(m).wait_recv()
                feat_pass(m).start()

    await_bytes(rows_of(8 * (S - 1)), v.sr_sem.at[0])
    go(st_forward)
    pass_features(inner)
    relay(0, 0)
    pass_features(jnp.logical_not(inner))
    for n in (0, 2, 1):
        z_send(1, n)
    relay(0, 1)

    def hw_copy(n, slot, **where):
        return remote(v.hw_send, v.hwq.at[slot], v.hs.at[0], v.hr.at[slot], **where)

    @pl.when(hh == t)
    def _():
        v.hwq[c] = v.hw_send[...]

    def unpack_features(slot):
        for q in range(S):
            at = 0
            for value in unpack(v.a_in[slot, q], TILE):
                rows = pl.ds(pl.multiple_of(slot * TILE + at, 8), value.shape[0])
                v.feat_all[q, rows, :] = value
                at += value.shape[0]

    @pl.when(stray)
    def _():
        feat_copy.wait_recv()
        unpack_features(p)

    @pl.when(stray)
    def _():
        for m in range(2):
            feat_pass(m).wait_recv()

    unpack_features(1 - p)
    await_bytes(rows_of(8 * S), v.sr_sem.at[1])
    col_copy(1, 1 - p, space=pair).wait_recv()
    pl.when(home)(col_copy(0, p, tm=tx).wait_recv)
    cor_copy(0, space=far).wait_recv()
    pl.when(jnp.logical_not(hub))(row_forward(0, space=pair).wait_recv)

    scale = 1.0 / float(per_group * TILE * S * T)
    everyone = [v.st_in[tt, ss] for tt in range(T) for ss in range(S)]
    total8 = everyone[0]
    for part in everyone[1:]:
        total8 = total8 + part
    summed = group_sum(total8)
    center8 = summed * scale
    gathered = jnp.zeros((8, LANES), F32)
    for part in everyone:
        away = part * (1.0 / TILE) - center8
        gathered = gathered + away * away * float(TILE)
    inverse4 = lax.rsqrt((group_sum(gathered)[0:S] + summed[S : 2 * S]) * scale + EPSILON)

    def build_taps(n, q, value, columns, corner, row, center, inverse):
        gain, shift = v.prm[n, q, 0:1, :], v.prm[n, q, 1:2, :]

        def act(values):
            u = (values - center) * inverse * gain + shift
            return u / (1.0 + jnp.exp(-u))

        inside = act(value)
        line = act(row)
        top, bottom = jnp.where(hh == 1, line, 0.0), jnp.where(hh == 0, line, 0.0)
        tail = jnp.zeros((8, LANES), F32)
        for b in range(3):
            at = AT + 1 - b
            v.taps[q, b, AT + (LAST + 1) * W : AT + (LAST + 1) * W + 8, :] = tail
            v.taps[q, b, at : at + W, :] = top
            v.taps[q, b, at + W : at + W + REG, :] = inside
            v.taps[q, b, at + W + REG : at + 2 * W + REG, :] = bottom
        tip = act(corner)
        sides = [(0, 1, jnp.where(hh == 1, tip, 0.0)), (LAST, 1, jnp.where(hh == 0, tip, 0.0))]
        sides += [(1 + first, count, act(raw)) for first, count, raw in columns]
        for first, count, piece in sides:
            at = AT + first * W
            from_left = jnp.where(c == 1, piece, 0.0)
            from_right = jnp.where(c == 0, piece, 0.0)
            if count == 1:
                v.taps[q, 0, at : at + 1, :] = from_left
                v.taps[q, 2, at + W - 1 : at + W, :] = from_right
            else:
                v.taps[q, 0, pl.ds(at, count, stride=W), :] = from_left
                v.taps[q, 2, pl.ds(at + W - 1, count, stride=W), :] = from_right

    for q in range(S):
        v.nrm[q, 0:1, :] = center8[q : q + 1]
        v.nrm[q, 1:2, :] = inverse4[q : q + 1]
        v.nrm[q, 2:3, :] = v.corf_in[q : q + 1, :]

    def first_taps(q, carry):
        build_taps(
            0, q, v.feat_all[q],
            [(0, R, v.colf_in[0, q, 0:R, :]), (R, R, v.colf_in[1, q, 0:R, :])],
            v.nrm[q, 2:3, :], v.rowf_in[q, 0:W, :], v.nrm[q, 0:1, :], v.nrm[q, 1:2, :],
        )
        return carry

    def operand(q):
        highs, lows = [], []
        for a in range(3):
            for b in range(3):
                high, low = split_pair(v.taps[q, b, AT + a * W : AT + a * W + REG, :])
                highs.append(high)
                lows.append(low)
        return jnp.concatenate(
            [jnp.concatenate(highs, axis=1), jnp.concatenate(lows, axis=1)], axis=0
        )

    def conv_block(k, q):
        part = jnp.dot(operand(q), v.mat[k, q], preferred_element_type=F32)
        return part[0:REG, 0:LANES] + part[0:REG, LANES:] + part[REG:, 0:LANES]

    lax.fori_loop(0, S, first_taps, 0)
    relay2(0, 0, far)
    relay(0, 2)
    v.acc[...] = jnp.zeros(v.acc.shape, F32)

    def first_step(i, carry):
        z = nth_weights(i)

        @pl.when(i > 0)
        def _():
            finish_weights(0, i - 1, z)

        v.acc[...] += conv_block(0, z)

        @pl.when(i < 2)
        def _():
            relay2(0, i + 1, nth_weights(i + 2))

        @pl.when(i == 1)
        def _():
            relay(1, 0)

        return carry

    lax.fori_loop(0, 4, first_step, 0)
    first = v.acc[...]
    v.conv_raw[own] = first

    def rim_exchange(k, full):
        value = full[...]
        total, spread = channel_stats(value)
        column = jnp.where(
            c == 0, full[pl.ds(W - 1, 2 * R, stride=W), :], full[pl.ds(0, 2 * R, stride=W), :]
        )
        row = jnp.where(hh == 0, value[REG - W : REG], value[0:W])
        corner = jnp.where(hh == 0, column[2 * R - 1 : 2 * R], column[0:1])
        for ref, first, rows in ((v.rowm, W, row), (v.colm, 2 * R, column), (v.corm, 1, corner)):
            ref[k, 0:first, :] = rows
            ref[k, first : first + 1, :] = total
            ref[k, first + 1 : first + 2, :] = spread
        copies = [
            remote(v.corm.at[k], v.corm_in.at[k], v.ks.at[0], v.kr.at[k], space=far, chan=oc),
            remote(v.rowm.at[k], v.rowm_in.at[k], v.ks.at[0], v.kr.at[k], space=far),
            remote(v.colm.at[k], v.colm_in.at[k], v.ks.at[0], v.kr.at[k], chan=oc),
        ]
        for copy in copies:
            go(copy)
        return total, spread

    def rim_finish(k, total, spread):
        await_bytes(rows_of(MR + up(W + 2, 8) + 8), v.kr.at[k])
        parts = [(total, spread)]
        for ref, first in ((v.rowm_in, W), (v.colm_in, 2 * R), (v.corm_in, 1)):
            parts.append((ref[k, first : first + 1, :], ref[k, first + 1 : first + 2, :]))
        whole = parts[0][0] + parts[1][0] + parts[2][0] + parts[3][0]
        wide = lambda row: jnp.broadcast_to(row, (8, LANES))
        center = group_sum(wide(whole))[0:1] * scale
        spreads = jnp.zeros((1, LANES), F32)
        for part_total, part_spread in parts:
            away = part_total * (1.0 / REG) - center
            spreads = spreads + part_spread + away * away * float(REG)
        inverse = lax.rsqrt(group_sum(wide(spreads))[0:1] * scale + EPSILON)
        return center, inverse

    rims1 = rim_exchange(0, v.conv_raw.at[own])
    pack(v.ypack, first, PM)
    near_copy = remote(v.ypack, v.yin.at[0], v.vs.at[0], v.vr.at[0], space=pair)
    go(near_copy)
    side_copy = remote(v.ypack, v.yin.at[2], v.vs.at[0], v.vr.at[1], tm=tx)
    go(side_copy)
    PH = up(PM // 2, 8)
    upper, lower = pl.ds(0, PH), pl.ds(PH, PM - PH)
    cross_x = remote(
        v.yin.at[0, upper], v.yin.at[1, upper], v.vs.at[0], v.vr.at[2], tm=tx
    )
    cross_z = remote(
        v.yin.at[2, lower], v.yin.at[1, lower], v.vs.at[0], v.vr.at[2], space=pair
    )
    own_mat(1)
    relay(1, 2)
    relay(1, 1)
    relay2(1, 0, far)
    center, inverse = rim_finish(0, *rims1)
    v.rl_in[own, 0 : 2 * R, :] = v.colm_in[0, 0 : 2 * R, :]
    v.rl_in[own, 2 * R : 2 * R + 1, :] = v.corm_in[0, 0:1, :]
    v.rl_in[own, 2 * R + 1 : 2 * R + 2, :] = center
    v.rl_in[own, 2 * R + 2 : 2 * R + 3, :] = inverse
    v.rl_in[own, MR : MR + W, :] = v.rowm_in[0, 0:W, :]

    def rl_copy(n, q, **where):
        ref = v.rl_in.at[q]
        return remote(ref, ref, v.ls.at[0], v.lr.at[q], **where)

    go(rl_copy(0, own, space=pair))
    go(rl_copy(1, own, space=pair, tm=tx))
    go(rl_copy(2, own, tm=tx))
    go_if(hh == t, hw_copy(0, c, chan=oc))
    go_if(hh == t, hw_copy(1, c, space=far))

    def second_taps(q):
        build_taps(
            1, q, v.conv_raw[q], [(0, 2 * R, v.rl_in[q, 0 : 2 * R, :])],
            v.rl_in[q, 2 * R : 2 * R + 1, :], v.rl_in[q, MR : MR + W, :],
            v.rl_in[q, 2 * R + 1 : 2 * R + 2, :], v.rl_in[q, 2 * R + 2 : 2 * R + 3, :],
        )

    def second_step(j, carry):
        q = nth_block(j)

        @pl.when(j == 1)
        def _():
            relay2(1, 1, far2)

        @pl.when(j == 2)
        def _():
            finish_weights(1, 2 - lax.rem(t + hh, 2), near)

        @pl.when(j == 3)
        def _():
            finish_weights(1, 1 + lax.rem(t + hh, 2), cross)

        @pl.when((j == 1) & (t == hh))
        def _():
            finish_weights(1, 0, far)

        @pl.when(j == 1)
        def _():
            rl_copy(2, side, tm=tx).wait_recv()

        @pl.when(j == 2)
        def _():
            rl_copy(0, near, space=pair).wait_recv()

        @pl.when(j == 3)
        def _():
            await_bytes(rows_of(PM), v.vr.at[2])
            rl_copy(1, cross, space=pair, tm=tx).wait_recv()

        @pl.when((j == 3) & (hh != t))
        def _():
            hw_copy(1, c, space=far).wait_recv()
            remote(v.hwq.at[c], v.hwq.at[c], v.hs.at[0], v.hr.at[c], chan=oc).start()

        @pl.when(j > 0)
        def _():
            at = 0
            for value in unpack(v.yin[lax.rem(j + 1, 3)], REG):
                v.conv_raw[q, at : at + value.shape[0], :] = value
                at += value.shape[0]

        second_taps(q)

        @pl.when((j == 0) & (t != hh))
        def _():
            finish_weights(1, 0, far)

        v.acc[...] += conv_block(1, q)

        @pl.when(j == 0)
        def _():
            relay2(1, 2, pair)
            side_copy.wait_recv()
            cross_z.start()
            near_copy.wait_recv()
            cross_x.start()

        return carry

    v.acc[...] = v.feat_all[own]
    lax.fori_loop(0, S, second_step, 0)
    v.hid[...] = v.acc[...]
    rims2 = rim_exchange(1, v.hid)

    hw_copy(0, oc, chan=oc).wait_recv()
    bias_copy.wait_recv()
    blank = jnp.zeros((LANES - 3 * Z, LANES), F32)
    for b in range(3):
        rows = [v.hwq[cc, a * 3 + b] for a in range(3) for cc in range(C)] + [blank]
        high, low = split_pair(jnp.concatenate(rows, axis=0))
        for place, value in ((3 * b, high), (3 * b + 1, high), (3 * b + 2, low)):
            v.wh_mat[:, place * LANES : (place + 1) * LANES] = value
    ours, other_bias = v.bias_out[...], v.bias_in[...]
    bias = jnp.where(
        own == 0,
        jnp.concatenate(
            [jnp.where(c == cc, ours, other_bias) for cc in range(C)], axis=0
        ),
        0.0,
    )

    for first, mat in ((0, v.wn_mat), (4 * (Z + 4), wc_out)):
        for b in range(2):
            for a in range(2):
                at = (b * 2 + a) * Z
                for n in range(strips):
                    high, low = split_pair(v.pw_raw[n, pl.ds(first + a * 2 + b, Z, stride=4), :])
                    lanes = slice(n * LANES, (n + 1) * LANES)
                    mat[at : at + Z, lanes] = high
                    mat[4 * Z + at : 4 * Z + at + Z, lanes] = high
                    mat[8 * Z + at : 8 * Z + at + Z, lanes] = low
    mark_sum = jnp.concatenate(
        [
            jnp.sum(v.pw_raw[n, 4 * Z : 4 * (Z + 4), :], axis=0, keepdims=True)
            for n in range(strips)
        ],
        axis=1,
    )

    PR, PC, PP = dims["PR"], dims["PC"], dims["PP"]
    FULLW = W * T
    cells, turned, patch = v.cells, v.turned, v.patch
    cells[...] = jnp.zeros(cells.shape, F32)
    patch[...] = jnp.zeros(patch.shape, F32)

    def build_patches():
        turned[...] = cells[...].T
        for b in range(2):
            picked = turned[pl.ds(b, PC, stride=2), :]
            for i in range(PR):
                patch[i * PP : i * PP + PC, b * 2 * Z : (b + 1) * 2 * Z] = picked[
                    :, i * 2 * Z : (i + 1) * 2 * Z
                ]

    for f in range(FR):
        for i in range(R):
            cells[i * Z : (i + 1) * Z, 0:FULLW] = v.noisy[f, i]
        build_patches()
        got = jnp.dot(split_columns(patch[:, 0 : 4 * Z]), v.wn_mat[...], preferred_element_type=F32)
        opening = (t * FR + f) == 0
        base_out[f] = got + v.patch_b[...].reshape(1, -1) + jnp.where(opening, mark_sum, 0.0)

    center, inverse = rim_finish(1, *rims2)
    build_taps(
        2, own, v.hid[...], [(0, 2 * R, v.colm_in[1, 0 : 2 * R, :])], v.corm_in[1, 0:1, :],
        v.rowm_in[1, 0:W, :], center, inverse,
    )

    columns = []
    for b in range(3):
        high, low = split_pair(v.taps[own, b, AT : AT + v.mixed.shape[0], :])
        columns += [high, low, high]
    v.mixed[...] = lax.dot_general(
        jnp.concatenate(columns, axis=1),
        v.wh_mat[...],
        (((1,), (1,)), ((), ())),
        preferred_element_type=F32,
    )
    for j in range(2):
        shifted = [v.mixed[j * TILE + a * W : j * TILE + a * W + LANES, :] for a in range(3)]
        joined = jnp.where(
            col_id < Z, shifted[0], jnp.where(col_id < 2 * Z, shifted[1], shifted[2])
        ).T
        v.lat_send[j] = joined[0:Z] + joined[Z : 2 * Z] + joined[2 * Z : 3 * Z] + bias
    v.lat_in[c, own] = v.lat_send[p]

    def lat_copy(dp, dt, dc, slot_c, slot_q):
        return remote(
            v.lat_send.at[1 - p if dp else p], v.lat_in.at[slot_c, slot_q],
            v.ts.at[0], v.tr.at[0],
            space=pair if dp else s, tm=tx if dt else t, chan=oc if dc else c,
        )

    hops = [(1, 1, 1), (1, 1, 0), (0, 1, 1), (0, 1, 0), (1, 0, 1), (1, 0, 0), (0, 0, 1)]
    for dp, dt, dc in hops:
        go_if(((tx if dt else t) == 0) | (c == 1), lat_copy(dp, dt, dc, c, own))

    pl.when(t == 0)(functools.partial(await_bytes, rows_of(7 * Z), v.tr.at[0]))
    pl.when((t == 1) & (c == 1))(functools.partial(await_bytes, rows_of(3 * Z), v.tr.at[0]))
    pl.when((t == 1) & (c == 0))(functools.partial(await_bytes, rows_of(4 * Z), v.tr.at[0]))

    def latent_of(tt):
        return v.lat_in[tt, 0] + v.lat_in[tt, 1] + v.lat_in[tt, 2] + v.lat_in[tt, 3]

    value = latent_of(t)
    for r in range(R):
        latent[r] = value[:, r * W : (r + 1) * W]
    for f in range(FR):
        cells[...] = jnp.zeros(cells.shape, F32)
        opening = (t * FR + f) == 0
        for tt in range(T):
            value = latent_of(tt)
            for i in range(R):
                cells[i * Z : (i + 1) * Z, tt * W : (tt + 1) * W] = value[:, i * W : (i + 1) * W]
        for i in range(R):
            rows = slice(i * Z, (i + 1) * Z)
            cells[rows, 0:FULLW] = jnp.where(opening, cells[rows, 0:FULLW], v.later[f, i])
        build_patches()
        patch_out[f] = patch[...]
    RR = up(W + 2, 8)
    drains = (
        (home, rows_of(S * AM), v.as_sem), (home, rows_of(S * AM), v.fs),
        (home, rows_of(S * AM), v.gs), (None, rows_of(8 * (2 * S - 1)), v.ss_sem),
        (stray, rows_of(3 * S * 8), v.cs_sem), (hub, rows_of(S * RR), v.rs_sem),
        (inner & stray, rows_of(4 * 8), v.os_sem), (None, rows_of(ZH), v.is_sem),
        (home, v.wq.at[0, pl.ds(0, 3)], v.zs), (None, v.wq.at[0, pl.ds(0, 3), pl.ds(0, 2)], v.ys),
        (None, v.wq.at[0, pl.ds(0, 3)], v.bs), (home, v.wown, v.es),
        (None, rows_of(2 * (MR + RR + 8)), v.ks), (None, v.yin, v.vs),
        (None, rows_of(3 * (MR + RR)), v.ls), (hh == t, rows_of(2 * 9 * ZH), v.hs),
        (hh != t, rows_of(9 * ZH), v.hs),
        (c == 1, rows_of(7 * Z), v.ts), ((c == 0) & (t == 0), rows_of(3 * Z), v.ts),
        ((c == 0) & (t == 1), rows_of(4 * Z), v.ts),
    )
    for condition, ref, sem in drains:
        wait = functools.partial(await_bytes, ref, sem.at[0])
        wait() if condition is None else pl.when(condition)(wait)
    pl.when(hub)(functools.partial(await_bytes, rows_of(3 * S * RR), v.rs_sem.at[1]))


def up(value, unit):
    return -(-value // unit) * unit


def packed_rows(rows, width, unit):
    free = LANES - width
    if free <= 0 or width % free or rows % 8:
        return rows
    main = up(-(-rows * width // LANES), unit)
    fits = main < rows and (rows - main) * (width // free) <= main
    return main if fits else rows


def plan(mesh_shape, features, noisy_latents, patch_weight, head_weight):
    S, T, C, G = (mesh_shape[axis] for axis in ("space", "tm", "chan", "groups"))
    R, W, CH = features.shape
    FR, Z = noisy_latents.shape[:2]
    dims = dict(S=S, T=T, C=C, R=R, W=W, CH=CH, Z=Z, FR=FR)
    dims["PR"], dims["PC"] = R // 2, W * T // 2
    dims["PP"] = up(W * T // 2, 8)
    dims["N"] = patch_weight.shape[1]
    CB = CH // S
    TILE = R * W
    dims["AM"] = packed_rows(TILE, CB, 16)
    dims["PM"] = packed_rows(2 * TILE, CB, 8)
    dims["WQ"] = 9 * (CB // 4)
    dims["WM"] = packed_rows(dims["WQ"], CB, 8)
    fits = (
        (S, T, C, G) == (4, 2, 2, 2)
        and CH % S == 0
        and CB <= LANES
        and CB % (4 * 8) == 0
        and CB % (CH // NGROUP) == 0
        and TILE % 8 == 0
        and TILE <= LANES
        and R % 2 == 0
        and R <= 8
        and all(dims[name] % 8 == 0 for name in ("AM", "PM", "WQ", "WM"))
        and dims["WM"] > 8
        and 2 * R + 2 <= up(2 * R + 2, 8)
        and head_weight.shape[3] * C == Z
        and Z % 16 == 0
        and 3 * Z <= LANES
        and R * Z <= LANES
        and W * T <= LANES
        and W * T % 2 == 0
        and 4 * Z <= LANES
        and dims["N"] % LANES == 0
    )
    return dims if fits else None


def fused(dims, args):
    S, T, C = dims["S"], dims["T"], dims["C"]
    R, W, CH = dims["R"], dims["W"], dims["CH"]
    Z, FR, N = dims["Z"], dims["FR"], dims["N"]
    CB, NH = CH // S, CH // C
    TILE, REG = R * W, 2 * R * W
    (f, g1, s1, w1, g2, s2, w2, g3, s3, hw, hb, noisy, later, pw, pb) = args
    flat = lambda v: v.reshape((9,) + v.shape[2:])
    by_row = lambda v: jnp.transpose(v, (0, 2, 1, 3))
    operands = (
        f, g1, s1, flat(w1), g2, s2, flat(w2), g3, s3,
        flat(jnp.transpose(hw, (0, 1, 3, 2))), hb, by_row(noisy), by_row(later), pw, pb,
    )
    vmem = pl.BlockSpec(memory_space=pltpu.VMEM)
    far = pl.BlockSpec(memory_space=pl.ANY)
    dma = lambda *shape: pltpu.SemaphoreType.DMA(shape)
    buf = lambda *shape: pltpu.VMEM(shape, F32)
    half = lambda *shape: pltpu.VMEM(shape, BF16)
    PR, PC, PP = dims["PR"], dims["PC"], dims["PP"]
    MR, RR = up(2 * R + 2, 8), up(W + 2, 8)
    TR = up(8 + 2 * W + TILE + LANES, 8)
    scratch = {
        name: pltpu.VMEM(operands[k].shape, F32)
        for name, k in (
            ("feat", 0), ("gain1", 1), ("shift1", 2), ("w1_raw", 3), ("gain2", 4), ("shift2", 5),
            ("w2_raw", 6), ("gain3", 7), ("shift3", 8), ("head_w", 9), ("head_b", 10),
            ("noisy", 11), ("later", 12), ("patch_b", 14),
        )
    }
    scratch |= {
        "pw_raw": buf(N // LANES, pw.shape[0], LANES),
        "prm": buf(3, S, 8, LANES),
        "tile": buf(S, TILE, LANES),
        "feat_all": buf(S, REG, LANES),
        "a_pack": buf(S, dims["AM"], LANES),
        "a_in": buf(2, S, dims["AM"], LANES),
        "st": buf(8, LANES),
        "st_in": buf(T, S, 8, LANES),
        "colf": buf(S, 8, LANES),
        "colf_in": buf(2, S, 8, LANES),
        "rowf": buf(S, RR, LANES),
        "rowf_in": buf(S, RR, LANES),
        "corf": buf(8, LANES),
        "corf_in": buf(8, LANES),
        "wpack": buf(2, 2, C, dims["WM"], LANES),
        "wown": buf(2, 9 * CB, LANES),
        "bias_out": buf(Z // C, LANES),
        "bias_in": buf(Z // C, LANES),
        "wq": buf(2, S, 4, dims["WM"], LANES),
        "wf": buf(9 * CB, LANES),
        "mat": half(2, S, 9 * LANES, 2 * LANES),
        "taps": buf(S, 3, TR, LANES),
        "nrm": buf(S, 8, LANES),
        "acc": buf(REG, LANES),
        "conv_raw": buf(S, REG, LANES),
        "ypack": buf(dims["PM"], LANES),
        "yin": buf(3, dims["PM"], LANES),
        "hid": buf(REG, LANES),
        "colm": buf(2, MR, LANES),
        "colm_in": buf(2, MR, LANES),
        "rowm": buf(2, RR, LANES),
        "rowm_in": buf(2, RR, LANES),
        "corm": buf(2, 8, LANES),
        "corm_in": buf(2, 8, LANES),
        "rl_in": buf(S, MR + RR, LANES),
        "hw_send": buf(9, Z // C, LANES),
        "hwq": buf(C, 9, Z // C, LANES),
        "wh_mat": half(LANES, 9 * LANES),
        "wn_mat": half(12 * Z, N),
        "mixed": buf(TR - 8, LANES),
        "lat_send": buf(2, Z, LANES),
        "lat_in": buf(C, S, Z, LANES),
        "cells": buf(LANES, LANES),
        "turned": buf(LANES, LANES),
        "patch": buf(PR * PP, LANES),
        "load_sem": dma(15),
        "as_sem": dma(1), "ar_sem": dma(1), "fs": dma(1), "fr": dma(2), "gs": dma(1),
        "ss_sem": dma(1), "sr_sem": dma(2),
        "cs_sem": dma(1), "cr_sem": dma(2),
        "rs_sem": dma(2), "rr_sem": dma(2),
        "os_sem": dma(1), "or_sem": dma(1),
        "is_sem": dma(1), "ir_sem": dma(1),
        "zs": dma(1), "zr": dma(2, 3, 2),
        "ys": dma(1), "yr": dma(2, 3, 2),
        "bs": dma(1), "br": dma(2, 3),
        "es": dma(1), "er": dma(2),
        "ks": dma(1), "kr": dma(2),
        "vs": dma(1), "vr": dma(3),
        "ls": dma(1), "lr": dma(S),
        "hs": dma(1), "hr": dma(C),
        "ts": dma(1), "tr": dma(1),
    }
    patch, base, wc, latent = pl.pallas_call(
        functools.partial(fused_kernel, dims, tuple(scratch)),
        out_shape=(
            jax.ShapeDtypeStruct((FR, PR * PP, LANES), F32),
            jax.ShapeDtypeStruct((FR, PR * PP, N), F32),
            jax.ShapeDtypeStruct((12 * Z, N), BF16),
            jax.ShapeDtypeStruct((R, Z, W), F32),
        ),
        in_specs=[pl.BlockSpec(memory_space=pltpu.HBM)] * 15,
        out_specs=(vmem, vmem, vmem, vmem),
        scratch_shapes=list(scratch.values()),
        compiler_params=pltpu.CompilerParams(
            collective_id=0, has_side_effects=True, vmem_limit_bytes=32 * 2**20
        ),
        name="fused_block",
    )(*[pltpu.with_memory_space_constraint(v, pltpu.HBM) for v in operands])
    NB = 4 if N % (4 * LANES) == 0 else 1
    tokens, latent = pl.pallas_call(
        functools.partial(finish_kernel, dims, NB),
        out_shape=(
            jax.ShapeDtypeStruct((PR, PC, FR, N), F32),
            jax.ShapeDtypeStruct((R, Z, W), F32),
        ),
        in_specs=[vmem] * 4,
        out_specs=(pl.BlockSpec(memory_space=pltpu.HBM), pl.BlockSpec(memory_space=pltpu.HBM)),
        scratch_shapes=[buf(PR, PC, FR, N), dma(NB + 1)],
        compiler_params=pltpu.CompilerParams(vmem_limit_bytes=8 * 2**20),
        name="finish_tokens",
    )(patch, base, wc, latent)
    return jnp.transpose(tokens, (2, 0, 1, 3)), jnp.transpose(latent, (0, 2, 1))


def solution(mesh):
    shape = dict(mesh.shape)

    def step(*args):
        dims = plan(shape, args[0], args[11], args[13], args[9])
        return on_device(*args) if dims is None else fused(dims, args)

    return jax.shard_map(
        step,
        mesh=mesh,
        in_specs=(
            P(("groups", "space"), "tm", None),
            P(),
            P(),
            P(None, None, "space", "chan"),
            P(),
            P(),
            P(None, None, "space", "chan"),
            P(),
            P(),
            P(None, None, "space", "chan"),
            P("chan"),
            P(("groups", "tm"), None, "space", None),
            P(("groups", "tm"), None, "space", None),
            P(None, "chan"),
            P("chan"),
        ),
        out_specs=(P(("groups", "tm"), "space", None, "chan"), P(("groups", "space"), "tm", None)),
        check_vma=False,
    )
```
